32 devices in a mesh: orient: 8 (over z, y), brow: 2 (over core), bcol: 2 (over x).
Axes of the slice: x: 2, y: 2, z: 4, core: 2. Of those that a mesh axis runs over, the one named last changes fastest.
Arguments:
- volume: float32 [8, 64, 208], P('orient', 'brow', 'bcol'), may hold values from -700 to 700
- template: float32 [24, 24, 24], replicated, may hold values from 0 to 1
- voxel_maps: int32 [8, 13824], P('orient'), may hold values from 0 to 13823, as said below
Outputs:
- best: float32 [8, 64, 208], P('orient', 'brow', 'bcol')
The draws below stay inside these ranges and needn't reach their ends.
Inputs may be any that keep to these rules, and one draw needn't show every extreme that they name: `voxel_maps`: each row holds every number of 0 to 13823 exactly once.
All inputs are finite; a program needn't handle non-finite values.
Results may differ from the reference program's by a relative error of at most 0.00013.
Values sent between devices are 32-bit elements; how exact they have to be, the bound alone decides.
A program may use at most 64 MiB of HBM per device.

```python
import math
import jax
import jax.numpy as jnp
from jax import lax

TS = 24
HALF = 12
VOX = 13824
NZ = 8
NX = 64
NY = 208
ROT = 8


def draw_volume(key, part):
    subkeys = jax.random.split(jax.random.fold_in(key, 17), 3)
    row_scale = jnp.exp(jax.random.uniform(subkeys[1], (NZ, NX, 1), minval=0.0, maxval=math.log(10.0)))
    col_scale = jnp.exp(jax.random.uniform(subkeys[2], (1, 1, NY), minval=0.0, maxval=math.log(10.0)))
    noise_part = jnp.clip(jax.random.normal(subkeys[0], (NZ, NX, NY)), -6.0, 6.0)
    samples = noise_part * row_scale * col_scale
    return samples.astype(jnp.float32)


def cycled_row(row_key):
    identity = jnp.arange(VOX, dtype=jnp.int32)
    order = jax.random.permutation(row_key, identity)
    moved_count = max(VOX // 16, 2)
    moved = order[:moved_count]
    targets = jnp.roll(moved, 1)
    return identity.at[moved].set(targets)


def draw_voxel_maps(key, part):
    row_keys = jax.random.split(jax.random.fold_in(key, 29), ROT)
    return jax.vmap(cycled_row)(row_keys).astype(jnp.int32)


def setup_inputs(seed: int = 0) -> dict:
    streams_of = jax.random.split(jax.random.key(seed), 4)
    volume = draw_volume(jax.random.fold_in(streams_of[3], 71), 0)
    template = jnp.clip(jax.random.uniform(streams_of[1], (TS, TS, TS), jnp.float32, 0.0, 1.0), 0.0, 1.0)
    voxel_maps = draw_voxel_maps(jax.random.fold_in(streams_of[3], 71), 0)
    return dict(volume=volume, template=template, voxel_maps=voxel_maps)


epsilon = 1e-06
floor_share = 0.1

def whiten_window(volume):
    spectrum = jnp.fft.fft(volume, axis=-1)
    power_spec = spectrum.real * spectrum.real + spectrum.imag * spectrum.imag
    smoothed = (jnp.roll(power_spec, 1, axis=-1) + power_spec + jnp.roll(power_spec, -1, axis=-1)) / 3.0
    smoothed = smoothed + floor_share * lax.optimization_barrier(jnp.mean(power_spec, axis=-1, keepdims=True)) + epsilon
    weights = lax.rsqrt(smoothed)
    return jnp.fft.ifft(spectrum * weights, axis=-1).real * math.sqrt(NY)

def reference(volume, template, voxel_maps):
    whitened = whiten_window(volume)
    padded = jnp.pad(whitened, HALF)
    flattened = template.reshape(-1)
    centred = flattened - jnp.mean(flattened)
    normed = centred / jnp.sqrt(jnp.sum(centred * centred) + epsilon)
    full_shape = padded.shape
    volume_spec = jnp.fft.fftn(padded)
    energy = lax.reduce_window(padded * padded, jnp.zeros((), padded.dtype), lax.add, (TS, TS, TS), (1, 1, 1), 'VALID')[:NZ, :NX, :NY]
    scaling = lax.rsqrt(energy / VOX + epsilon)

    def one_rotation(maximum, index_map):
        rotated = normed[index_map].reshape(TS, TS, TS)
        tpl_spec = jnp.fft.fftn(rotated, s=full_shape)
        correlation = jnp.fft.ifftn(volume_spec * jnp.conj(tpl_spec)).real[:NZ, :NX, :NY]
        return (jnp.maximum(maximum, correlation * scaling), None)
    initial = jnp.full((NZ, NX, NY), -jnp.inf, dtype=whitened.dtype)
    maximum, unused = lax.scan(one_rotation, initial, voxel_maps)
    return maximum
```

```python
import math

import numpy as np
import jax
import jax.numpy as jnp
from jax import lax
from jax.experimental import pallas as pl
from jax.experimental.pallas import tpu as pltpu
from jax.sharding import PartitionSpec as P

epsilon = 1e-06
floor_share = 0.1
highest = lax.Precision.HIGHEST
LANES = 128
MESH = pl.DeviceIdType.MESH


def round_up(value, step):
    return -(-value // step) * step


def forward_table(length, parts):
    half = length // 2 + 1
    padded = round_up(half, LANES)
    angles = 2.0 * np.pi * (np.outer(np.arange(length), np.arange(half)) % length) / length
    table = np.zeros((length, 2 * padded))
    table[:, :half] = np.cos(angles)
    table[:, padded : padded + half] = -np.sin(angles)
    return table.reshape(parts, length // parts, 2 * padded).astype(np.float32)


def smoothing_table(length):
    half = length // 2 + 1
    padded = round_up(half, LANES)
    table = np.zeros((padded, padded))
    fold = np.minimum(np.arange(length), length - np.arange(length))
    for k in range(half):
        for shift in (-1, 0, 1):
            table[fold[(k + shift) % length], k] += 1.0 / 3.0
        for other in range(length):
            table[fold[other], k] += floor_share / length
    return table.astype(np.float32)


def windowed_inverse(length, parts, margin):
    half = length // 2 + 1
    padded = round_up(half, LANES)
    width = length // parts
    tables = np.zeros((parts, 2 * padded, width + 2 * margin))
    k = np.arange(half)
    share = np.where((k == 0) | (2 * k == length), 1.0, 2.0)[:, None] / math.sqrt(length)
    for part in range(parts):
        columns = np.arange(width + 2 * margin) + part * width - margin
        inside = (columns >= 0) & (columns < length)
        angles = 2.0 * np.pi * (np.outer(k, columns) % length) / length
        tables[part, :half] = share * np.cos(angles) * inside
        tables[part, padded : padded + half] = -share * np.sin(angles) * inside
    return tables.astype(np.float32)


def packed_dft(count, size):
    k = np.arange(size)
    real = k <= size // 2
    freq = np.where(real, k, k - size // 2)
    angles = 2.0 * np.pi * (np.outer(np.arange(count), freq) % size) / size
    return angles, real, freq


def volume_table(size):
    angles, real, freq = packed_dft(size, size)
    return np.where(real, np.cos(angles), -np.sin(angles)).astype(np.float32)


def template_table(count, size):
    angles, real, freq = packed_dft(count, size)
    straight = np.cos(angles)
    edge = (freq == 0) | (freq == size // 2)
    crossed = np.where(real, -np.sin(angles), np.sin(angles)) * ~edge
    return np.concatenate([straight, crossed], axis=1).astype(np.float32)


def score_table(size, count):
    angles, real, freq = packed_dft(count, size)
    share = np.where((freq == 0) | (freq == size // 2), 1.0, 2.0)
    return (np.where(real, np.cos(angles), -np.sin(angles)) * share / size).T.astype(np.float32)


def box_table(size, count, edge):
    offsets = np.arange(size)[:, None] - np.arange(count)[None, :]
    return ((offsets >= 0) & (offsets < edge)).astype(np.float32)


def dot(a, b):
    return jnp.dot(a, b, precision=highest, preferred_element_type=jnp.float32)


def split_table(template_ref, normed):
    lines, edge = template_ref.shape
    template = template_ref[...]
    centred = template - jnp.sum(template, keepdims=True) / (lines * edge)
    normed[...] = centred / jnp.sqrt(jnp.sum(centred * centred, keepdims=True) + epsilon)
    table = jnp.concatenate([normed[pl.ds(j, lines // 8, stride=8), :] for j in range(8)], axis=1)
    spare = round_up(lines // 8, 16) - lines // 8
    table = jnp.concatenate([table, jnp.zeros((spare, 8 * edge), jnp.float32)], axis=0)
    upper = table.astype(jnp.bfloat16)
    lower = (table - upper.astype(jnp.float32)).astype(jnp.bfloat16)
    return jnp.concatenate([upper, lower], axis=0)


def look_up(pieces, index):
    count, span = pieces.shape
    width = index.shape[1]
    high = ((index.astype(jnp.float32) + 0.5) * (1.0 / span)).astype(jnp.int32)
    low = index - high * span
    chosen = lax.broadcasted_iota(jnp.int32, (span, width), 0) == low
    lanes = jnp.dot(
        pieces,
        jnp.where(chosen, 1.0, 0.0).astype(jnp.bfloat16),
        preferred_element_type=jnp.float32,
    )
    lanes = lanes[: count // 2] + lanes[count // 2 :]
    mine = lax.broadcasted_iota(jnp.int32, lanes.shape, 0) == high
    return jnp.sum(jnp.where(mine, lanes, 0.0), axis=0, keepdims=True)


def match_kernel(
    sizes,
    fetch,
    brick_ref,
    template_ref,
    index_ref,
    template_dft_ref,
    forward_ref,
    smoothing_ref,
    inverse_ref,
    volume_dft_ref,
    score_dft_ref,
    box_ref,
    best_ref,
    scaling_ref,
    normed,
    rotated,
    rotations,
    straight_ref,
    crossed_ref,
    pencils,
    tall,
    windows,
    spectrum,
    swapped,
    energy,
    totals,
    sems0,
    sems1,
    sems2,
):
    orients, brows, bcols, edge, voxels, base, first, last = sizes
    half_edge = edge // 2
    rows, cols = brick_ref.shape[1:]
    tile_rows = windows.shape[1]
    me = lax.axis_index("orient")
    row_id = lax.axis_index("brow")
    col_id = lax.axis_index("bcol")
    group = brows * bcols
    place = row_id * bcols + col_id

    def brick_peer(step):
        other = lax.rem(place + step, group)
        return {"orient": me, "brow": other // bcols, "bcol": lax.rem(other, bcols)}

    def partner(step):
        assert orients & (orients - 1) == 0
        other, weight = 0, 1
        while weight < orients:
            other = other + lax.rem(me // weight + step // weight, 2) * weight
            weight *= 2
        return other

    def plane_peer(step):
        return {"orient": partner(step), "brow": row_id, "bcol": col_id}

    windows[...] = jnp.zeros_like(windows)
    barrier = pltpu.get_barrier_semaphore()
    for step in range(1, group):
        pl.semaphore_signal(barrier, inc=1, device_id=brick_peer(step), device_id_type=MESH)
    for step in range(1, orients):
        pl.semaphore_signal(barrier, inc=1, device_id=plane_peer(step), device_id_type=MESH)

    fetch()
    energy[...] = jnp.zeros_like(energy)
    totals[...] = jnp.zeros_like(totals)
    tall[...] = jnp.zeros_like(tall)
    if first > base or last < base + rotated.shape[0]:
        rotated[...] = jnp.zeros_like(rotated)
    pieces = split_table(template_ref, normed)

    pl.semaphore_wait(barrier, group + orients - 2)

    gathers = []
    for step in range(1, group):
        copy = pltpu.make_async_remote_copy(
            src_ref=brick_ref.at[0],
            dst_ref=pencils.at[col_id, row_id],
            send_sem=sems1.at[0, step],
            recv_sem=sems1.at[1, step],
            device_id=brick_peer(step),
            device_id_type=MESH,
        )
        copy.start()
        gathers.append(copy)
    pencils[col_id, row_id] = brick_ref[0]
    plane_voxels = edge * edge

    @pl.loop(0, (last - first) // 2)
    def _(pair):
        start = pl.multiple_of((first + 2 * pair) * plane_voxels, 2 * plane_voxels)
        found = look_up(pieces, index_ref[0:1, pl.ds(start, 2 * plane_voxels)])
        for i in range(2):
            rotated[first - base + 2 * pair + i] = found[:, i * plane_voxels : (i + 1) * plane_voxels]

    rotations[me] = rotated[pl.ds(half_edge - me - base, orients)]
    parts = brows if orients % brows == 0 else 1
    part_planes = orients // parts
    shares = []
    for step in range(1, orients):
        target = partner(step)
        copy = pltpu.make_async_remote_copy(
            src_ref=rotated.at[pl.ds(half_edge - target - base + lax.rem(row_id, parts) * part_planes, part_planes)],
            dst_ref=rotations.at[me, pl.ds(lax.rem(row_id, parts) * part_planes, part_planes)],
            send_sem=sems0.at[0, 0, step],
            recv_sem=sems0.at[0, 1, step],
            device_id=plane_peer(step),
            device_id_type=MESH,
        )
        copy.start()
        shares.append(copy)
    for copy in gathers:
        copy.wait_recv()

    both = None
    for part in range(bcols):
        term = dot(pencils[part].reshape(brows * rows, cols), forward_ref[part])
        both = term if both is None else both + term
    padded = both.shape[1] // 2
    real, imag = both[:, :padded], both[:, padded:]
    weights = lax.rsqrt(dot(real * real + imag * imag, smoothing_ref[...]) + epsilon)
    tall[half_edge : half_edge + brows * rows, :] = dot(
        real * weights, inverse_ref[col_id, :padded, :]
    ) + dot(imag * weights, inverse_ref[col_id, padded:, :])
    start = pl.multiple_of(row_id * rows, 8)
    windows[me] = tall[pl.ds(start, tile_rows), :]
    idle = half_edge // 8 * 8 if brows == 2 else 0
    filled = pl.ds(pl.multiple_of((brows - 1 - row_id) * idle, 8), tile_rows - idle)

    sends = []
    for step in range(1, orients):
        copy = pltpu.make_async_remote_copy(
            src_ref=windows.at[me, filled],
            dst_ref=windows.at[me, filled],
            send_sem=sems2.at[0, step],
            recv_sem=sems2.at[1, step],
            device_id=plane_peer(step),
            device_id_type=MESH,
        )
        copy.start()
        sends.append(copy)

    def unfold(rotation):
        planes = rotations[rotation][:, 0, :]
        lines = jnp.concatenate(
            [planes[:, b * edge : (b + 1) * edge] for b in range(edge)], axis=0
        )
        turned = dot_short(lines, template_dft_ref[...])
        size = turned.shape[1] // 2
        straight_ref[rotation] = turned[:, :size].reshape(edge, orients, size)
        crossed_ref[rotation] = turned[:, size:].reshape(edge, orients, size)

    unfold(me)

    def share_of(step, turn):
        source = partner(step)
        owner = lax.rem(row_id, parts) * part_planes
        block = rotations.at[source, pl.ds(owner, part_planes)]
        to = plane_peer(step)
        if turn:
            to = {"orient": me, "brow": lax.rem(row_id + turn, brows), "bcol": col_id}
        return pltpu.make_async_remote_copy(
            src_ref=block,
            dst_ref=block,
            send_sem=sems0.at[turn, 0, step],
            recv_sem=sems0.at[turn, 1, step],
            device_id=to,
            device_id_type=MESH,
        )

    @pl.loop(1, orients)
    def _(step):
        share_of(step, 0).wait_recv()
        for turn in range(1, parts):
            share_of(step, turn).start()

    @pl.loop(1, orients)
    def _(step):
        for turn in range(1, parts):
            share_of(step, turn).wait()
        unfold(partner(step))

    bunch = math.gcd(orients, 8)

    def absorb(plane):
        window = windows[plane]
        gap = plane - me
        near = jnp.logical_and(gap >= -half_edge, gap < half_edge).astype(jnp.float32)
        energy[...] += window * window * near
        transformed = dot_short(window, volume_dft_ref[...])
        spectrum[...] = transformed
        swapped[...] = pltpu.roll(transformed, transformed.shape[1] // 2, 1)

        def targets(piece):
            lowest = piece * bunch
            held = [totals[lowest + r] for r in range(bunch)]
            for b in range(edge):
                near_part = spectrum[b : b + rows, :]
                far_part = swapped[b : b + rows, :]
                for r in range(bunch):
                    held[r] = held[r] + (
                        near_part * straight_ref[lowest + r, b, pl.ds(plane, 1), :]
                        + far_part * crossed_ref[lowest + r, b, pl.ds(plane, 1), :]
                    )
            for r in range(bunch):
                totals[lowest + r] = held[r]

        if orients == bunch:
            targets(0)
        else:
            pl.loop(0, orients // bunch)(targets)

    absorb(me)

    @pl.loop(1, orients)
    def _(step):
        source = partner(step)
        pltpu.make_async_remote_copy(
            src_ref=windows.at[source, filled],
            dst_ref=windows.at[source, filled],
            send_sem=sems2.at[0, step],
            recv_sem=sems2.at[1, step],
            device_id=plane_peer(step),
            device_id_type=MESH,
        ).wait_recv()
        absorb(source)

    summed = energy[0:rows, :]
    for b in range(1, edge):
        summed = summed + energy[b : b + rows, :]
    scaling = lax.rsqrt(dot(summed, box_ref[...]) / voxels + epsilon)
    size = spectrum.shape[1]
    scored = dot_short(totals[...].reshape(orients * rows, size), score_dft_ref[...])
    best = jnp.max(scored.reshape(orients, rows, cols), axis=0)
    best_ref[0] = best
    scaling_ref[0] = scaling
    for copy in gathers + shares + sends:
        copy.wait_send()


def dot_short(a, b):
    return jnp.dot(a, b, precision=lax.Precision.HIGH, preferred_element_type=jnp.float32)


def staged(sizes, count, *refs):
    sources, results = refs[:count], refs[count : count + 2]
    held, rest = refs[count + 2 : 2 * count + 2], refs[2 * count + 2 : -1]
    copies = [
        pltpu.make_async_copy(source, target, refs[-1].at[i])
        for i, (source, target) in enumerate(zip(sources, held))
    ]
    for copy in copies:
        copy.start()

    def fetch():
        for copy in copies:
            copy.wait()

    match_kernel(sizes, fetch, *held, *results, *rest)


def shards(volume, template, voxel_maps):
    orients, brows, bcols = (lax.axis_size(axis) for axis in ("orient", "brow", "bcol"))
    planes, rows, cols = volume.shape
    edge = template.shape[0]
    half_edge = edge // 2
    voxels = edge**3
    length = cols * bcols
    size = cols + edge
    tile_rows = rows + edge
    base = (half_edge - orients + 1) // 2 * 2
    first = max(0, base)
    last = min(edge, round_up(half_edge + orients, 2))
    held = round_up(half_edge + orients, 2) - base
    group = brows * bcols
    vmem = pl.BlockSpec(memory_space=pltpu.VMEM)
    constants = (
        template_table(edge, size),
        forward_table(length, bcols),
        smoothing_table(length),
        windowed_inverse(length, bcols, half_edge),
        volume_table(size),
        score_table(size, cols),
        box_table(size, cols, edge),
    )
    sizes = (orients, brows, bcols, edge, voxels, base, first, last)
    operands = (volume, template.reshape(edge * edge, edge), voxel_maps)
    operands += tuple(jnp.asarray(c) for c in constants)
    best, scaling = pl.pallas_call(
        lambda *refs: staged(sizes, len(operands), *refs),
        out_shape=(pltpu.VMEM((1, rows, cols), jnp.float32),) * 2,
        in_specs=[pl.BlockSpec(memory_space=pl.ANY)] * len(operands),
        out_specs=(vmem, vmem),
        scratch_shapes=[pltpu.VMEM(x.shape, x.dtype) for x in operands]
        + [
            pltpu.VMEM((edge * edge, edge), jnp.float32),
            pltpu.VMEM((held, 1, edge * edge), jnp.float32),
            pltpu.VMEM((orients, orients, 1, edge * edge), jnp.float32),
            pltpu.VMEM((orients, edge, orients, size), jnp.float32),
            pltpu.VMEM((orients, edge, orients, size), jnp.float32),
            pltpu.VMEM((bcols, brows, rows, cols), jnp.float32),
            pltpu.VMEM((brows * rows + edge, size), jnp.float32),
            pltpu.VMEM((orients, tile_rows, size), jnp.float32),
            pltpu.VMEM((tile_rows, size), jnp.float32),
            pltpu.VMEM((tile_rows, size), jnp.float32),
            pltpu.VMEM((tile_rows, size), jnp.float32),
            pltpu.VMEM((orients, rows, size), jnp.float32),
            pltpu.SemaphoreType.DMA((brows, 2, orients)),
            pltpu.SemaphoreType.DMA((2, group)),
            pltpu.SemaphoreType.DMA((2, orients)),
            pltpu.SemaphoreType.DMA((len(operands),)),
        ],
        compiler_params=pltpu.CompilerParams(collective_id=0, has_side_effects=True),
        name="match",
    )(*operands)
    return best * scaling


def solution(mesh):
    in_specs = (P("orient", "brow", "bcol"), P(), P("orient", None))
    out_specs = P("orient", "brow", "bcol")
    return jax.shard_map(shards, mesh=mesh, in_specs=in_specs, out_specs=out_specs, check_vma=False)
```

```python
import math

import numpy as np
import jax
import jax.numpy as jnp
from jax import lax
from jax.experimental import pallas as pl
from jax.experimental.pallas import tpu as pltpu
from jax.sharding import PartitionSpec as P

epsilon = 1e-06
floor_share = 0.1
LANES = 128
MESH = pl.DeviceIdType.MESH


def round_up(value, step):
    return -(-value // step) * step


def forward_table(length, parts):
    half = length // 2 + 1
    padded = round_up(half, LANES)
    angles = 2.0 * np.pi * (np.outer(np.arange(length), np.arange(half)) % length) / length
    table = np.zeros((length, 2 * padded))
    table[:, :half] = np.cos(angles)
    table[:, padded : padded + half] = -np.sin(angles)
    return table.reshape(parts, length // parts, 2 * padded).astype(np.float32)


def smoothing_table(length):
    half = length // 2 + 1
    padded = round_up(half, LANES)
    table = np.zeros((padded, padded))
    fold = np.minimum(np.arange(length), length - np.arange(length))
    for k in range(half):
        for shift in (-1, 0, 1):
            table[fold[(k + shift) % length], k] += 1.0 / 3.0
        for other in range(length):
            table[fold[other], k] += floor_share / length
    return table.astype(np.float32)


def windowed_inverse(length, parts, margin):
    half = length // 2 + 1
    padded = round_up(half, LANES)
    width = length // parts
    tables = np.zeros((parts, 2 * padded, width + 2 * margin))
    k = np.arange(half)
    share = np.where((k == 0) | (2 * k == length), 1.0, 2.0)[:, None] / math.sqrt(length)
    for part in range(parts):
        columns = np.arange(width + 2 * margin) + part * width - margin
        inside = (columns >= 0) & (columns < length)
        angles = 2.0 * np.pi * (np.outer(k, columns) % length) / length
        tables[part, :half] = share * np.cos(angles) * inside
        tables[part, padded : padded + half] = -share * np.sin(angles) * inside
    return tables.astype(np.float32)


def split(table):
    upper = table.astype(jnp.bfloat16)
    lower = (table - upper.astype(np.float64)).astype(jnp.bfloat16)
    return upper, lower


def left_table(table):
    upper, lower = split(table)
    return np.concatenate([upper, lower, upper], axis=1)


def right_table(table):
    upper, lower = split(table)
    return np.concatenate([upper, upper, lower], axis=0)


def odd_waves(count, size):
    angles = np.pi * (np.outer(np.arange(count), 2 * np.arange(size // 2) + 1) % (2 * size)) / size
    return np.cos(angles), np.sin(angles)


def line_table(count, size):
    cos, sin = odd_waves(count, size)
    return np.concatenate([cos, -sin, -sin, -cos], axis=1)


def row_waves(size, count):
    angles = 2.0 * np.pi * (np.outer(np.arange(size), np.arange(count)) % size) / size
    return np.cos(angles), np.sin(angles)


def template_lines(edge, size, strips):
    span = edge // strips
    waves = line_table(edge, size)
    table = np.zeros((LANES, 2, span, size))
    for b in range(span):
        for half in range(2):
            table[b * edge : (b + 1) * edge, half, b] = waves[:, half * size : (half + 1) * size]
    return right_table(table.reshape(LANES, -1))


def template_rows(size, edge, strips):
    order = np.arange(edge).reshape(strips, edge // strips).T.reshape(-1)
    return left_table(np.concatenate([wave[:, order] for wave in row_waves(size, edge)], axis=1))


def volume_rows(size):
    cos, sin = row_waves(size, size)
    return left_table(np.block([[cos, sin], [-sin, cos]]))


def score_rows(size, rows):
    cos, sin = (wave.T / size for wave in row_waves(size, rows))
    return left_table(np.block([[cos, -sin], [sin, cos]]))


def score_lines(size, count):
    cos, sin = (wave.T * (2.0 / size) for wave in odd_waves(count, size))
    return right_table(np.concatenate([cos, cos, -sin, -sin], axis=0))


def box_table(size, count, edge):
    offsets = np.arange(size)[:, None] - np.arange(count)[None, :]
    return ((offsets >= 0) & (offsets < edge)).astype(jnp.bfloat16)


def split_table(template_ref, normed):
    lines, edge = template_ref.shape
    template = template_ref[...]
    centred = template - jnp.sum(template, keepdims=True) / (lines * edge)
    normed[...] = centred / jnp.sqrt(jnp.sum(centred * centred, keepdims=True) + epsilon)
    table = jnp.concatenate([normed[pl.ds(j, lines // 8, stride=8), :] for j in range(8)], axis=1)
    spare = round_up(lines // 8, 16) - lines // 8
    table = jnp.concatenate([table, jnp.zeros((spare, 8 * edge), jnp.float32)], axis=0)
    upper = table.astype(jnp.bfloat16)
    lower = (table - upper.astype(jnp.float32)).astype(jnp.bfloat16)
    return jnp.concatenate([upper, lower], axis=0)


def look_up(pieces, index):
    count, span = pieces.shape
    width = index.shape[1]
    high = ((index.astype(jnp.float32) + 0.5) * (1.0 / span)).astype(jnp.int32)
    low = index - high * span
    chosen = lax.broadcasted_iota(jnp.int32, (span, width), 0) == low
    lanes = jnp.dot(
        pieces,
        jnp.where(chosen, 1.0, 0.0).astype(jnp.bfloat16),
        preferred_element_type=jnp.float32,
    )
    lanes = lanes[: count // 2] + lanes[count // 2 :]
    mine = lax.broadcasted_iota(jnp.int32, lanes.shape, 0) == high
    return jnp.sum(jnp.where(mine, lanes, 0.0), axis=0, keepdims=True)


def halves(x):
    upper = x.astype(jnp.bfloat16)
    return upper, (x - upper.astype(jnp.float32)).astype(jnp.bfloat16)


def product(a, b):
    return jnp.dot(a, b, preferred_element_type=jnp.float32)


def by_table(x, table):
    upper, lower = halves(x)
    return product(jnp.concatenate([upper, lower, upper], axis=1), table)


def table_by(table, x):
    upper, lower = halves(x)
    return product(table, jnp.concatenate([upper, upper, lower], axis=0))


def match_kernel(
    sizes,
    refs,
    copies,
    rotated,
    rotations,
    lines,
    templates,
    volumes,
    pencils,
    windows,
    energy,
    scores,
    normed,
    own_sem,
    gather_sems,
    share_sems,
    turn_sems,
    window_sems,
    send_sems,
    best_ref,
    scaling_ref,
):
    orients, brows, bcols, parts, edge, base, margin, batch, strips = sizes
    half_edge = edge // 2
    rows, cols = refs["brick"].shape[1:]
    tile_rows, size = energy.shape
    skip = margin - half_edge
    me = lax.axis_index("orient")
    row_id = lax.axis_index("brow")
    col_id = lax.axis_index("bcol")
    share = orients // parts
    mine = lax.rem(row_id, parts)
    plane_voxels = edge * edge
    span = edge // strips

    def column_peer(step):
        return {"orient": me, "brow": row_id, "bcol": lax.rem(col_id + step, bcols)}

    def partner(step):
        assert orients & (orients - 1) == 0
        other, weight = 0, 1
        while weight < orients:
            other = other + lax.rem(me // weight + step // weight, 2) * weight
            weight *= 2
        return other

    partners = [partner(step) for step in range(orients)]

    def plane_peer(step, turn=0):
        return {"orient": partners[step], "brow": lax.rem(row_id + turn, brows), "bcol": col_id}

    def first_of(part, plane):
        start = orients - plane
        rest = lax.rem(start, 2 * parts) + 2 * parts - 2 * part
        return start // (2 * parts) * 2 + (rest - 1) // (2 * parts) + (rest - 2) // (2 * parts)

    def plane_of(slot):
        part, index = slot // share, slot % share
        found = first_of(part, me) + index
        return found // 2 * (2 * parts) + 2 * part + lax.rem(found, 2) - orients + me

    windows[...] = jnp.zeros_like(windows)
    barrier = pltpu.get_barrier_semaphore()
    for step in range(1, bcols):
        pl.semaphore_signal(barrier, inc=1, device_id=column_peer(step), device_id_type=MESH)
    for step in range(orients):
        for turn in range(brows):
            if step or turn:
                pl.semaphore_signal(barrier, inc=1, device_id=plane_peer(step, turn), device_id_type=MESH)
    for copy in copies.values():
        copy.start()
    own = pltpu.make_async_copy(refs["brick"].at[0], pencils.at[col_id], own_sem)
    own.start()
    energy[...] = jnp.zeros_like(energy)
    rotated[...] = jnp.zeros_like(rotated)
    planes_of = [plane_of(slot) for slot in range(orients)]
    pl.semaphore_wait(barrier, bcols - 1 + orients * brows - 1)

    def gather_of(step, place):
        return pltpu.make_async_remote_copy(
            src_ref=refs["brick"].at[0],
            dst_ref=pencils.at[place],
            send_sem=send_sems.at[0],
            recv_sem=gather_sems.at[step],
            device_id=column_peer(step),
            device_id_type=MESH,
        )

    for step in range(1, bcols):
        gather_of(step, col_id).start()

    copies["template"].wait()
    pieces = split_table(refs["template"], normed)
    copies["index"].wait()

    @pl.loop(0, orients // parts)
    def _(pair):
        plane = base + 2 * mine + 2 * parts * pair

        def fill():
            start = pl.multiple_of(plane * plane_voxels, 2 * plane_voxels)
            found = look_up(pieces, refs["index"][0:1, pl.ds(start, 2 * plane_voxels)])
            for i in range(2):
                rotated[2 * pair + i, :, :plane_voxels] = found[:, i * plane_voxels : (i + 1) * plane_voxels]

        if base < 0 or base + 2 * orients > edge:
            pl.when(jnp.logical_and(plane >= 0, plane < edge))(fill)
        else:
            fill()

    def block(rotation, part):
        return rotations.at[rotation, pl.ds(part * share, share)]

    def share_of(step, rotation):
        return pltpu.make_async_remote_copy(
            src_ref=rotated.at[pl.ds(first_of(mine, partners[step]), share)],
            dst_ref=block(rotation, mine),
            send_sem=send_sems.at[1],
            recv_sem=share_sems.at[step],
            device_id=plane_peer(step),
            device_id_type=MESH,
        )

    def turn_of(step, turn):
        return pltpu.make_async_remote_copy(
            src_ref=block(partners[step], mine),
            dst_ref=block(partners[step], mine),
            send_sem=send_sems.at[2],
            recv_sem=turn_sems.at[step],
            device_id=plane_peer(0, turn),
            device_id_type=MESH,
        )

    for step in reversed(range(1, orients)):
        share_of(step, me).start()
    rotations[me, pl.ds(mine * share, share)] = rotated[pl.ds(first_of(mine, me), share)]
    for turn in range(1, parts):
        turn_of(0, turn).start()

    own.wait()
    for step in range(1, bcols):
        gather_of(step, lax.rem(col_id + bcols - step, bcols)).wait_recv()
    for name in ("forward", "smoothing", "inverse"):
        copies[name].wait()
    both = None
    for part in range(bcols):
        term = dot_short(pencils[part], refs["forward"][part])
        both = term if both is None else both + term
    padded = both.shape[1] // 2
    real, imag = both[:, :padded], both[:, padded:]
    weights = lax.rsqrt(dot_short(real * real + imag * imag, refs["smoothing"][...]) + epsilon)
    windows[me, margin : margin + rows] = dot_short(
        real * weights, refs["inverse"][col_id, :padded, :]
    ) + dot_short(imag * weights, refs["inverse"][col_id, padded:, :])

    def window_of(step, plane):
        part = windows.at[plane, pl.ds(margin, rows)]
        return pltpu.make_async_remote_copy(
            src_ref=part,
            dst_ref=part,
            send_sem=send_sems.at[3],
            recv_sem=window_sems.at[step],
            device_id=plane_peer(step),
            device_id_type=MESH,
        )

    def margin_of(step, plane):
        return pltpu.make_async_remote_copy(
            src_ref=windows.at[plane, pl.ds(pl.multiple_of(rows - row_id * (rows - margin), 8), margin)],
            dst_ref=windows.at[plane, pl.ds(pl.multiple_of(row_id * (margin + rows), 8), margin)],
            send_sem=send_sems.at[4 if step == 0 else 3],
            recv_sem=window_sems.at[step],
            device_id=plane_peer(step, 1),
            device_id_type=MESH,
        )

    for step in reversed(range(orients)):
        if step:
            window_of(step, me).start()
        if brows > 1:
            margin_of(step, me).start()
    for name in ("template_lines", "template_rows", "volume_lines", "volume_rows", "score_rows", "score_lines", "box"):
        copies[name].wait()

    def transform(steps):
        tiles = []
        for step in steps:
            plane = partners[step]
            count = (rows if step else 0) + (margin if brows > 1 else 0)
            if count:
                arrived = windows.at[plane, pl.ds(0, count)]
                pltpu.make_async_copy(arrived, arrived, window_sems.at[step]).wait()
            tile = windows[plane, skip : skip + tile_rows]
            gap = plane - me
            near = jnp.logical_and(gap >= -half_edge, gap < half_edge).astype(jnp.float32)
            energy[...] += tile * tile * near
            tiles.append(tile)
        turned = by_table(jnp.concatenate(tiles, axis=0), refs["volume_lines"][...])
        for first in range(0, len(steps), 2):
            pair = []
            for i in range(first, first + 2):
                part = turned[i * tile_rows : (i + 1) * tile_rows]
                pair.append(jnp.concatenate([part[:, :size], part[:, size:]], axis=0))
            spun = table_by(refs["volume_rows"][...], jnp.concatenate(pair, axis=1))
            for i in range(2):
                volumes[partners[steps[first + i]]] = spun[:, i * size : (i + 1) * size]

    def unfold(steps):
        for step in steps:
            if parts > 1:
                arrived = rotations.at[partners[step], pl.ds(0, orients - share)]
                pltpu.make_async_copy(arrived, arrived, turn_sems.at[step]).wait()
        planes = jnp.concatenate([rotations[partners[step]][:, 0, :] for step in steps], axis=0)
        width = span * edge
        pieces = [planes[:, j * width : j * width + LANES] for j in range(strips)]
        turned = by_table(jnp.concatenate(pieces, axis=0), refs["template_lines"][...])
        for k in range(2 * span):
            lines[k] = turned[:, k * size : (k + 1) * size]
        count = len(steps) * orients
        for i, step in enumerate(steps):
            for first in range(0, orients, 2):
                pair = [
                    jnp.concatenate(
                        [lines[k, pl.ds(i * orients + slot, strips, stride=count), :] for k in range(2 * span)],
                        axis=0,
                    )
                    for slot in (first, first + 1)
                ]
                spun = table_by(refs["template_rows"][...], jnp.concatenate(pair, axis=1))
                for j in range(2):
                    templates[partners[step], planes_of[first + j]] = spun[:, j * size : (j + 1) * size]

    def forward(steps):
        for step in steps:
            if step:
                share_of(step, partners[step]).wait_recv()
                for turn in range(1, parts):
                    turn_of(step, turn).start()

    groups = [list(range(first, first + batch)) for first in range(0, orients, batch)]
    for steps in groups:
        forward(steps)
    for steps in groups:
        unfold(steps)
        transform(steps)

    bunch = math.gcd(orients, 8)

    def combine(lowest):
        def gather(held, start):
            held = list(held)
            for i in range(bunch):
                straight = volumes[start + i, :tile_rows, :]
                crossed = volumes[start + i, tile_rows:, :]
                for j in range(2):
                    wave = templates[lowest + j, start + i]
                    held[2 * j] = held[2 * j] + straight * wave
                    held[2 * j + 1] = held[2 * j + 1] + crossed * wave
            return tuple(held)

        held = (jnp.zeros((tile_rows, size), jnp.float32),) * 4
        if orients == bunch:
            held = gather(held, 0)
        else:
            held = lax.fori_loop(0, orients // bunch, lambda i, h: gather(h, i * bunch), held)
        return jnp.concatenate([jnp.concatenate(held[:2], axis=0), jnp.concatenate(held[2:], axis=0)], axis=1)

    def finish(lowest):
        for first in range(0, bunch, 2):
            turned = table_by(refs["score_rows"][...], combine(lowest + first))
            for i in range(2):
                part = turned[:, i * size : (i + 1) * size]
                start = pl.multiple_of((lowest + first + i) * rows, rows)
                scores[pl.ds(start, rows), :size] = part[:rows]
                scores[pl.ds(start, rows), size:] = part[rows:]

    if orients == bunch:
        finish(0)
    else:
        pl.loop(0, orients // bunch)(lambda i: finish(i * bunch))

    summed = energy[0:rows, :]
    for b in range(1, edge):
        summed = summed + energy[b : b + rows, :]
    upper, lower = halves(summed)
    boxed = product(upper, refs["box"][...]) + product(lower, refs["box"][...])
    scaling_ref[0] = lax.rsqrt(boxed / edge**3 + epsilon)
    scored = by_table(scores[...], refs["score_lines"][...])
    best_ref[0] = jnp.max(scored.reshape(orients, rows, cols), axis=0)
    sent = [
        pencils.at[pl.ds(0, bcols - 1)],
        rotations.at[pl.ds(0, orients - 1), pl.ds(0, share)],
        rotations.at[pl.ds(0, orients), pl.ds(0, orients - share)],
        windows.at[pl.ds(0, orients - 1), pl.ds(0, rows + (margin if brows > 1 else 0))],
        windows.at[0, pl.ds(0, margin)],
    ]
    wanted = [bcols > 1, True, parts > 1, True, brows > 1]
    for i, ref in enumerate(sent):
        if wanted[i]:
            pltpu.make_async_copy(ref, ref, send_sems.at[i]).wait()


def dot_short(a, b):
    return jnp.dot(a, b, precision=lax.Precision.HIGH, preferred_element_type=jnp.float32)


names = (
    "template",
    "index",
    "forward",
    "smoothing",
    "inverse",
    "template_lines",
    "template_rows",
    "volume_lines",
    "volume_rows",
    "score_rows",
    "score_lines",
    "box",
)


def staged(sizes, *refs):
    brick, sources = refs[0], refs[1 : len(names) + 1]
    results = refs[len(names) + 1 : len(names) + 3]
    held = refs[len(names) + 3 : 2 * len(names) + 3]
    rest = refs[2 * len(names) + 3 : -1]
    copies = {
        name: pltpu.make_async_copy(source, target, refs[-1].at[i])
        for i, (name, source, target) in enumerate(zip(names, sources, held))
    }
    named = dict(zip(names, held), brick=brick)
    match_kernel(sizes, named, copies, *rest, *results)


def shards(volume, template, voxel_maps):
    orients, brows, bcols = (lax.axis_size(axis) for axis in ("orient", "brow", "bcol"))
    planes, rows, cols = volume.shape
    edge = template.shape[0]
    half_edge = edge // 2
    length = cols * bcols
    size = cols + edge
    tile_rows = rows + edge
    margin = round_up(half_edge, 8)
    strips = 8
    batch = math.gcd(orients, 4)
    parts = brows if orients % (2 * brows) == 0 else 1
    base = half_edge - orients
    assert brows <= 2 and margin <= rows and tile_rows <= rows + 2 * margin
    assert base % 2 == 0 and orients % 2 == 0
    assert edge % strips == 0 and edge // strips * edge <= LANES
    width = edge // strips * edge * (strips - 1) + LANES
    width = round_up(width, LANES)
    vmem = pl.BlockSpec(memory_space=pltpu.VMEM)
    constants = (
        forward_table(length, bcols),
        smoothing_table(length),
        windowed_inverse(length, bcols, half_edge),
        template_lines(edge, size, strips),
        template_rows(tile_rows, edge, strips),
        right_table(line_table(size, size)),
        volume_rows(tile_rows),
        score_rows(tile_rows, rows),
        score_lines(size, cols),
        box_table(size, cols, edge),
    )
    sizes = (orients, brows, bcols, parts, edge, base, margin, batch, strips)
    operands = (volume, template.reshape(edge * edge, edge), voxel_maps)
    operands += tuple(jnp.asarray(c) for c in constants)
    best, scaling = pl.pallas_call(
        lambda *refs: staged(sizes, *refs),
        out_shape=(pltpu.VMEM((1, rows, cols), jnp.float32),) * 2,
        in_specs=[pl.BlockSpec(memory_space=pl.ANY)] * len(operands),
        out_specs=(vmem, vmem),
        scratch_shapes=[pltpu.VMEM(x.shape, x.dtype) for x in operands[1:]]
        + [
            pltpu.VMEM((2 * orients // parts, 1, width), jnp.float32),
            pltpu.VMEM((orients, orients, 1, width), jnp.float32),
            pltpu.VMEM((2 * edge // strips, strips * batch * orients, size), jnp.float32),
            pltpu.VMEM((orients, orients, tile_rows, size), jnp.float32),
            pltpu.VMEM((orients, 2 * tile_rows, size), jnp.float32),
            pltpu.VMEM((bcols, rows, cols), jnp.float32),
            pltpu.VMEM((orients, rows + 2 * margin, size), jnp.float32),
            pltpu.VMEM((tile_rows, size), jnp.float32),
            pltpu.VMEM((orients * rows, 2 * size), jnp.float32),
            pltpu.VMEM((edge * edge, edge), jnp.float32),
            pltpu.SemaphoreType.DMA,
            pltpu.SemaphoreType.DMA((bcols,)),
            pltpu.SemaphoreType.DMA((orients,)),
            pltpu.SemaphoreType.DMA((orients,)),
            pltpu.SemaphoreType.DMA((orients,)),
            pltpu.SemaphoreType.DMA((5,)),
            pltpu.SemaphoreType.DMA((len(names),)),
        ],
        compiler_params=pltpu.CompilerParams(collective_id=0, has_side_effects=True),
        name="match",
    )(*operands)
    return best * scaling


def solution(mesh):
    in_specs = (P("orient", "brow", "bcol"), P(), P("orient", None))
    out_specs = P("orient", "brow", "bcol")
    return jax.shard_map(shards, mesh=mesh, in_specs=in_specs, out_specs=out_specs, check_vma=False)
```

```python
import math

import numpy as np
import jax
import jax.numpy as jnp
from jax import lax
from jax.experimental import pallas as pl
from jax.experimental.pallas import tpu as pltpu
from jax.sharding import PartitionSpec as P

epsilon = 1e-06
floor_share = 0.1
LANES = 128
MESH = pl.DeviceIdType.MESH


def round_up(value, step):
    return -(-value // step) * step


def forward_table(length, parts):
    half = length // 2 + 1
    padded = round_up(half, LANES)
    angles = 2.0 * np.pi * (np.outer(np.arange(length), np.arange(half)) % length) / length
    table = np.zeros((length, 2 * padded))
    table[:, :half] = np.cos(angles)
    table[:, padded : padded + half] = -np.sin(angles)
    return table.reshape(parts, length // parts, 2 * padded).astype(np.float32)


def smoothing_table(length):
    half = length // 2 + 1
    padded = round_up(half, LANES)
    table = np.zeros((padded, padded))
    fold = np.minimum(np.arange(length), length - np.arange(length))
    for k in range(half):
        for shift in (-1, 0, 1):
            table[fold[(k + shift) % length], k] += 1.0 / 3.0
        for other in range(length):
            table[fold[other], k] += floor_share / length
    return table.astype(np.float32)


def windowed_inverse(length, parts, margin):
    half = length // 2 + 1
    padded = round_up(half, LANES)
    width = length // parts
    tables = np.zeros((parts, 2 * padded, width + 2 * margin))
    k = np.arange(half)
    share = np.where((k == 0) | (2 * k == length), 1.0, 2.0)[:, None] / math.sqrt(length)
    for part in range(parts):
        columns = np.arange(width + 2 * margin) + part * width - margin
        inside = (columns >= 0) & (columns < length)
        angles = 2.0 * np.pi * (np.outer(k, columns) % length) / length
        tables[part, :half] = share * np.cos(angles) * inside
        tables[part, padded : padded + half] = -share * np.sin(angles) * inside
    return tables.astype(np.float32)


def split(table):
    upper = table.astype(jnp.bfloat16)
    lower = (table - upper.astype(np.float64)).astype(jnp.bfloat16)
    return upper, lower


def left_table(table):
    upper, lower = split(table)
    return np.concatenate([upper, lower, upper], axis=1)


def right_table(table):
    upper, lower = split(table)
    return np.concatenate([upper, upper, lower], axis=0)


def odd_waves(count, size):
    angles = np.pi * (np.outer(np.arange(count), 2 * np.arange(size // 2) + 1) % (2 * size)) / size
    return np.cos(angles), np.sin(angles)


def line_table(count, size):
    cos, sin = odd_waves(count, size)
    return np.concatenate([cos, -sin, -sin, -cos], axis=1)


def row_waves(size, count):
    angles = 2.0 * np.pi * (np.outer(np.arange(size), np.arange(count)) % size) / size
    return np.cos(angles), np.sin(angles)


def template_lines(edge, size, strips):
    span = edge // strips
    waves = line_table(edge, size)
    table = np.zeros((LANES, 2, span, size))
    for b in range(span):
        for half in range(2):
            table[b * edge : (b + 1) * edge, half, b] = waves[:, half * size : (half + 1) * size]
    return right_table(table.reshape(LANES, -1))


def template_rows(size, edge, strips):
    order = np.arange(edge).reshape(strips, edge // strips).T.reshape(-1)
    return left_table(np.concatenate([wave[:, order] for wave in row_waves(size, edge)], axis=1))


def volume_rows(size):
    cos, sin = row_waves(size, size)
    return left_table(np.block([[cos, sin], [-sin, cos]]))


def score_rows(size, rows):
    cos, sin = (wave.T / size for wave in row_waves(size, rows))
    return left_table(np.block([[cos, -sin], [sin, cos]]))


def score_lines(size, count):
    cos, sin = (wave.T * (2.0 / size) for wave in odd_waves(count, size))
    return right_table(np.concatenate([cos, cos, -sin, -sin], axis=0))


def box_table(size, count, edge):
    offsets = np.arange(size)[:, None] - np.arange(count)[None, :]
    return ((offsets >= 0) & (offsets < edge)).astype(jnp.bfloat16)


def split_table(template_ref, normed):
    lines, edge = template_ref.shape
    template = template_ref[...]
    centred = template - jnp.sum(template, keepdims=True) / (lines * edge)
    normed[...] = centred / jnp.sqrt(jnp.sum(centred * centred, keepdims=True) + epsilon)
    table = jnp.concatenate([normed[pl.ds(j, lines // 8, stride=8), :] for j in range(8)], axis=1)
    spare = round_up(lines // 8, 16) - lines // 8
    table = jnp.concatenate([table, jnp.zeros((spare, 8 * edge), jnp.float32)], axis=0)
    upper = table.astype(jnp.bfloat16)
    lower = (table - upper.astype(jnp.float32)).astype(jnp.bfloat16)
    return jnp.concatenate([upper, lower], axis=0)


def look_up(pieces, index):
    count, span = pieces.shape
    width = index.shape[1]
    high = ((index.astype(jnp.float32) + 0.5) * (1.0 / span)).astype(jnp.int32)
    low = index - high * span
    chosen = lax.broadcasted_iota(jnp.int32, (span, width), 0) == low
    lanes = jnp.dot(
        pieces,
        jnp.where(chosen, 1.0, 0.0).astype(jnp.bfloat16),
        preferred_element_type=jnp.float32,
    )
    lanes = lanes[: count // 2] + lanes[count // 2 :]
    mine = lax.broadcasted_iota(jnp.int32, lanes.shape, 0) == high
    return jnp.sum(jnp.where(mine, lanes, 0.0), axis=0, keepdims=True)


def halves(x):
    upper = x.astype(jnp.bfloat16)
    return upper, (x - upper.astype(jnp.float32)).astype(jnp.bfloat16)


def product(a, b):
    return jnp.dot(a, b, preferred_element_type=jnp.float32)


def by_table(x, table):
    upper, lower = halves(x)
    return product(jnp.concatenate([upper, lower, upper], axis=1), table)


def table_by(table, x):
    upper, lower = halves(x)
    return product(table, jnp.concatenate([upper, upper, lower], axis=0))


def match_kernel(
    sizes,
    refs,
    copies,
    rotated,
    rotations,
    lines,
    templates,
    volumes,
    pencils,
    windows,
    energy,
    scores,
    normed,
    table,
    own_sem,
    gather_sems,
    share_sems,
    turn_sems,
    window_sems,
    margin_sems,
    send_sems,
    tokens,
    best_ref,
    scaling_ref,
):
    orients, brows, bcols, parts, edge, base, margin, batch, strips = sizes
    half_edge = edge // 2
    rows, cols = refs["brick"].shape[1:]
    tile_rows, size = energy.shape
    skip = margin - half_edge
    me = lax.axis_index("orient")
    row_id = lax.axis_index("brow")
    col_id = lax.axis_index("bcol")
    share = orients // parts
    mine = lax.rem(row_id, parts)
    plane_voxels = edge * edge
    span = edge // strips

    def column_peer(step):
        return {"orient": me, "brow": row_id, "bcol": lax.rem(col_id + step, bcols)}

    def partner(step):
        assert orients & (orients - 1) == 0
        other, weight = 0, 1
        while weight < orients:
            other = other + lax.rem(me // weight + step // weight, 2) * weight
            weight *= 2
        return other

    partners = [partner(step) for step in range(orients)]
    pair, last = me // 2, orients // 2 - 1

    def plane_peer(plane):
        return {"orient": plane, "brow": row_id, "bcol": col_id}

    def row_peer(turn):
        return {"orient": me, "brow": lax.rem(row_id + turn, brows), "bcol": col_id}

    def target(k):
        return k + (k + orients - me) // orients

    def greet(semaphore, peer):
        pl.semaphore_signal(semaphore, inc=1, device_id=peer, device_id_type=MESH)

    def first_of(part, plane):
        start = orients - plane
        rest = lax.rem(start, 2 * parts) + 2 * parts - 2 * part
        return start // (2 * parts) * 2 + (rest - 1) // (2 * parts) + (rest - 2) // (2 * parts)

    def plane_of(slot):
        part, index = slot // share, slot % share
        found = first_of(part, me) + index
        return found // 2 * (2 * parts) + 2 * part + lax.rem(found, 2) - orients + me

    windows[...] = jnp.zeros_like(windows)
    barrier = pltpu.get_barrier_semaphore()
    for step in range(1, bcols):
        greet(barrier, column_peer(step))
    for turn in range(1, brows):
        greet(barrier, row_peer(turn))
    greet(barrier, plane_peer(partners[1]))

    @pl.when(pair > 0)
    def _():
        for i in range(2):
            greet(barrier, plane_peer(2 * pair - 2 + i))

    @pl.when(pair < last)
    def _():
        for i in range(2):
            greet(barrier, plane_peer(2 * pair + 2 + i))

    for copy in copies.values():
        copy.start()
    own = pltpu.make_async_copy(refs["brick"].at[0], pencils.at[col_id], own_sem)
    own.start()
    energy[...] = jnp.zeros_like(energy)
    rotated[...] = jnp.zeros_like(rotated)
    planes_of = [plane_of(slot) for slot in range(orients)]

    def tabulate():
        copies["template"].wait()
        table[...] = split_table(refs["template"], normed)
        copies["index"].wait()

    def find(first, end):
        @pl.loop(first, end)
        def _(index):
            plane = base + 2 * mine + 2 * parts * index

            def fill():
                start = pl.multiple_of(plane * plane_voxels, 2 * plane_voxels)
                found = look_up(table[...], refs["index"][0:1, pl.ds(start, 2 * plane_voxels)])
                for i in range(2):
                    rotated[2 * index + i, :, :plane_voxels] = found[:, i * plane_voxels : (i + 1) * plane_voxels]

            if base < 0 or base + 2 * orients > edge:
                pl.when(jnp.logical_and(plane >= 0, plane < edge))(fill)
            else:
                fill()

    @pl.when(pair < last)
    def _():
        tabulate()
        find(0, share // 2)

    beside = (pair + last) // (last + 1) + (2 * last - pair) // (last + 1)
    pl.semaphore_wait(barrier, bcols - 1 + brows - 1 + 1 + 2 * beside)

    def gather_of(step, place):
        return pltpu.make_async_remote_copy(
            src_ref=refs["brick"].at[0],
            dst_ref=pencils.at[place],
            send_sem=send_sems.at[0],
            recv_sem=gather_sems.at[step],
            device_id=column_peer(step),
            device_id_type=MESH,
        )

    for step in range(1, bcols):
        gather_of(step, col_id).start()

    lower, upper = tokens.at[0], tokens.at[1]
    above, below = plane_peer(me + 2), plane_peer(me - 2)

    @pl.when(jnp.logical_and(pair == last - 1, pair > 0))
    def _():
        greet(upper, below)

    @pl.when(jnp.logical_and(pair == 1, pair < last))
    def _():
        greet(lower, above)

    @pl.when(jnp.logical_and(pair > 1, pair < last))
    def _():
        pl.semaphore_wait(lower, 1)
        greet(lower, above)

    @pl.when(pair == last)
    def _():
        tabulate()
        find(0, share // 2)

    find(share // 2, share)

    def block(rotation, part):
        return rotations.at[rotation, pl.ds(part * share, share)]

    def share_of(plane):
        return pltpu.make_async_remote_copy(
            src_ref=rotated.at[pl.ds(first_of(mine, plane), share)],
            dst_ref=block(me, mine),
            send_sem=send_sems.at[1],
            recv_sem=share_sems.at[me],
            device_id=plane_peer(plane),
            device_id_type=MESH,
        )

    def turn_of(rotation, turn):
        return pltpu.make_async_remote_copy(
            src_ref=block(rotation, mine),
            dst_ref=block(rotation, mine),
            send_sem=send_sems.at[2],
            recv_sem=turn_sems.at[rotation],
            device_id=row_peer(turn),
            device_id_type=MESH,
        )

    rotations[me, pl.ds(mine * share, share)] = rotated[pl.ds(first_of(mine, me), share)]
    for turn in range(1, parts):
        turn_of(me, turn).start()
    share_of(partners[1]).start()

    @pl.when(pair > 0)
    def _():
        for i in range(2):
            share_of(2 * pair - 2 + i).start()

    @pl.when(pair < last)
    def _():
        for i in range(2):
            share_of(2 * pair + 2 + i).start()

    @pl.when(pair < last - 1)
    def _():
        pl.semaphore_wait(upper, 1)

    @pl.when(jnp.logical_and(pair > 0, pair < last - 1))
    def _():
        greet(upper, below)

    @pl.when(jnp.logical_and(pair > 1, pair == last))
    def _():
        pl.semaphore_wait(lower, 1)

    for other in range(last + 1):

        @pl.when(jnp.logical_or(other > pair + 1, other < pair - 1))
        def _():
            for i in range(2):
                share_of(2 * other + i).start()

    def forward(steps):
        for step in steps:
            if step:
                arrived = block(partners[step], mine)
                pltpu.make_async_copy(arrived, arrived, share_sems.at[partners[step]]).wait()
                for turn in range(1, parts):
                    turn_of(partners[step], turn).start()

    groups = [list(range(first, first + batch)) for first in range(0, orients, batch)]
    early = 2 * pair < last

    @pl.when(early)
    def _():
        forward(groups[0])

    own.wait()
    for step in range(1, bcols):
        gather_of(step, lax.rem(col_id + bcols - step, bcols)).wait_recv()
    for name in ("forward", "smoothing", "inverse"):
        copies[name].wait()
    both = None
    for part in range(bcols):
        term = dot_short(pencils[part], refs["forward"][part])
        both = term if both is None else both + term
    padded = both.shape[1] // 2
    real, imag = both[:, :padded], both[:, padded:]
    weights = lax.rsqrt(dot_short(real * real + imag * imag, refs["smoothing"][...]) + epsilon)
    windows[me, margin : margin + rows] = dot_short(
        real * weights, refs["inverse"][col_id, :padded, :]
    ) + dot_short(imag * weights, refs["inverse"][col_id, padded:, :])

    def window_of(plane):
        part = windows.at[me, pl.ds(margin, rows)]
        return pltpu.make_async_remote_copy(
            src_ref=part,
            dst_ref=part,
            send_sem=send_sems.at[3],
            recv_sem=window_sems.at[me],
            device_id=plane_peer(plane),
            device_id_type=MESH,
        )

    def margin_of(plane):
        return pltpu.make_async_remote_copy(
            src_ref=windows.at[plane, pl.ds(pl.multiple_of(rows - row_id * (rows - margin), 8), margin)],
            dst_ref=windows.at[plane, pl.ds(pl.multiple_of(row_id * (margin + rows), 8), margin)],
            send_sem=send_sems.at[4],
            recv_sem=margin_sems.at[plane],
            device_id=row_peer(1),
            device_id_type=MESH,
        )

    for k in range(orients - 1):
        window_of(target(k)).start()
    if brows > 1:
        margin_of(me).start()
    for name in ("template_lines", "template_rows", "volume_lines", "volume_rows", "score_rows", "score_lines", "box"):
        copies[name].wait()

    def transform(steps):
        tiles = []
        for step in steps:
            plane = partners[step]
            if brows > 1:
                arrived = windows.at[plane, pl.ds(0, margin)]
                pltpu.make_async_copy(arrived, arrived, margin_sems.at[plane]).wait()
            tile = windows[plane, skip : skip + tile_rows]
            gap = plane - me
            near = jnp.logical_and(gap >= -half_edge, gap < half_edge).astype(jnp.float32)
            energy[...] += tile * tile * near
            tiles.append(tile)
        turned = by_table(jnp.concatenate(tiles, axis=0), refs["volume_lines"][...])
        for first in range(0, len(steps), 2):
            pair = []
            for i in range(first, first + 2):
                part = turned[i * tile_rows : (i + 1) * tile_rows]
                pair.append(jnp.concatenate([part[:, :size], part[:, size:]], axis=0))
            spun = table_by(refs["volume_rows"][...], jnp.concatenate(pair, axis=1))
            for i in range(2):
                volumes[partners[steps[first + i]]] = spun[:, i * size : (i + 1) * size]

    def unfold(steps):
        for step in steps:
            if parts > 1:
                arrived = rotations.at[partners[step], pl.ds(0, orients - share)]
                pltpu.make_async_copy(arrived, arrived, turn_sems.at[partners[step]]).wait()
        planes = jnp.concatenate([rotations[partners[step]][:, 0, :] for step in steps], axis=0)
        width = span * edge
        pieces = [planes[:, j * width : j * width + LANES] for j in range(strips)]
        turned = by_table(jnp.concatenate(pieces, axis=0), refs["template_lines"][...])
        for k in range(2 * span):
            lines[k] = turned[:, k * size : (k + 1) * size]
        count = len(steps) * orients
        for i, step in enumerate(steps):
            for first in range(0, orients, 2):
                pair = [
                    jnp.concatenate(
                        [lines[k, pl.ds(i * orients + slot, strips, stride=count), :] for k in range(2 * span)],
                        axis=0,
                    )
                    for slot in (first, first + 1)
                ]
                spun = table_by(refs["template_rows"][...], jnp.concatenate(pair, axis=1))
                for j in range(2):
                    templates[partners[step], planes_of[first + j]] = spun[:, j * size : (j + 1) * size]

    def spread(steps):
        for step in steps:
            if step:
                arrived = windows.at[partners[step], pl.ds(margin, rows)]
                pltpu.make_async_copy(arrived, arrived, window_sems.at[partners[step]]).wait()
                if brows > 1:
                    margin_of(partners[step]).start()

    @pl.when(jnp.logical_not(early))
    def _():
        forward(groups[0])

    unfold(groups[0])
    for steps in groups[1:]:
        forward(steps)
    for steps in groups:
        spread(steps)
    for steps in groups[1:]:
        unfold(steps)
    for steps in groups:
        transform(steps)

    bunch = math.gcd(orients, 8)

    def combine(lowest):
        def gather(held, start):
            held = list(held)
            for i in range(bunch):
                straight = volumes[start + i, :tile_rows, :]
                crossed = volumes[start + i, tile_rows:, :]
                for j in range(2):
                    wave = templates[lowest + j, start + i]
                    held[2 * j] = held[2 * j] + straight * wave
                    held[2 * j + 1] = held[2 * j + 1] + crossed * wave
            return tuple(held)

        held = (jnp.zeros((tile_rows, size), jnp.float32),) * 4
        if orients == bunch:
            held = gather(held, 0)
        else:
            held = lax.fori_loop(0, orients // bunch, lambda i, h: gather(h, i * bunch), held)
        return jnp.concatenate([jnp.concatenate(held[:2], axis=0), jnp.concatenate(held[2:], axis=0)], axis=1)

    def finish(lowest):
        for first in range(0, bunch, 2):
            turned = table_by(refs["score_rows"][...], combine(lowest + first))
            for i in range(2):
                part = turned[:, i * size : (i + 1) * size]
                start = pl.multiple_of((lowest + first + i) * rows, rows)
                scores[pl.ds(start, rows), :size] = part[:rows]
                scores[pl.ds(start, rows), size:] = part[rows:]

    if orients == bunch:
        finish(0)
    else:
        pl.loop(0, orients // bunch)(lambda i: finish(i * bunch))

    summed = energy[0:rows, :]
    for b in range(1, edge):
        summed = summed + energy[b : b + rows, :]
    upper, lower = halves(summed)
    boxed = product(upper, refs["box"][...]) + product(lower, refs["box"][...])
    scaling_ref[0] = lax.rsqrt(boxed / edge**3 + epsilon)
    scored = by_table(scores[...], refs["score_lines"][...])
    best_ref[0] = jnp.max(scored.reshape(orients, rows, cols), axis=0)
    sent = [
        pencils.at[pl.ds(0, bcols - 1)],
        rotations.at[pl.ds(0, orients - 1), pl.ds(0, share)],
        rotations.at[pl.ds(0, orients), pl.ds(0, orients - share)],
        windows.at[pl.ds(0, orients - 1), pl.ds(margin, rows)],
        windows.at[pl.ds(0, orients), pl.ds(0, margin)],
    ]
    wanted = [bcols > 1, True, parts > 1, True, brows > 1]
    for i, ref in enumerate(sent):
        if wanted[i]:
            pltpu.make_async_copy(ref, ref, send_sems.at[i]).wait()


def dot_short(a, b):
    return jnp.dot(a, b, precision=lax.Precision.HIGH, preferred_element_type=jnp.float32)


names = (
    "template",
    "index",
    "forward",
    "smoothing",
    "inverse",
    "template_lines",
    "template_rows",
    "volume_lines",
    "volume_rows",
    "score_rows",
    "score_lines",
    "box",
)


def staged(sizes, *refs):
    brick, sources = refs[0], refs[1 : len(names) + 1]
    results = refs[len(names) + 1 : len(names) + 3]
    held = refs[len(names) + 3 : 2 * len(names) + 3]
    rest = refs[2 * len(names) + 3 : -1]
    copies = {
        name: pltpu.make_async_copy(source, target, refs[-1].at[i])
        for i, (name, source, target) in enumerate(zip(names, sources, held))
    }
    named = dict(zip(names, held), brick=brick)
    match_kernel(sizes, named, copies, *rest, *results)


def shards(volume, template, voxel_maps):
    orients, brows, bcols = (lax.axis_size(axis) for axis in ("orient", "brow", "bcol"))
    planes, rows, cols = volume.shape
    edge = template.shape[0]
    half_edge = edge // 2
    length = cols * bcols
    size = cols + edge
    tile_rows = rows + edge
    margin = round_up(half_edge, 8)
    strips = 8
    batch = math.gcd(orients, 4)
    parts = brows if orients % (2 * brows) == 0 else 1
    base = half_edge - orients
    assert brows <= 2 and margin <= rows and tile_rows <= rows + 2 * margin
    assert base % 2 == 0 and orients % 2 == 0
    assert edge % strips == 0 and edge // strips * edge <= LANES
    width = edge // strips * edge * (strips - 1) + LANES
    width = round_up(width, LANES)
    vmem = pl.BlockSpec(memory_space=pltpu.VMEM)
    constants = (
        forward_table(length, bcols),
        smoothing_table(length),
        windowed_inverse(length, bcols, half_edge),
        template_lines(edge, size, strips),
        template_rows(tile_rows, edge, strips),
        right_table(line_table(size, size)),
        volume_rows(tile_rows),
        score_rows(tile_rows, rows),
        score_lines(size, cols),
        box_table(size, cols, edge),
    )
    sizes = (orients, brows, bcols, parts, edge, base, margin, batch, strips)
    operands = (volume, template.reshape(edge * edge, edge), voxel_maps)
    operands += tuple(jnp.asarray(c) for c in constants)
    best, scaling = pl.pallas_call(
        lambda *refs: staged(sizes, *refs),
        out_shape=(pltpu.VMEM((1, rows, cols), jnp.float32),) * 2,
        in_specs=[pl.BlockSpec(memory_space=pl.ANY)] * len(operands),
        out_specs=(vmem, vmem),
        scratch_shapes=[pltpu.VMEM(x.shape, x.dtype) for x in operands[1:]]
        + [
            pltpu.VMEM((2 * orients // parts, 1, width), jnp.float32),
            pltpu.VMEM((orients, orients, 1, width), jnp.float32),
            pltpu.VMEM((2 * edge // strips, strips * batch * orients, size), jnp.float32),
            pltpu.VMEM((orients, orients, tile_rows, size), jnp.float32),
            pltpu.VMEM((orients, 2 * tile_rows, size), jnp.float32),
            pltpu.VMEM((bcols, rows, cols), jnp.float32),
            pltpu.VMEM((orients, rows + 2 * margin, size), jnp.float32),
            pltpu.VMEM((tile_rows, size), jnp.float32),
            pltpu.VMEM((orients * rows, 2 * size), jnp.float32),
            pltpu.VMEM((edge * edge, edge), jnp.float32),
            pltpu.VMEM((2 * round_up(edge * edge // 8, 16), 8 * edge), jnp.bfloat16),
            pltpu.SemaphoreType.DMA,
            pltpu.SemaphoreType.DMA((bcols,)),
            pltpu.SemaphoreType.DMA((orients,)),
            pltpu.SemaphoreType.DMA((orients,)),
            pltpu.SemaphoreType.DMA((orients,)),
            pltpu.SemaphoreType.DMA((orients,)),
            pltpu.SemaphoreType.DMA((5,)),
            pltpu.SemaphoreType.REGULAR((2,)),
            pltpu.SemaphoreType.DMA((len(names),)),
        ],
        compiler_params=pltpu.CompilerParams(collective_id=0, has_side_effects=True),
        name="match",
    )(*operands)
    return best * scaling


def solution(mesh):
    in_specs = (P("orient", "brow", "bcol"), P(), P("orient", None))
    out_specs = P("orient", "brow", "bcol")
    return jax.shard_map(shards, mesh=mesh, in_specs=in_specs, out_specs=out_specs, check_vma=False)
```

```python
import math

import numpy as np
import jax
import jax.numpy as jnp
from jax import lax
from jax.experimental import pallas as pl
from jax.experimental.pallas import tpu as pltpu
from jax.sharding import PartitionSpec as P

epsilon = 1e-06
floor_share = 0.1
LANES = 128
MESH = pl.DeviceIdType.MESH


def round_up(value, step):
    return -(-value // step) * step


def forward_table(length, parts):
    half = length // 2 + 1
    padded = round_up(half, LANES)
    angles = 2.0 * np.pi * (np.outer(np.arange(length), np.arange(half)) % length) / length
    table = np.zeros((length, 2 * padded))
    table[:, :half] = np.cos(angles)
    table[:, padded : padded + half] = -np.sin(angles)
    return table.reshape(parts, length // parts, 2 * padded).astype(np.float32)


def smoothing_table(length):
    half = length // 2 + 1
    padded = round_up(half, LANES)
    table = np.zeros((padded, padded))
    fold = np.minimum(np.arange(length), length - np.arange(length))
    for k in range(half):
        for shift in (-1, 0, 1):
            table[fold[(k + shift) % length], k] += 1.0 / 3.0
        for other in range(length):
            table[fold[other], k] += floor_share / length
    return table.astype(np.float32)


def windowed_inverse(length, parts, margin):
    half = length // 2 + 1
    padded = round_up(half, LANES)
    width = length // parts
    tables = np.zeros((parts, 2 * padded, width + 2 * margin))
    k = np.arange(half)
    share = np.where((k == 0) | (2 * k == length), 1.0, 2.0)[:, None] / math.sqrt(length)
    for part in range(parts):
        columns = np.arange(width + 2 * margin) + part * width - margin
        inside = (columns >= 0) & (columns < length)
        angles = 2.0 * np.pi * (np.outer(k, columns) % length) / length
        tables[part, :half] = share * np.cos(angles) * inside
        tables[part, padded : padded + half] = -share * np.sin(angles) * inside
    return tables.astype(np.float32)


def split(table):
    upper = table.astype(jnp.bfloat16)
    lower = (table - upper.astype(np.float64)).astype(jnp.bfloat16)
    return upper, lower


def left_table(table):
    upper, lower = split(table)
    return np.concatenate([upper, lower, upper], axis=1)


def right_table(table):
    upper, lower = split(table)
    return np.concatenate([upper, upper, lower], axis=0)


def odd_waves(count, size):
    angles = np.pi * (np.outer(np.arange(count), 2 * np.arange(size // 2) + 1) % (2 * size)) / size
    return np.cos(angles), np.sin(angles)


def line_table(count, size):
    cos, sin = odd_waves(count, size)
    return np.concatenate([cos, -sin, -sin, -cos], axis=1)


def row_waves(size, count):
    angles = 2.0 * np.pi * (np.outer(np.arange(size), np.arange(count)) % size) / size
    return np.cos(angles), np.sin(angles)


def template_lines(edge, size, strips):
    span = edge // strips
    waves = line_table(edge, size)
    table = np.zeros((LANES, 2, span, size))
    for b in range(span):
        for half in range(2):
            table[b * edge : (b + 1) * edge, half, b] = waves[:, half * size : (half + 1) * size]
    return right_table(table.reshape(LANES, -1))


def template_rows(size, edge, strips):
    order = np.arange(edge).reshape(strips, edge // strips).T.reshape(-1)
    return left_table(np.concatenate([wave[:, order] for wave in row_waves(size, edge)], axis=1))


def volume_rows(size):
    cos, sin = row_waves(size, size)
    return left_table(np.block([[cos, sin], [-sin, cos]]))


def score_rows(size, rows):
    cos, sin = (wave.T / size for wave in row_waves(size, rows))
    return left_table(np.block([[cos, -sin], [sin, cos]]))


def score_lines(size, count):
    cos, sin = (wave.T * (2.0 / size) for wave in odd_waves(count, size))
    return right_table(np.concatenate([cos, cos, -sin, -sin], axis=0))


def box_table(size, count, edge):
    offsets = np.arange(size)[:, None] - np.arange(count)[None, :]
    return ((offsets >= 0) & (offsets < edge)).astype(jnp.bfloat16)


def split_table(template_ref, normed):
    lines, edge = template_ref.shape
    template = template_ref[...]
    centred = template - jnp.sum(template, keepdims=True) / (lines * edge)
    normed[...] = centred / jnp.sqrt(jnp.sum(centred * centred, keepdims=True) + epsilon)
    table = jnp.concatenate([normed[pl.ds(j, lines // 8, stride=8), :] for j in range(8)], axis=1)
    spare = round_up(lines // 8, 16) - lines // 8
    table = jnp.concatenate([table, jnp.zeros((spare, 8 * edge), jnp.float32)], axis=0)
    upper = table.astype(jnp.bfloat16)
    lower = (table - upper.astype(jnp.float32)).astype(jnp.bfloat16)
    return jnp.concatenate([upper, lower], axis=0)


def look_up(pieces, index):
    count, span = pieces.shape
    width = index.shape[1]
    high = ((index.astype(jnp.float32) + 0.5) * (1.0 / span)).astype(jnp.int32)
    low = index - high * span
    chosen = lax.broadcasted_iota(jnp.int32, (span, width), 0) == low
    lanes = jnp.dot(
        pieces,
        jnp.where(chosen, 1.0, 0.0).astype(jnp.bfloat16),
        preferred_element_type=jnp.float32,
    )
    lanes = lanes[: count // 2] + lanes[count // 2 :]
    mine = lax.broadcasted_iota(jnp.int32, lanes.shape, 0) == high
    return jnp.sum(jnp.where(mine, lanes, 0.0), axis=0, keepdims=True)


def halves(x):
    upper = x.astype(jnp.bfloat16)
    return upper, (x - upper.astype(jnp.float32)).astype(jnp.bfloat16)


def product(a, b):
    return jnp.dot(a, b, preferred_element_type=jnp.float32)


def by_table(x, table):
    upper, lower = halves(x)
    return product(jnp.concatenate([upper, lower, upper], axis=1), table)


def table_by(table, x):
    upper, lower = halves(x)
    return product(table, jnp.concatenate([upper, upper, lower], axis=0))


def match_kernel(
    sizes,
    refs,
    copies,
    rotated,
    rotations,
    lines,
    templates,
    volumes,
    pencils,
    windows,
    energy,
    scores,
    normed,
    table,
    own_sem,
    gather_sems,
    share_sems,
    turn_sems,
    window_sems,
    margin_sems,
    send_sems,
    tokens,
    best_ref,
    scaling_ref,
):
    orients, brows, bcols, parts, edge, base, margin, batch, strips = sizes
    half_edge = edge // 2
    rows, cols = refs["brick"].shape[1:]
    tile_rows, size = energy.shape
    skip = margin - half_edge
    me = lax.axis_index("orient")
    row_id = lax.axis_index("brow")
    col_id = lax.axis_index("bcol")
    share = orients // parts
    mine = lax.rem(row_id, parts)
    plane_voxels = edge * edge
    span = edge // strips

    def column_peer(column):
        return {"orient": me, "brow": row_id, "bcol": column}

    def partner(step):
        assert orients & (orients - 1) == 0
        other, weight = 0, 1
        while weight < orients:
            other = other + lax.rem(me // weight + step // weight, 2) * weight
            weight *= 2
        return other

    partners = [partner(step) for step in range(orients)]
    pair, last = me // 2, orients // 2 - 1
    odd = lax.rem(me, 2)
    by_column, by_row, by_pair, by_near, by_far = (tokens.at[i] for i in range(5))

    def plane_peer(plane):
        return {"orient": plane, "brow": row_id, "bcol": col_id}

    def row_peer(row):
        return {"orient": me, "brow": row, "bcol": col_id}

    def expect(semaphore, count):
        pl.when(count > 0)(lambda: pl.semaphore_wait(semaphore, count))

    def each(count, own, step, do):
        for other in range(count):

            @pl.when(step * other > step * own)
            def _():
                do(other)

    def greet(semaphore, peer):
        pl.semaphore_signal(semaphore, inc=1, device_id=peer, device_id_type=MESH)

    def first_of(part, plane):
        start = orients - plane
        rest = lax.rem(start, 2 * parts) + 2 * parts - 2 * part
        return start // (2 * parts) * 2 + (rest - 1) // (2 * parts) + (rest - 2) // (2 * parts)

    def plane_of(slot):
        part, index = slot // share, slot % share
        found = first_of(part, me) + index
        return found // 2 * (2 * parts) + 2 * part + lax.rem(found, 2) - orients + me

    windows[...] = jnp.zeros_like(windows)
    barrier = pltpu.get_barrier_semaphore()
    @pl.when(odd == 0)
    def _():
        each(orients, me, 1, lambda plane: greet(barrier, plane_peer(plane)))

    @pl.when(odd == 1)
    def _():
        each(orients // 2, pair, 1, lambda other: greet(barrier, plane_peer(2 * other + 1)))

    each(bcols, col_id, 1, lambda column: greet(barrier, column_peer(column)))
    each(brows, row_id, 1, lambda row: greet(barrier, row_peer(row)))
    for copy in copies.values():
        copy.start()
    own = pltpu.make_async_copy(refs["brick"].at[0], pencils.at[col_id], own_sem)
    own.start()
    energy[...] = jnp.zeros_like(energy)
    rotated[...] = jnp.zeros_like(rotated)
    planes_of = [plane_of(slot) for slot in range(orients)]

    def tabulate():
        copies["template"].wait()
        table[...] = split_table(refs["template"], normed)
        copies["index"].wait()

    def find(first, end):
        @pl.loop(first, end)
        def _(index):
            plane = base + 2 * mine + 2 * parts * index

            def fill():
                start = pl.multiple_of(plane * plane_voxels, 2 * plane_voxels)
                found = look_up(table[...], refs["index"][0:1, pl.ds(start, 2 * plane_voxels)])
                for i in range(2):
                    rotated[2 * index + i, :, :plane_voxels] = found[:, i * plane_voxels : (i + 1) * plane_voxels]

            if base < 0 or base + 2 * orients > edge:
                pl.when(jnp.logical_and(plane >= 0, plane < edge))(fill)
            else:
                fill()

    expect(barrier, pair + odd * (pair + 1) + col_id + row_id)

    def gather_of(column):
        return pltpu.make_async_remote_copy(
            src_ref=refs["brick"].at[0],
            dst_ref=pencils.at[col_id],
            send_sem=send_sems.at[0],
            recv_sem=gather_sems.at[col_id],
            device_id=column_peer(column),
            device_id_type=MESH,
        )

    each(bcols, col_id, -1, lambda column: gather_of(column).start())
    each(bcols, col_id, -1, lambda column: greet(by_column, column_peer(column)))
    each(brows, row_id, -1, lambda row: greet(by_row, row_peer(row)))

    @pl.when(odd == 1)
    def _():
        def answer(other):
            for i in range(2):
                greet(by_far, plane_peer(2 * other + i))

        greet(by_pair, plane_peer(me - 1))
        each(orients // 2, pair - 1, -1, answer)

        @pl.when(pair > 0)
        def _():
            for i in range(2):
                greet(by_near, plane_peer(2 * pair - 2 + i))

    tabulate()
    find(0, share // 4)
    expect(by_column, bcols - 1 - col_id)
    each(bcols, col_id, 1, lambda column: gather_of(column).start())
    find(share // 4, share)
    expect(by_row, brows - 1 - row_id)

    def block(rotation, part):
        return rotations.at[rotation, pl.ds(part * share, share)]

    def share_of(plane):
        return pltpu.make_async_remote_copy(
            src_ref=rotated.at[pl.ds(first_of(mine, plane), share)],
            dst_ref=block(me, mine),
            send_sem=send_sems.at[1],
            recv_sem=share_sems.at[me],
            device_id=plane_peer(plane),
            device_id_type=MESH,
        )

    def turn_of(rotation, turn):
        row = lax.rem(row_id + turn, brows)
        return pltpu.make_async_remote_copy(
            src_ref=block(rotation, mine),
            dst_ref=block(rotation, mine),
            send_sem=send_sems.at[2],
            recv_sem=turn_sems.at[rotation],
            device_id=row_peer(row),
            device_id_type=MESH,
        )

    rotations[me, pl.ds(mine * share, share)] = rotated[pl.ds(first_of(mine, me), share)]
    for turn in range(1, parts):
        turn_of(me, turn).start()
    expect(by_pair, 1 - odd)
    each(orients, me, -1, lambda plane: share_of(plane).start())
    pl.when(odd == 0)(lambda: share_of(me + 1).start())
    near = (2 * last - pair) // (last + 1)
    far = last - pair - near

    def send(kind, planes):
        def one(plane):
            if planes == "near":
                pl.when(plane < 2 * pair + 4)(lambda: kind(plane).start())
            else:
                pl.when(plane >= 2 * pair + 4)(lambda: kind(plane).start())

        each(orients, 2 * pair + 1, 1, one)

    expect(by_near, near)
    send(share_of, "near")

    def forward(steps):
        for step in steps:
            if step:
                arrived = block(partners[step], mine)
                pltpu.make_async_copy(arrived, arrived, share_sems.at[partners[step]]).wait()
                for turn in range(1, parts):
                    turn_of(partners[step], turn).start()

    groups = [list(range(first, first + batch)) for first in range(0, orients, batch)]
    own.wait()
    for step in range(1, bcols):
        column = lax.rem(col_id + step, bcols)
        arrived = pencils.at[column]
        pltpu.make_async_copy(arrived, arrived, gather_sems.at[column]).wait()
    for name in ("forward", "smoothing", "inverse"):
        copies[name].wait()
    both = None
    for part in range(bcols):
        term = dot_short(pencils[part], refs["forward"][part])
        both = term if both is None else both + term
    padded = both.shape[1] // 2
    real, imag = both[:, :padded], both[:, padded:]
    weights = lax.rsqrt(dot_short(real * real + imag * imag, refs["smoothing"][...]) + epsilon)
    windows[me, margin : margin + rows] = dot_short(
        real * weights, refs["inverse"][col_id, :padded, :]
    ) + dot_short(imag * weights, refs["inverse"][col_id, padded:, :])

    def window_of(plane):
        part = windows.at[me, pl.ds(margin, rows)]
        return pltpu.make_async_remote_copy(
            src_ref=part,
            dst_ref=part,
            send_sem=send_sems.at[3],
            recv_sem=window_sems.at[me],
            device_id=plane_peer(plane),
            device_id_type=MESH,
        )

    def margin_of(plane):
        return pltpu.make_async_remote_copy(
            src_ref=windows.at[plane, pl.ds(pl.multiple_of(rows - row_id * (rows - margin), 8), margin)],
            dst_ref=windows.at[plane, pl.ds(pl.multiple_of(row_id * (margin + rows), 8), margin)],
            send_sem=send_sems.at[4],
            recv_sem=margin_sems.at[plane],
            device_id=row_peer(lax.rem(row_id + 1, brows)),
            device_id_type=MESH,
        )

    each(orients, me, -1, lambda plane: window_of(plane).start())
    pl.when(odd == 0)(lambda: window_of(me + 1).start())
    send(window_of, "near")
    if brows > 1:
        margin_of(me).start()
    for name in ("template_lines", "template_rows", "volume_lines", "volume_rows", "score_rows", "score_lines", "box"):
        copies[name].wait()

    def transform(steps):
        tiles = []
        for step in steps:
            plane = partners[step]
            if brows > 1:
                arrived = windows.at[plane, pl.ds(0, margin)]
                pltpu.make_async_copy(arrived, arrived, margin_sems.at[plane]).wait()
            tile = windows[plane, skip : skip + tile_rows]
            gap = plane - me
            near = jnp.logical_and(gap >= -half_edge, gap < half_edge).astype(jnp.float32)
            energy[...] += tile * tile * near
            tiles.append(tile)
        turned = by_table(jnp.concatenate(tiles, axis=0), refs["volume_lines"][...])
        for first in range(0, len(steps), 2):
            pair = []
            for i in range(first, first + 2):
                part = turned[i * tile_rows : (i + 1) * tile_rows]
                pair.append(jnp.concatenate([part[:, :size], part[:, size:]], axis=0))
            spun = table_by(refs["volume_rows"][...], jnp.concatenate(pair, axis=1))
            for i in range(2):
                volumes[partners[steps[first + i]]] = spun[:, i * size : (i + 1) * size]

    def unfold(steps):
        for step in steps:
            if parts > 1:
                arrived = rotations.at[partners[step], pl.ds(0, orients - share)]
                pltpu.make_async_copy(arrived, arrived, turn_sems.at[partners[step]]).wait()
        width = span * edge
        pieces = []
        for step in steps:
            planes = rotations[partners[step]][:, 0, :]
            pieces += [planes[:, j * width : j * width + LANES] for j in range(strips)]
        turned = by_table(jnp.concatenate(pieces, axis=0), refs["template_lines"][...])
        for k in range(2 * span):
            lines[k] = turned[:, k * size : (k + 1) * size]
        for i, step in enumerate(steps):
            for first in range(0, orients, 2):
                pair = [
                    jnp.concatenate(
                        [lines[k, pl.ds(i * strips * orients + slot, strips, stride=orients), :] for k in range(2 * span)],
                        axis=0,
                    )
                    for slot in (first, first + 1)
                ]
                spun = table_by(refs["template_rows"][...], jnp.concatenate(pair, axis=1))
                for j in range(2):
                    templates[partners[step], planes_of[first + j]] = spun[:, j * size : (j + 1) * size]

    def spread(steps):
        for step in steps:
            if step:
                arrived = windows.at[partners[step], pl.ds(margin, rows)]
                pltpu.make_async_copy(arrived, arrived, window_sems.at[partners[step]]).wait()
                if brows > 1:
                    margin_of(partners[step]).start()

    forward(groups[0])
    expect(by_far, far)
    send(share_of, "far")
    send(window_of, "far")
    unfold(groups[0])
    spread(groups[0])
    for steps in groups[1:]:
        forward(steps)
    transform(groups[0])
    for steps in groups[1:]:
        unfold(steps)
        spread(steps)
        transform(steps)

    bunch = math.gcd(orients, 8)

    def combine(lowest):
        def gather(held, start):
            held = list(held)
            for i in range(bunch):
                straight = volumes[start + i, :tile_rows, :]
                crossed = volumes[start + i, tile_rows:, :]
                for j in range(2):
                    wave = templates[lowest + j, start + i]
                    held[2 * j] = held[2 * j] + straight * wave
                    held[2 * j + 1] = held[2 * j + 1] + crossed * wave
            return tuple(held)

        held = (jnp.zeros((tile_rows, size), jnp.float32),) * 4
        if orients == bunch:
            held = gather(held, 0)
        else:
            held = lax.fori_loop(0, orients // bunch, lambda i, h: gather(h, i * bunch), held)
        return jnp.concatenate([jnp.concatenate(held[:2], axis=0), jnp.concatenate(held[2:], axis=0)], axis=1)

    def finish(lowest):
        for first in range(0, bunch, 2):
            turned = table_by(refs["score_rows"][...], combine(lowest + first))
            for i in range(2):
                part = turned[:, i * size : (i + 1) * size]
                start = pl.multiple_of((lowest + first + i) * rows, rows)
                scores[pl.ds(start, rows), :size] = part[:rows]
                scores[pl.ds(start, rows), size:] = part[rows:]

    if orients == bunch:
        finish(0)
    else:
        pl.loop(0, orients // bunch)(lambda i: finish(i * bunch))

    summed = energy[0:rows, :]
    for b in range(1, edge):
        summed = summed + energy[b : b + rows, :]
    upper, lower = halves(summed)
    boxed = product(upper, refs["box"][...]) + product(lower, refs["box"][...])
    scaling_ref[0] = lax.rsqrt(boxed / edge**3 + epsilon)
    scored = by_table(scores[...], refs["score_lines"][...])
    best_ref[0] = jnp.max(scored.reshape(orients, rows, cols), axis=0)
    sent = [
        pencils.at[pl.ds(0, bcols - 1)],
        rotations.at[pl.ds(0, orients - 1), pl.ds(0, share)],
        rotations.at[pl.ds(0, orients), pl.ds(0, orients - share)],
        windows.at[pl.ds(0, orients - 1), pl.ds(margin, rows)],
        windows.at[pl.ds(0, orients), pl.ds(0, margin)],
    ]
    wanted = [bcols > 1, True, parts > 1, True, brows > 1]
    for i, ref in enumerate(sent):
        if wanted[i]:
            pltpu.make_async_copy(ref, ref, send_sems.at[i]).wait()


def dot_short(a, b):
    return jnp.dot(a, b, precision=lax.Precision.HIGH, preferred_element_type=jnp.float32)


names = (
    "template",
    "index",
    "forward",
    "smoothing",
    "inverse",
    "template_lines",
    "template_rows",
    "volume_lines",
    "volume_rows",
    "score_rows",
    "score_lines",
    "box",
)


def staged(sizes, *refs):
    brick, sources = refs[0], refs[1 : len(names) + 1]
    results = refs[len(names) + 1 : len(names) + 3]
    held = refs[len(names) + 3 : 2 * len(names) + 3]
    rest = refs[2 * len(names) + 3 : -1]
    copies = {
        name: pltpu.make_async_copy(source, target, refs[-1].at[i])
        for i, (name, source, target) in enumerate(zip(names, sources, held))
    }
    named = dict(zip(names, held), brick=brick)
    match_kernel(sizes, named, copies, *rest, *results)


def shards(volume, template, voxel_maps):
    orients, brows, bcols = (lax.axis_size(axis) for axis in ("orient", "brow", "bcol"))
    planes, rows, cols = volume.shape
    edge = template.shape[0]
    half_edge = edge // 2
    length = cols * bcols
    size = cols + edge
    tile_rows = rows + edge
    margin = round_up(half_edge, 8)
    strips = 8
    batch = math.gcd(orients, 4)
    parts = brows if orients % (2 * brows) == 0 else 1
    base = half_edge - orients
    assert brows <= 2 and margin <= rows and tile_rows <= rows + 2 * margin
    assert base % 2 == 0 and orients % 2 == 0
    assert edge % strips == 0 and edge // strips * edge <= LANES
    width = edge // strips * edge * (strips - 1) + LANES
    width = round_up(width, LANES)
    vmem = pl.BlockSpec(memory_space=pltpu.VMEM)
    constants = (
        forward_table(length, bcols),
        smoothing_table(length),
        windowed_inverse(length, bcols, half_edge),
        template_lines(edge, size, strips),
        template_rows(tile_rows, edge, strips),
        right_table(line_table(size, size)),
        volume_rows(tile_rows),
        score_rows(tile_rows, rows),
        score_lines(size, cols),
        box_table(size, cols, edge),
    )
    sizes = (orients, brows, bcols, parts, edge, base, margin, batch, strips)
    operands = (volume, template.reshape(edge * edge, edge), voxel_maps)
    operands += tuple(jnp.asarray(c) for c in constants)
    best, scaling = pl.pallas_call(
        lambda *refs: staged(sizes, *refs),
        out_shape=(pltpu.VMEM((1, rows, cols), jnp.float32),) * 2,
        in_specs=[pl.BlockSpec(memory_space=pl.ANY)] * len(operands),
        out_specs=(vmem, vmem),
        scratch_shapes=[pltpu.VMEM(x.shape, x.dtype) for x in operands[1:]]
        + [
            pltpu.VMEM((2 * orients // parts, 1, width), jnp.float32),
            pltpu.VMEM((orients, orients, 1, width), jnp.float32),
            pltpu.VMEM((2 * edge // strips, strips * batch * orients, size), jnp.float32),
            pltpu.VMEM((orients, orients, tile_rows, size), jnp.float32),
            pltpu.VMEM((orients, 2 * tile_rows, size), jnp.float32),
            pltpu.VMEM((bcols, rows, cols), jnp.float32),
            pltpu.VMEM((orients, rows + 2 * margin, size), jnp.float32),
            pltpu.VMEM((tile_rows, size), jnp.float32),
            pltpu.VMEM((orients * rows, 2 * size), jnp.float32),
            pltpu.VMEM((edge * edge, edge), jnp.float32),
            pltpu.VMEM((2 * round_up(edge * edge // 8, 16), 8 * edge), jnp.bfloat16),
            pltpu.SemaphoreType.DMA,
            pltpu.SemaphoreType.DMA((bcols,)),
            pltpu.SemaphoreType.DMA((orients,)),
            pltpu.SemaphoreType.DMA((orients,)),
            pltpu.SemaphoreType.DMA((orients,)),
            pltpu.SemaphoreType.DMA((orients,)),
            pltpu.SemaphoreType.DMA((5,)),
            pltpu.SemaphoreType.REGULAR((5,)),
            pltpu.SemaphoreType.DMA((len(names),)),
        ],
        compiler_params=pltpu.CompilerParams(collective_id=0, has_side_effects=True),
        name="match",
    )(*operands)
    return best * scaling


def solution(mesh):
    in_specs = (P("orient", "brow", "bcol"), P(), P("orient", None))
    out_specs = P("orient", "brow", "bcol")
    return jax.shard_map(shards, mesh=mesh, in_specs=in_specs, out_specs=out_specs, check_vma=False)
```

```python
import math

import numpy as np
import jax
import jax.numpy as jnp
from jax import lax
from jax.experimental import pallas as pl
from jax.experimental.pallas import tpu as pltpu
from jax.sharding import PartitionSpec as P

epsilon = 1e-06
floor_share = 0.1
LANES = 128
MESH = pl.DeviceIdType.MESH


def round_up(value, step):
    return -(-value // step) * step


def forward_table(length, parts):
    half = length // 2 + 1
    padded = round_up(half, LANES)
    angles = 2.0 * np.pi * (np.outer(np.arange(length), np.arange(half)) % length) / length
    table = np.zeros((length, 2 * padded))
    table[:, :half] = np.cos(angles)
    table[:, padded : padded + half] = -np.sin(angles)
    return table.reshape(parts, length // parts, 2 * padded).astype(np.float32)


def smoothing_table(length):
    half = length // 2 + 1
    padded = round_up(half, LANES)
    table = np.zeros((padded, padded))
    fold = np.minimum(np.arange(length), length - np.arange(length))
    for k in range(half):
        for shift in (-1, 0, 1):
            table[fold[(k + shift) % length], k] += 1.0 / 3.0
        for other in range(length):
            table[fold[other], k] += floor_share / length
    return table.astype(np.float32)


def windowed_inverse(length, parts, margin):
    half = length // 2 + 1
    padded = round_up(half, LANES)
    width = length // parts
    tables = np.zeros((parts, 2 * padded, width + 2 * margin))
    k = np.arange(half)
    share = np.where((k == 0) | (2 * k == length), 1.0, 2.0)[:, None] / math.sqrt(length)
    for part in range(parts):
        columns = np.arange(width + 2 * margin) + part * width - margin
        inside = (columns >= 0) & (columns < length)
        angles = 2.0 * np.pi * (np.outer(k, columns) % length) / length
        tables[part, :half] = share * np.cos(angles) * inside
        tables[part, padded : padded + half] = -share * np.sin(angles) * inside
    return tables.astype(np.float32)


def split(table):
    upper = table.astype(jnp.bfloat16)
    lower = (table - upper.astype(np.float64)).astype(jnp.bfloat16)
    return upper, lower


def left_table(table):
    upper, lower = split(table)
    return np.concatenate([upper, lower, upper], axis=1)


def right_table(table):
    upper, lower = split(table)
    return np.concatenate([upper, upper, lower], axis=0)


def odd_waves(count, size):
    angles = np.pi * (np.outer(np.arange(count), 2 * np.arange(size // 2) + 1) % (2 * size)) / size
    return np.cos(angles), np.sin(angles)


def line_table(count, size):
    cos, sin = odd_waves(count, size)
    return np.concatenate([cos, -sin, -sin, -cos], axis=1)


def row_waves(size, count):
    angles = 2.0 * np.pi * (np.outer(np.arange(size), np.arange(count)) % size) / size
    return np.cos(angles), np.sin(angles)


def template_lines(edge, size, strips):
    span = edge // strips
    waves = line_table(edge, size)
    table = np.zeros((LANES, 2, span, size))
    for b in range(span):
        for half in range(2):
            table[b * edge : (b + 1) * edge, half, b] = waves[:, half * size : (half + 1) * size]
    return right_table(table.reshape(LANES, -1))


def template_rows(size, edge, strips):
    order = np.arange(edge).reshape(strips, edge // strips).T.reshape(-1)
    return left_table(np.concatenate([wave[:, order] for wave in row_waves(size, edge)], axis=1))


def volume_rows(size):
    cos, sin = row_waves(size, size)
    return left_table(np.block([[cos, sin], [-sin, cos]]))


def score_rows(size, rows):
    cos, sin = (wave.T / size for wave in row_waves(size, rows))
    return left_table(np.block([[cos, -sin], [sin, cos]]))


def score_lines(size, count):
    cos, sin = (wave.T * (2.0 / size) for wave in odd_waves(count, size))
    return right_table(np.concatenate([cos, cos, -sin, -sin], axis=0))


def box_table(size, count, edge):
    offsets = np.arange(size)[:, None] - np.arange(count)[None, :]
    return ((offsets >= 0) & (offsets < edge)).astype(jnp.bfloat16)


def split_table(template_ref, shifted):
    lines, edge = template_ref.shape
    template = template_ref[...] - 0.5
    shifted[...] = template
    mean = jnp.sum(template, keepdims=True) / (lines * edge)
    centred = template - mean
    scale = lax.rsqrt(jnp.sum(centred * centred, keepdims=True) + epsilon)
    table = jnp.concatenate([shifted[pl.ds(j, lines // 8, stride=8), :] for j in range(8)], axis=1)
    spare = round_up(lines // 8, 16) - lines // 8
    table = jnp.concatenate([table, jnp.zeros((spare, 8 * edge), jnp.float32)], axis=0)
    return jnp.concatenate(halves(table), axis=0), mean, scale


def look_up(pieces, index):
    count, span = pieces.shape
    width = index.shape[1]
    high = ((index.astype(jnp.float32) + 0.5) * (1.0 / span)).astype(jnp.int32)
    low = (index - high * span).astype(jnp.float32).astype(jnp.bfloat16)
    row = lax.broadcasted_iota(jnp.int32, (span, width), 0).astype(jnp.float32).astype(jnp.bfloat16)
    one = jnp.ones((), jnp.bfloat16)
    lanes = product(pieces, jnp.where(row == low, one, jnp.zeros_like(one)))
    lanes = lanes[: count // 2] + lanes[count // 2 :]
    mine = lax.broadcasted_iota(jnp.int32, lanes.shape, 0) == high
    return jnp.sum(jnp.where(mine, lanes, 0.0), axis=0, keepdims=True)


def halves(x):
    upper = x.astype(jnp.bfloat16)
    return upper, (x - upper.astype(jnp.float32)).astype(jnp.bfloat16)


def product(a, b):
    return jnp.dot(a, b, preferred_element_type=jnp.float32)


def by_table(x, table):
    upper, lower = halves(x)
    return product(jnp.concatenate([upper, lower, upper], axis=1), table)


def table_by(table, x):
    upper, lower = halves(x)
    return product(table, jnp.concatenate([upper, upper, lower], axis=0))


def match_kernel(
    sizes,
    refs,
    copies,
    rotated,
    rotations,
    lines,
    templates,
    volumes,
    pencils,
    windows,
    energy,
    scores,
    normed,
    table,
    stats,
    own_sem,
    gather_sems,
    share_sems,
    turn_sems,
    window_sems,
    margin_sems,
    send_sems,
    tokens,
    best_ref,
    scaling_ref,
):
    orients, brows, bcols, parts, edge, base, margin, batch, strips = sizes
    half_edge = edge // 2
    rows, cols = refs["brick"].shape[1:]
    tile_rows, size = energy.shape
    skip = margin - half_edge
    me = lax.axis_index("orient")
    row_id = lax.axis_index("brow")
    col_id = lax.axis_index("bcol")
    share = orients // parts
    mine = lax.rem(row_id, parts)
    plane_voxels = edge * edge
    span = edge // strips

    def column_peer(column):
        return {"orient": me, "brow": row_id, "bcol": column}

    def partner(step):
        assert orients & (orients - 1) == 0
        other, weight = 0, 1
        while weight < orients:
            other = other + lax.rem(me // weight + step // weight, 2) * weight
            weight *= 2
        return other

    partners = [partner(step) for step in range(orients)]
    pair, last = me // 2, orients // 2 - 1
    odd = lax.rem(me, 2)
    by_column, by_row, by_pair, by_near, by_far = (tokens.at[i] for i in range(5))

    def plane_peer(plane):
        return {"orient": plane, "brow": row_id, "bcol": col_id}

    def row_peer(row):
        return {"orient": me, "brow": row, "bcol": col_id}

    def expect(semaphore, count):
        pl.when(count > 0)(lambda: pl.semaphore_wait(semaphore, count))

    def each(count, own, step, do):
        for other in range(count):

            @pl.when(step * other > step * own)
            def _():
                do(other)

    def greet(semaphore, peer):
        pl.semaphore_signal(semaphore, inc=1, device_id=peer, device_id_type=MESH)

    def first_of(part, plane):
        start = orients - plane
        rest = lax.rem(start, 2 * parts) + 2 * parts - 2 * part
        return start // (2 * parts) * 2 + (rest - 1) // (2 * parts) + (rest - 2) // (2 * parts)

    def plane_of(slot):
        part, index = slot // share, slot % share
        found = first_of(part, me) + index
        return found // 2 * (2 * parts) + 2 * part + lax.rem(found, 2) - orients + me

    windows[...] = jnp.zeros_like(windows)
    barrier = pltpu.get_barrier_semaphore()
    @pl.when(odd == 0)
    def _():
        each(orients, me, 1, lambda plane: greet(barrier, plane_peer(plane)))

    @pl.when(odd == 1)
    def _():
        each(orients // 2, pair, 1, lambda other: greet(barrier, plane_peer(2 * other + 1)))

    each(bcols, col_id, 1, lambda column: greet(barrier, column_peer(column)))
    each(brows, row_id, 1, lambda row: greet(barrier, row_peer(row)))
    tables = ("template_lines", "template_rows", "volume_lines", "volume_rows", "score_rows", "score_lines", "box")
    for name, copy in copies.items():
        if name not in tables:
            copy.start()
    own = pltpu.make_async_copy(refs["brick"].at[0], pencils.at[col_id], own_sem)
    own.start()
    energy[...] = jnp.zeros_like(energy)
    rotated[...] = jnp.zeros_like(rotated)
    planes_of = [plane_of(slot) for slot in range(orients)]

    def tabulate():
        copies["template"].wait()
        table[...], stats[0:1, 0:1], stats[1:2, 0:1] = split_table(refs["template"], normed)
        copies["index"].wait()

    def find(first, end):
        def one(index):
            plane = base + 2 * mine + 2 * parts * index

            def fill():
                start = pl.multiple_of(plane * plane_voxels, 2 * plane_voxels)
                found = look_up(table[...], refs["index"][0:1, pl.ds(start, 2 * plane_voxels)])
                found = (found - stats[0:1, 0:1]) * stats[1:2, 0:1]
                for i in range(2):
                    rotated[2 * index + i, :, :plane_voxels] = found[:, i * plane_voxels : (i + 1) * plane_voxels]

            if base < 0 or base + 2 * orients > edge:
                pl.when(jnp.logical_and(plane >= 0, plane < edge))(fill)
            else:
                fill()

        if share <= 4:
            for index in range(first, end):
                one(index)
        else:
            pl.loop(first, end)(one)

    expect(barrier, pair + odd * (pair + 1) + col_id + row_id)

    def gather_of(column):
        return pltpu.make_async_remote_copy(
            src_ref=refs["brick"].at[0],
            dst_ref=pencils.at[col_id],
            send_sem=send_sems.at[0],
            recv_sem=gather_sems.at[col_id],
            device_id=column_peer(column),
            device_id_type=MESH,
        )

    each(bcols, col_id, -1, lambda column: gather_of(column).start())
    each(bcols, col_id, -1, lambda column: greet(by_column, column_peer(column)))
    each(brows, row_id, -1, lambda row: greet(by_row, row_peer(row)))

    @pl.when(odd == 1)
    def _():
        def answer(other):
            for i in range(2):
                greet(by_far, plane_peer(2 * other + i))

        greet(by_pair, plane_peer(me - 1))
        each(orients // 2, pair - 1, -1, answer)

        @pl.when(pair > 0)
        def _():
            for i in range(2):
                greet(by_near, plane_peer(2 * pair - 2 + i))

    for name in tables:
        copies[name].start()
    tabulate()
    find(0, share // 2)
    expect(by_column, bcols - 1 - col_id)
    each(bcols, col_id, 1, lambda column: gather_of(column).start())
    find(share // 2, share)
    expect(by_row, brows - 1 - row_id)

    def block(rotation, part):
        return rotations.at[rotation, pl.ds(part * share, share)]

    def share_of(plane):
        return pltpu.make_async_remote_copy(
            src_ref=rotated.at[pl.ds(first_of(mine, plane), share)],
            dst_ref=block(me, mine),
            send_sem=send_sems.at[1],
            recv_sem=share_sems.at[me],
            device_id=plane_peer(plane),
            device_id_type=MESH,
        )

    def turn_of(rotation, turn):
        row = lax.rem(row_id + turn, brows)
        return pltpu.make_async_remote_copy(
            src_ref=block(rotation, mine),
            dst_ref=block(rotation, mine),
            send_sem=send_sems.at[2],
            recv_sem=turn_sems.at[rotation],
            device_id=row_peer(row),
            device_id_type=MESH,
        )

    rotations[me, pl.ds(mine * share, share)] = rotated[pl.ds(first_of(mine, me), share)]
    for turn in range(1, parts):
        turn_of(me, turn).start()
    expect(by_pair, 1 - odd)
    each(orients, me, -1, lambda plane: share_of(plane).start())
    pl.when(odd == 0)(lambda: share_of(me + 1).start())
    near = (2 * last - pair) // (last + 1)
    far = last - pair - near

    def send(kind, planes):
        def one(plane):
            if planes == "near":
                pl.when(plane < 2 * pair + 4)(lambda: kind(plane).start())
            else:
                pl.when(plane >= 2 * pair + 4)(lambda: kind(plane).start())

        each(orients, 2 * pair + 1, 1, one)

    expect(by_near, near)
    send(share_of, "near")

    def forward(steps):
        for step in steps:
            if step:
                arrived = block(partners[step], mine)
                pltpu.make_async_copy(arrived, arrived, share_sems.at[partners[step]]).wait()
                for turn in range(1, parts):
                    turn_of(partners[step], turn).start()

    groups = [list(range(first, first + batch)) for first in range(0, orients, batch)]
    own.wait()
    for step in range(1, bcols):
        column = lax.rem(col_id + step, bcols)
        arrived = pencils.at[column]
        pltpu.make_async_copy(arrived, arrived, gather_sems.at[column]).wait()
    for name in ("forward", "smoothing", "inverse"):
        copies[name].wait()
    both = None
    for part in range(bcols):
        term = dot_short(pencils[part], refs["forward"][part])
        both = term if both is None else both + term
    padded = both.shape[1] // 2
    real, imag = both[:, :padded], both[:, padded:]
    weights = lax.rsqrt(dot_short(real * real + imag * imag, refs["smoothing"][...]) + epsilon)
    windows[me, margin : margin + rows] = dot_short(
        real * weights, refs["inverse"][col_id, :padded, :]
    ) + dot_short(imag * weights, refs["inverse"][col_id, padded:, :])

    def window_of(plane):
        part = windows.at[me, pl.ds(margin, rows)]
        return pltpu.make_async_remote_copy(
            src_ref=part,
            dst_ref=part,
            send_sem=send_sems.at[3],
            recv_sem=window_sems.at[me],
            device_id=plane_peer(plane),
            device_id_type=MESH,
        )

    def margin_of(plane):
        return pltpu.make_async_remote_copy(
            src_ref=windows.at[plane, pl.ds(pl.multiple_of(rows - row_id * (rows - margin), 8), margin)],
            dst_ref=windows.at[plane, pl.ds(pl.multiple_of(row_id * (margin + rows), 8), margin)],
            send_sem=send_sems.at[4],
            recv_sem=margin_sems.at[plane],
            device_id=row_peer(lax.rem(row_id + 1, brows)),
            device_id_type=MESH,
        )

    each(orients, me, -1, lambda plane: window_of(plane).start())
    pl.when(odd == 0)(lambda: window_of(me + 1).start())
    send(window_of, "near")
    if brows > 1:
        margin_of(me).start()
    for name in tables:
        copies[name].wait()

    def transform(steps):
        tiles = []
        for step in steps:
            plane = partners[step]
            if brows > 1:
                arrived = windows.at[plane, pl.ds(0, margin)]
                pltpu.make_async_copy(arrived, arrived, margin_sems.at[plane]).wait()
            tile = windows[plane, skip : skip + tile_rows]
            gap = plane - me
            near = jnp.logical_and(gap >= -half_edge, gap < half_edge).astype(jnp.float32)
            energy[...] += tile * tile * near
            tiles.append(tile)
        turned = by_table(jnp.concatenate(tiles, axis=0), refs["volume_lines"][...])
        for first in range(0, len(steps), 2):
            pair = []
            for i in range(first, first + 2):
                part = turned[i * tile_rows : (i + 1) * tile_rows]
                pair.append(jnp.concatenate([part[:, :size], part[:, size:]], axis=0))
            spun = table_by(refs["volume_rows"][...], jnp.concatenate(pair, axis=1))
            for i in range(2):
                volumes[partners[steps[first + i]]] = spun[:, i * size : (i + 1) * size]

    def unfold(steps):
        for step in steps:
            if parts > 1:
                arrived = rotations.at[partners[step], pl.ds(0, orients - share)]
                pltpu.make_async_copy(arrived, arrived, turn_sems.at[partners[step]]).wait()
        width = span * edge
        pieces = []
        for step in steps:
            planes = rotations[partners[step]][:, 0, :]
            pieces += [planes[:, j * width : j * width + LANES] for j in range(strips)]
        turned = by_table(jnp.concatenate(pieces, axis=0), refs["template_lines"][...])
        for k in range(2 * span):
            lines[k] = turned[:, k * size : (k + 1) * size]
        for i, step in enumerate(steps):
            for first in range(0, orients, 2):
                pair = [
                    jnp.concatenate(
                        [lines[k, pl.ds(i * strips * orients + slot, strips, stride=orients), :] for k in range(2 * span)],
                        axis=0,
                    )
                    for slot in (first, first + 1)
                ]
                spun = table_by(refs["template_rows"][...], jnp.concatenate(pair, axis=1))
                for j in range(2):
                    templates[partners[step], planes_of[first + j]] = spun[:, j * size : (j + 1) * size]

    def spread(steps):
        for step in steps:
            if step:
                arrived = windows.at[partners[step], pl.ds(margin, rows)]
                pltpu.make_async_copy(arrived, arrived, window_sems.at[partners[step]]).wait()
                if brows > 1:
                    margin_of(partners[step]).start()

    forward(groups[0])
    expect(by_far, far)
    send(share_of, "far")
    send(window_of, "far")
    unfold(groups[0])
    spread(groups[0])
    for steps in groups[1:]:
        forward(steps)
    transform(groups[0])
    for steps in groups[1:]:
        unfold(steps)
        spread(steps)
        transform(steps)

    bunch = math.gcd(orients, 8)

    def combine(lowest):
        def gather(held, start):
            held = list(held)
            for i in range(bunch):
                straight = volumes[start + i, :tile_rows, :]
                crossed = volumes[start + i, tile_rows:, :]
                for j in range(2):
                    wave = templates[lowest + j, start + i]
                    held[2 * j] = held[2 * j] + straight * wave
                    held[2 * j + 1] = held[2 * j + 1] + crossed * wave
            return tuple(held)

        held = (jnp.zeros((tile_rows, size), jnp.float32),) * 4
        if orients == bunch:
            held = gather(held, 0)
        else:
            held = lax.fori_loop(0, orients // bunch, lambda i, h: gather(h, i * bunch), held)
        return jnp.concatenate([jnp.concatenate(held[:2], axis=0), jnp.concatenate(held[2:], axis=0)], axis=1)

    def finish(lowest):
        for first in range(0, bunch, 2):
            turned = table_by(refs["score_rows"][...], combine(lowest + first))
            for i in range(2):
                part = turned[:, i * size : (i + 1) * size]
                start = pl.multiple_of((lowest + first + i) * rows, rows)
                scores[pl.ds(start, rows), :size] = part[:rows]
                scores[pl.ds(start, rows), size:] = part[rows:]

    if orients == bunch:
        finish(0)
    else:
        pl.loop(0, orients // bunch)(lambda i: finish(i * bunch))

    summed = energy[0:rows, :]
    for b in range(1, edge):
        summed = summed + energy[b : b + rows, :]
    upper, lower = halves(summed)
    boxed = product(upper, refs["box"][...]) + product(lower, refs["box"][...])
    scaling_ref[0] = lax.rsqrt(boxed / edge**3 + epsilon)
    scored = by_table(scores[...], refs["score_lines"][...])
    best_ref[0] = jnp.max(scored.reshape(orients, rows, cols), axis=0)
    sent = [
        pencils.at[pl.ds(0, bcols - 1)],
        rotations.at[pl.ds(0, orients - 1), pl.ds(0, share)],
        rotations.at[pl.ds(0, orients), pl.ds(0, orients - share)],
        windows.at[pl.ds(0, orients - 1), pl.ds(margin, rows)],
        windows.at[pl.ds(0, orients), pl.ds(0, margin)],
    ]
    wanted = [bcols > 1, True, parts > 1, True, brows > 1]
    for i, ref in enumerate(sent):
        if wanted[i]:
            pltpu.make_async_copy(ref, ref, send_sems.at[i]).wait()


def dot_short(a, b):
    return jnp.dot(a, b, precision=lax.Precision.HIGH, preferred_element_type=jnp.float32)


names = (
    "template",
    "index",
    "forward",
    "smoothing",
    "inverse",
    "template_lines",
    "template_rows",
    "volume_lines",
    "volume_rows",
    "score_rows",
    "score_lines",
    "box",
)


def staged(sizes, *refs):
    brick, sources = refs[0], refs[1 : len(names) + 1]
    results = refs[len(names) + 1 : len(names) + 3]
    held = refs[len(names) + 3 : 2 * len(names) + 3]
    rest = refs[2 * len(names) + 3 : -1]
    copies = {
        name: pltpu.make_async_copy(source, target, refs[-1].at[i])
        for i, (name, source, target) in enumerate(zip(names, sources, held))
    }
    named = dict(zip(names, held), brick=brick)
    match_kernel(sizes, named, copies, *rest, *results)


def shards(volume, template, voxel_maps):
    orients, brows, bcols = (lax.axis_size(axis) for axis in ("orient", "brow", "bcol"))
    planes, rows, cols = volume.shape
    edge = template.shape[0]
    half_edge = edge // 2
    length = cols * bcols
    size = cols + edge
    tile_rows = rows + edge
    margin = round_up(half_edge, 8)
    strips = 8
    batch = math.gcd(orients, 4)
    parts = brows if orients % (2 * brows) == 0 else 1
    base = half_edge - orients
    assert brows <= 2 and margin <= rows and tile_rows <= rows + 2 * margin
    assert base % 2 == 0 and orients % 2 == 0
    assert edge % strips == 0 and edge // strips * edge <= LANES
    width = edge // strips * edge * (strips - 1) + LANES
    width = round_up(width, LANES)
    vmem = pl.BlockSpec(memory_space=pltpu.VMEM)
    constants = (
        forward_table(length, bcols),
        smoothing_table(length),
        windowed_inverse(length, bcols, half_edge),
        template_lines(edge, size, strips),
        template_rows(tile_rows, edge, strips),
        right_table(line_table(size, size)),
        volume_rows(tile_rows),
        score_rows(tile_rows, rows),
        score_lines(size, cols),
        box_table(size, cols, edge),
    )
    sizes = (orients, brows, bcols, parts, edge, base, margin, batch, strips)
    operands = (volume, template.reshape(edge * edge, edge), voxel_maps)
    operands += tuple(jnp.asarray(c) for c in constants)
    best, scaling = pl.pallas_call(
        lambda *refs: staged(sizes, *refs),
        out_shape=(pltpu.VMEM((1, rows, cols), jnp.float32),) * 2,
        in_specs=[pl.BlockSpec(memory_space=pl.ANY)] * len(operands),
        out_specs=(vmem, vmem),
        scratch_shapes=[pltpu.VMEM(x.shape, x.dtype) for x in operands[1:]]
        + [
            pltpu.VMEM((2 * orients // parts, 1, width), jnp.float32),
            pltpu.VMEM((orients, orients, 1, width), jnp.float32),
            pltpu.VMEM((2 * edge // strips, strips * batch * orients, size), jnp.float32),
            pltpu.VMEM((orients, orients, tile_rows, size), jnp.float32),
            pltpu.VMEM((orients, 2 * tile_rows, size), jnp.float32),
            pltpu.VMEM((bcols, rows, cols), jnp.float32),
            pltpu.VMEM((orients, rows + 2 * margin, size), jnp.float32),
            pltpu.VMEM((tile_rows, size), jnp.float32),
            pltpu.VMEM((orients * rows, 2 * size), jnp.float32),
            pltpu.VMEM((edge * edge, edge), jnp.float32),
            pltpu.VMEM((2 * round_up(edge * edge // 8, 16), 8 * edge), jnp.bfloat16),
            pltpu.VMEM((8, LANES), jnp.float32),
            pltpu.SemaphoreType.DMA,
            pltpu.SemaphoreType.DMA((bcols,)),
            pltpu.SemaphoreType.DMA((orients,)),
            pltpu.SemaphoreType.DMA((orients,)),
            pltpu.SemaphoreType.DMA((orients,)),
            pltpu.SemaphoreType.DMA((orients,)),
            pltpu.SemaphoreType.DMA((5,)),
            pltpu.SemaphoreType.REGULAR((5,)),
            pltpu.SemaphoreType.DMA((len(names),)),
        ],
        compiler_params=pltpu.CompilerParams(collective_id=0, has_side_effects=True),
        name="match",
    )(*operands)
    return best * scaling


def solution(mesh):
    in_specs = (P("orient", "brow", "bcol"), P(), P("orient", None))
    out_specs = P("orient", "brow", "bcol")
    return jax.shard_map(shards, mesh=mesh, in_specs=in_specs, out_specs=out_specs, check_vma=False)
```

```python
import math

import numpy as np
import jax
import jax.numpy as jnp
from jax import lax
from jax.experimental import pallas as pl
from jax.experimental.pallas import tpu as pltpu
from jax.sharding import PartitionSpec as P

epsilon = 1e-06
floor_share = 0.1
LANES = 128
MESH = pl.DeviceIdType.MESH


def round_up(value, step):
    return -(-value // step) * step


def forward_table(length, parts):
    half = length // 2 + 1
    padded = round_up(half, LANES)
    angles = 2.0 * np.pi * (np.outer(np.arange(length), np.arange(half)) % length) / length
    table = np.zeros((length, 2 * padded))
    table[:, :half] = np.cos(angles)
    table[:, padded : padded + half] = -np.sin(angles)
    return table.reshape(parts, length // parts, 2 * padded).astype(np.float32)


def smoothing_table(length):
    half = length // 2 + 1
    padded = round_up(half, LANES)
    table = np.zeros((padded, padded))
    fold = np.minimum(np.arange(length), length - np.arange(length))
    for k in range(half):
        for shift in (-1, 0, 1):
            table[fold[(k + shift) % length], k] += 1.0 / 3.0
        for other in range(length):
            table[fold[other], k] += floor_share / length
    return table.astype(np.float32)


def windowed_inverse(length, parts, margin):
    half = length // 2 + 1
    padded = round_up(half, LANES)
    width = length // parts
    tables = np.zeros((parts, 2 * padded, width + 2 * margin))
    k = np.arange(half)
    share = np.where((k == 0) | (2 * k == length), 1.0, 2.0)[:, None] / math.sqrt(length)
    for part in range(parts):
        columns = np.arange(width + 2 * margin) + part * width - margin
        inside = (columns >= 0) & (columns < length)
        angles = 2.0 * np.pi * (np.outer(k, columns) % length) / length
        tables[part, :half] = share * np.cos(angles) * inside
        tables[part, padded : padded + half] = -share * np.sin(angles) * inside
    return tables.astype(np.float32)


def split(table):
    upper = table.astype(jnp.bfloat16)
    lower = (table - upper.astype(np.float64)).astype(jnp.bfloat16)
    return upper, lower


def left_table(table):
    upper, lower = split(table)
    return np.concatenate([upper, lower, upper], axis=1)


def right_table(table):
    upper, lower = split(table)
    return np.concatenate([upper, upper, lower], axis=0)


def odd_waves(count, size):
    angles = np.pi * (np.outer(np.arange(count), 2 * np.arange(size // 2) + 1) % (2 * size)) / size
    return np.cos(angles), np.sin(angles)


def line_table(count, size):
    cos, sin = odd_waves(count, size)
    return np.concatenate([cos, -sin, -sin, -cos], axis=1)


def row_waves(size, count):
    angles = 2.0 * np.pi * (np.outer(np.arange(size), np.arange(count)) % size) / size
    return np.cos(angles), np.sin(angles)


def template_lines(edge, size, strips):
    span = edge // strips
    waves = line_table(edge, size)
    table = np.zeros((LANES, 2, span, size))
    for b in range(span):
        for half in range(2):
            table[b * edge : (b + 1) * edge, half, b] = waves[:, half * size : (half + 1) * size]
    return right_table(table.reshape(LANES, -1))


def template_rows(size, edge, strips):
    order = np.arange(edge).reshape(strips, edge // strips).T.reshape(-1)
    return left_table(np.concatenate([wave[:, order] for wave in row_waves(size, edge)], axis=1))


def volume_rows(size):
    cos, sin = row_waves(size, size)
    return left_table(np.block([[cos, sin], [-sin, cos]]))


def score_rows(size, rows):
    cos, sin = (wave.T / size for wave in row_waves(size, rows))
    return left_table(np.block([[cos, -sin], [sin, cos]]))


def score_lines(size, count):
    cos, sin = (wave.T * (2.0 / size) for wave in odd_waves(count, size))
    return right_table(np.concatenate([cos, cos, -sin, -sin], axis=0))


def box_table(size, count, edge):
    offsets = np.arange(size)[:, None] - np.arange(count)[None, :]
    return ((offsets >= 0) & (offsets < edge)).astype(jnp.bfloat16)


def split_table(template_ref, shifted):
    lines, edge = template_ref.shape
    template = template_ref[...] - 0.5
    shifted[...] = template
    mean = jnp.sum(template, keepdims=True) / (lines * edge)
    centred = template - mean
    scale = lax.rsqrt(jnp.sum(centred * centred, keepdims=True) + epsilon)
    table = jnp.concatenate([shifted[pl.ds(j, lines // 8, stride=8), :] for j in range(8)], axis=1)
    spare = round_up(lines // 8, 16) - lines // 8
    table = jnp.concatenate([table, jnp.zeros((spare, 8 * edge), jnp.float32)], axis=0)
    return jnp.concatenate(halves(table), axis=0), mean, scale


def look_up(pieces, index):
    count, span = pieces.shape
    width = index.shape[1]
    high = ((index.astype(jnp.float32) + 0.5) * (1.0 / span)).astype(jnp.int32)
    low = (index - high * span).astype(jnp.float32).astype(jnp.bfloat16)
    row = lax.broadcasted_iota(jnp.int32, (span, width), 0).astype(jnp.float32).astype(jnp.bfloat16)
    one = jnp.ones((), jnp.bfloat16)
    lanes = product(pieces, jnp.where(row == low, one, jnp.zeros_like(one)))
    lanes = lanes[: count // 2] + lanes[count // 2 :]
    mine = lax.broadcasted_iota(jnp.int32, lanes.shape, 0) == high
    return jnp.sum(jnp.where(mine, lanes, 0.0), axis=0, keepdims=True)


def halves(x):
    upper = x.astype(jnp.bfloat16)
    return upper, (x - upper.astype(jnp.float32)).astype(jnp.bfloat16)


def product(a, b):
    return jnp.dot(a, b, preferred_element_type=jnp.float32)


def by_table(x, table):
    upper, lower = halves(x)
    return product(jnp.concatenate([upper, lower, upper], axis=1), table)


def table_by(table, x):
    upper, lower = halves(x)
    return product(table, jnp.concatenate([upper, upper, lower], axis=0))


def match_kernel(
    sizes,
    refs,
    copies,
    rotated,
    rotations,
    lines,
    templates,
    volumes,
    pencils,
    windows,
    energy,
    scores,
    normed,
    table,
    stats,
    own_sem,
    gather_sems,
    share_sems,
    turn_sems,
    window_sems,
    margin_sems,
    send_sems,
    tokens,
    best_ref,
    scaling_ref,
):
    orients, brows, bcols, parts, edge, base, margin, batch, strips = sizes
    half_edge = edge // 2
    rows, cols = refs["brick"].shape[1:]
    tile_rows, size = energy.shape
    skip = margin - half_edge
    me = lax.axis_index("orient")
    row_id = lax.axis_index("brow")
    col_id = lax.axis_index("bcol")
    share = orients // parts
    mine = lax.rem(row_id, parts)
    plane_voxels = edge * edge
    span = edge // strips

    def column_peer(column):
        return {"orient": me, "brow": row_id, "bcol": column}

    def partner(step):
        assert orients & (orients - 1) == 0
        other, weight = 0, 1
        while weight < orients:
            other = other + lax.rem(me // weight + step // weight, 2) * weight
            weight *= 2
        return other

    partners = [partner(step) for step in range(orients)]
    pair, last = me // 2, orients // 2 - 1
    odd = lax.rem(me, 2)
    by_column, by_row, by_pair, by_near, by_far = (tokens.at[i] for i in range(5))

    def plane_peer(plane):
        return {"orient": plane, "brow": row_id, "bcol": col_id}

    def row_peer(row):
        return {"orient": me, "brow": row, "bcol": col_id}

    def expect(semaphore, count):
        pl.when(count > 0)(lambda: pl.semaphore_wait(semaphore, count))

    def each(count, own, step, do):
        for other in range(count):

            @pl.when(step * other > step * own)
            def _():
                do(other)

    def greet(semaphore, peer):
        pl.semaphore_signal(semaphore, inc=1, device_id=peer, device_id_type=MESH)

    def first_of(part, plane):
        start = orients - plane
        rest = lax.rem(start, 2 * parts) + 2 * parts - 2 * part
        return start // (2 * parts) * 2 + (rest - 1) // (2 * parts) + (rest - 2) // (2 * parts)

    def plane_of(slot):
        part, index = slot // share, slot % share
        found = first_of(part, me) + index
        return found // 2 * (2 * parts) + 2 * part + lax.rem(found, 2) - orients + me

    windows[...] = jnp.zeros_like(windows)
    barrier = pltpu.get_barrier_semaphore()
    @pl.when(odd == 0)
    def _():
        each(orients, me, 1, lambda plane: greet(barrier, plane_peer(plane)))

    @pl.when(odd == 1)
    def _():
        each(orients // 2, pair, 1, lambda other: greet(barrier, plane_peer(2 * other + 1)))

    each(bcols, col_id, 1, lambda column: greet(barrier, column_peer(column)))
    each(brows, row_id, 1, lambda row: greet(barrier, row_peer(row)))
    tables = ("template_lines", "template_rows", "volume_lines", "volume_rows", "score_rows", "score_lines", "box")
    for name, copy in copies.items():
        if name not in tables:
            copy.start()
    own = pltpu.make_async_copy(refs["brick"].at[0], pencils.at[col_id], own_sem)
    own.start()
    energy[...] = jnp.zeros_like(energy)
    rotated[...] = jnp.zeros_like(rotated)
    planes_of = [plane_of(slot) for slot in range(orients)]

    def tabulate():
        copies["template"].wait()
        table[...], stats[0:1, 0:1], stats[1:2, 0:1] = split_table(refs["template"], normed)
        copies["index"].wait()

    def find(first, end):
        def one(index):
            plane = base + 2 * mine + 2 * parts * index

            def fill():
                start = pl.multiple_of(plane * plane_voxels, 2 * plane_voxels)
                found = look_up(table[...], refs["index"][0:1, pl.ds(start, 2 * plane_voxels)])
                found = (found - stats[0:1, 0:1]) * stats[1:2, 0:1]
                for i in range(2):
                    rotated[2 * index + i, :, :plane_voxels] = found[:, i * plane_voxels : (i + 1) * plane_voxels]

            if base < 0 or base + 2 * orients > edge:
                pl.when(jnp.logical_and(plane >= 0, plane < edge))(fill)
            else:
                fill()

        if share <= 4:
            for index in range(first, end):
                one(index)
        else:
            pl.loop(first, end)(one)

    expect(barrier, pair + odd * (pair + 1) + col_id + row_id)

    def gather_of(column, brick):
        return pltpu.make_async_remote_copy(
            src_ref=brick,
            dst_ref=pencils.at[col_id],
            send_sem=send_sems.at[0],
            recv_sem=gather_sems.at[col_id],
            device_id=column_peer(column),
            device_id_type=MESH,
        )

    each(bcols, col_id, -1, lambda column: gather_of(column, refs["brick"].at[0]).start())
    each(bcols, col_id, -1, lambda column: greet(by_column, column_peer(column)))
    each(brows, row_id, -1, lambda row: greet(by_row, row_peer(row)))

    @pl.when(odd == 1)
    def _():
        def answer(other):
            for i in range(2):
                greet(by_far, plane_peer(2 * other + i))

        greet(by_pair, plane_peer(me - 1))
        each(orients // 2, pair - 1, -1, answer)

        @pl.when(pair > 0)
        def _():
            for i in range(2):
                greet(by_near, plane_peer(2 * pair - 2 + i))

    for name in tables:
        copies[name].start()
    tabulate()
    find(0, share // 2)
    expect(by_column, bcols - 1 - col_id)
    own.wait()
    each(bcols, col_id, 1, lambda column: gather_of(column, pencils.at[col_id]).start())
    find(share // 2, share)
    expect(by_row, brows - 1 - row_id)

    def block(rotation, part):
        return rotations.at[rotation, pl.ds(part * share, share)]

    def share_of(plane):
        return pltpu.make_async_remote_copy(
            src_ref=rotated.at[pl.ds(first_of(mine, plane), share)],
            dst_ref=block(me, mine),
            send_sem=send_sems.at[1],
            recv_sem=share_sems.at[me],
            device_id=plane_peer(plane),
            device_id_type=MESH,
        )

    def turn_of(rotation, turn):
        row = lax.rem(row_id + turn, brows)
        return pltpu.make_async_remote_copy(
            src_ref=block(rotation, mine),
            dst_ref=block(rotation, mine),
            send_sem=send_sems.at[2],
            recv_sem=turn_sems.at[rotation],
            device_id=row_peer(row),
            device_id_type=MESH,
        )

    rotations[me, pl.ds(mine * share, share)] = rotated[pl.ds(first_of(mine, me), share)]
    for turn in range(1, parts):
        turn_of(me, turn).start()
    expect(by_pair, 1 - odd)
    each(orients, me, -1, lambda plane: share_of(plane).start())
    pl.when(odd == 0)(lambda: share_of(me + 1).start())
    near = (2 * last - pair) // (last + 1)
    far = last - pair - near

    def send(kind, planes):
        def one(plane):
            if planes == "near":
                pl.when(plane < 2 * pair + 4)(lambda: kind(plane).start())
            else:
                pl.when(plane >= 2 * pair + 4)(lambda: kind(plane).start())

        each(orients, 2 * pair + 1, 1, one)

    expect(by_near, near)
    send(share_of, "near")

    def forward(steps):
        for step in steps:
            if step:
                arrived = block(partners[step], mine)
                pltpu.make_async_copy(arrived, arrived, share_sems.at[partners[step]]).wait()
                for turn in range(1, parts):
                    turn_of(partners[step], turn).start()

    groups = [list(range(first, first + batch)) for first in range(0, orients, batch)]
    for name in ("forward", "smoothing", "inverse"):
        copies[name].wait()
    both = dot_short(pencils[col_id], refs["forward"][col_id])
    for step in range(1, bcols):
        column = lax.rem(col_id + step, bcols)
        arrived = pencils.at[column]
        pltpu.make_async_copy(arrived, arrived, gather_sems.at[column]).wait()
    for step in range(1, bcols):
        column = lax.rem(col_id + step, bcols)
        both = both + dot_short(pencils[column], refs["forward"][column])
    padded = both.shape[1] // 2
    real, imag = both[:, :padded], both[:, padded:]
    weights = lax.rsqrt(dot_short(real * real + imag * imag, refs["smoothing"][...]) + epsilon)
    windows[me, margin : margin + rows] = dot_short(
        real * weights, refs["inverse"][col_id, :padded, :]
    ) + dot_short(imag * weights, refs["inverse"][col_id, padded:, :])

    def window_of(plane):
        part = windows.at[me, pl.ds(margin, rows)]
        return pltpu.make_async_remote_copy(
            src_ref=part,
            dst_ref=part,
            send_sem=send_sems.at[3],
            recv_sem=window_sems.at[me],
            device_id=plane_peer(plane),
            device_id_type=MESH,
        )

    def margin_of(plane):
        return pltpu.make_async_remote_copy(
            src_ref=windows.at[plane, pl.ds(pl.multiple_of(rows - row_id * (rows - margin), 8), margin)],
            dst_ref=windows.at[plane, pl.ds(pl.multiple_of(row_id * (margin + rows), 8), margin)],
            send_sem=send_sems.at[4],
            recv_sem=margin_sems.at[plane],
            device_id=row_peer(lax.rem(row_id + 1, brows)),
            device_id_type=MESH,
        )

    each(orients, me, -1, lambda plane: window_of(plane).start())
    pl.when(odd == 0)(lambda: window_of(me + 1).start())
    send(window_of, "near")
    if brows > 1:
        margin_of(me).start()
    for name in tables:
        copies[name].wait()

    def transform(steps):
        tiles = []
        for step in steps:
            plane = partners[step]
            if brows > 1:
                arrived = windows.at[plane, pl.ds(0, margin)]
                pltpu.make_async_copy(arrived, arrived, margin_sems.at[plane]).wait()
            tile = windows[plane, skip : skip + tile_rows]
            gap = plane - me
            near = jnp.logical_and(gap >= -half_edge, gap < half_edge).astype(jnp.float32)
            energy[...] += tile * tile * near
            tiles.append(tile)
        turned = by_table(jnp.concatenate(tiles, axis=0), refs["volume_lines"][...])
        for first in range(0, len(steps), 2):
            pair = []
            for i in range(first, first + 2):
                part = turned[i * tile_rows : (i + 1) * tile_rows]
                pair.append(jnp.concatenate([part[:, :size], part[:, size:]], axis=0))
            spun = table_by(refs["volume_rows"][...], jnp.concatenate(pair, axis=1))
            for i in range(2):
                volumes[partners[steps[first + i]]] = spun[:, i * size : (i + 1) * size]

    def unfold(steps):
        for step in steps:
            if parts > 1:
                arrived = rotations.at[partners[step], pl.ds(0, orients - share)]
                pltpu.make_async_copy(arrived, arrived, turn_sems.at[partners[step]]).wait()
        width = span * edge
        pieces = []
        for step in steps:
            planes = rotations[partners[step]][:, 0, :]
            pieces += [planes[:, j * width : j * width + LANES] for j in range(strips)]
        turned = by_table(jnp.concatenate(pieces, axis=0), refs["template_lines"][...])
        for k in range(2 * span):
            lines[k] = turned[:, k * size : (k + 1) * size]
        for i, step in enumerate(steps):
            for first in range(0, orients, 2):
                pair = [
                    jnp.concatenate(
                        [lines[k, pl.ds(i * strips * orients + slot, strips, stride=orients), :] for k in range(2 * span)],
                        axis=0,
                    )
                    for slot in (first, first + 1)
                ]
                spun = table_by(refs["template_rows"][...], jnp.concatenate(pair, axis=1))
                for j in range(2):
                    templates[partners[step], planes_of[first + j]] = spun[:, j * size : (j + 1) * size]

    def spread(steps):
        for step in steps:
            if step:
                arrived = windows.at[partners[step], pl.ds(margin, rows)]
                pltpu.make_async_copy(arrived, arrived, window_sems.at[partners[step]]).wait()
                if brows > 1:
                    margin_of(partners[step]).start()

    forward(groups[0])
    expect(by_far, far)
    send(share_of, "far")
    send(window_of, "far")
    unfold(groups[0])
    spread(groups[0])
    for steps in groups[1:]:
        forward(steps)
    transform(groups[0])
    for steps in groups[1:]:
        spread(steps)
        unfold(steps)
        transform(steps)

    bunch = math.gcd(orients, 8)

    def combine(lowest):
        def gather(held, start):
            held = list(held)
            for i in range(bunch):
                straight = volumes[start + i, :tile_rows, :]
                crossed = volumes[start + i, tile_rows:, :]
                for j in range(2):
                    wave = templates[lowest + j, start + i]
                    held[2 * j] = held[2 * j] + straight * wave
                    held[2 * j + 1] = held[2 * j + 1] + crossed * wave
            return tuple(held)

        held = (jnp.zeros((tile_rows, size), jnp.float32),) * 4
        if orients == bunch:
            held = gather(held, 0)
        else:
            held = lax.fori_loop(0, orients // bunch, lambda i, h: gather(h, i * bunch), held)
        return jnp.concatenate([jnp.concatenate(held[:2], axis=0), jnp.concatenate(held[2:], axis=0)], axis=1)

    def finish(lowest):
        for first in range(0, bunch, 2):
            turned = table_by(refs["score_rows"][...], combine(lowest + first))
            for i in range(2):
                part = turned[:, i * size : (i + 1) * size]
                start = pl.multiple_of((lowest + first + i) * rows, rows)
                scores[pl.ds(start, rows), :size] = part[:rows]
                scores[pl.ds(start, rows), size:] = part[rows:]

    if orients == bunch:
        finish(0)
    else:
        pl.loop(0, orients // bunch)(lambda i: finish(i * bunch))

    summed = energy[0:rows, :]
    for b in range(1, edge):
        summed = summed + energy[b : b + rows, :]
    upper, lower = halves(summed)
    boxed = product(upper, refs["box"][...]) + product(lower, refs["box"][...])
    scaling_ref[0] = lax.rsqrt(boxed / edge**3 + epsilon)
    scored = by_table(scores[...], refs["score_lines"][...])
    best_ref[0] = jnp.max(scored.reshape(orients, rows, cols), axis=0)
    sent = [
        pencils.at[pl.ds(0, bcols - 1)],
        rotations.at[pl.ds(0, orients - 1), pl.ds(0, share)],
        rotations.at[pl.ds(0, orients), pl.ds(0, orients - share)],
        windows.at[pl.ds(0, orients - 1), pl.ds(margin, rows)],
        windows.at[pl.ds(0, orients), pl.ds(0, margin)],
    ]
    wanted = [bcols > 1, True, parts > 1, True, brows > 1]
    for i, ref in enumerate(sent):
        if wanted[i]:
            pltpu.make_async_copy(ref, ref, send_sems.at[i]).wait()


def dot_short(a, b):
    return jnp.dot(a, b, precision=lax.Precision.HIGH, preferred_element_type=jnp.float32)


names = (
    "template",
    "index",
    "forward",
    "smoothing",
    "inverse",
    "template_lines",
    "template_rows",
    "volume_lines",
    "volume_rows",
    "score_rows",
    "score_lines",
    "box",
)


def staged(sizes, *refs):
    brick, sources = refs[0], refs[1 : len(names) + 1]
    results = refs[len(names) + 1 : len(names) + 3]
    held = refs[len(names) + 3 : 2 * len(names) + 3]
    rest = refs[2 * len(names) + 3 : -1]
    copies = {
        name: pltpu.make_async_copy(source, target, refs[-1].at[i])
        for i, (name, source, target) in enumerate(zip(names, sources, held))
    }
    named = dict(zip(names, held), brick=brick)
    match_kernel(sizes, named, copies, *rest, *results)


def shards(volume, template, voxel_maps):
    orients, brows, bcols = (lax.axis_size(axis) for axis in ("orient", "brow", "bcol"))
    planes, rows, cols = volume.shape
    edge = template.shape[0]
    half_edge = edge // 2
    length = cols * bcols
    size = cols + edge
    tile_rows = rows + edge
    margin = round_up(half_edge, 8)
    strips = 8
    batch = math.gcd(orients, 4)
    parts = brows if orients % (2 * brows) == 0 else 1
    base = half_edge - orients
    assert brows <= 2 and margin <= rows and tile_rows <= rows + 2 * margin
    assert base % 2 == 0 and orients % 2 == 0
    assert edge % strips == 0 and edge // strips * edge <= LANES
    width = edge // strips * edge * (strips - 1) + LANES
    width = round_up(width, LANES)
    vmem = pl.BlockSpec(memory_space=pltpu.VMEM)
    constants = (
        forward_table(length, bcols),
        smoothing_table(length),
        windowed_inverse(length, bcols, half_edge),
        template_lines(edge, size, strips),
        template_rows(tile_rows, edge, strips),
        right_table(line_table(size, size)),
        volume_rows(tile_rows),
        score_rows(tile_rows, rows),
        score_lines(size, cols),
        box_table(size, cols, edge),
    )
    sizes = (orients, brows, bcols, parts, edge, base, margin, batch, strips)
    operands = (volume, template.reshape(edge * edge, edge), voxel_maps)
    operands += tuple(jnp.asarray(c) for c in constants)
    best, scaling = pl.pallas_call(
        lambda *refs: staged(sizes, *refs),
        out_shape=(pltpu.VMEM((1, rows, cols), jnp.float32),) * 2,
        in_specs=[pl.BlockSpec(memory_space=pl.ANY)] * len(operands),
        out_specs=(vmem, vmem),
        scratch_shapes=[pltpu.VMEM(x.shape, x.dtype) for x in operands[1:]]
        + [
            pltpu.VMEM((2 * orients // parts, 1, width), jnp.float32),
            pltpu.VMEM((orients, orients, 1, width), jnp.float32),
            pltpu.VMEM((2 * edge // strips, strips * batch * orients, size), jnp.float32),
            pltpu.VMEM((orients, orients, tile_rows, size), jnp.float32),
            pltpu.VMEM((orients, 2 * tile_rows, size), jnp.float32),
            pltpu.VMEM((bcols, rows, cols), jnp.float32),
            pltpu.VMEM((orients, rows + 2 * margin, size), jnp.float32),
            pltpu.VMEM((tile_rows, size), jnp.float32),
            pltpu.VMEM((orients * rows, 2 * size), jnp.float32),
            pltpu.VMEM((edge * edge, edge), jnp.float32),
            pltpu.VMEM((2 * round_up(edge * edge // 8, 16), 8 * edge), jnp.bfloat16),
            pltpu.VMEM((8, LANES), jnp.float32),
            pltpu.SemaphoreType.DMA,
            pltpu.SemaphoreType.DMA((bcols,)),
            pltpu.SemaphoreType.DMA((orients,)),
            pltpu.SemaphoreType.DMA((orients,)),
            pltpu.SemaphoreType.DMA((orients,)),
            pltpu.SemaphoreType.DMA((orients,)),
            pltpu.SemaphoreType.DMA((5,)),
            pltpu.SemaphoreType.REGULAR((5,)),
            pltpu.SemaphoreType.DMA((len(names),)),
        ],
        compiler_params=pltpu.CompilerParams(collective_id=0, has_side_effects=True),
        name="match",
    )(*operands)
    return best * scaling


def solution(mesh):
    in_specs = (P("orient", "brow", "bcol"), P(), P("orient", None))
    out_specs = P("orient", "brow", "bcol")
    return jax.shard_map(shards, mesh=mesh, in_specs=in_specs, out_specs=out_specs, check_vma=False)
```

```python
import math

import numpy as np
import jax
import jax.numpy as jnp
from jax import lax
from jax.experimental import pallas as pl
from jax.experimental.pallas import tpu as pltpu
from jax.sharding import PartitionSpec as P

epsilon = 1e-06
floor_share = 0.1
LANES = 128
MESH = pl.DeviceIdType.MESH


def round_up(value, step):
    return -(-value // step) * step


def split(table):
    upper = table.astype(jnp.bfloat16)
    lower = (table - upper.astype(np.float64)).astype(jnp.bfloat16)
    return upper, lower


def forward_table(length, parts):
    half = length // 2 + 1
    padded = round_up(half, LANES)
    angles = 2.0 * np.pi * (np.outer(np.arange(length), np.arange(half)) % length) / length
    table = np.zeros((length, 2 * padded))
    table[:, :half] = np.cos(angles)
    table[:, padded : padded + half] = -np.sin(angles)
    return np.stack(split(table.reshape(parts, length // parts, 2 * padded)))


def smoothing_table(length):
    half = length // 2 + 1
    padded = round_up(half, LANES)
    table = np.zeros((padded, padded))
    fold = np.minimum(np.arange(length), length - np.arange(length))
    for k in range(half):
        for shift in (-1, 0, 1):
            table[fold[(k + shift) % length], k] += 1.0 / 3.0
        for other in range(length):
            table[fold[other], k] += floor_share / length
    return np.stack(split(table))


def windowed_inverse(length, parts, margin):
    half = length // 2 + 1
    padded = round_up(half, LANES)
    width = length // parts
    tables = np.zeros((parts, 2 * padded, width + 2 * margin))
    k = np.arange(half)
    share = np.where((k == 0) | (2 * k == length), 1.0, 2.0)[:, None] / math.sqrt(length)
    for part in range(parts):
        columns = np.arange(width + 2 * margin) + part * width - margin
        inside = (columns >= 0) & (columns < length)
        angles = 2.0 * np.pi * (np.outer(k, columns) % length) / length
        tables[part, :half] = share * np.cos(angles) * inside
        tables[part, padded : padded + half] = -share * np.sin(angles) * inside
    return np.stack(split(tables))


def left_table(table):
    upper, lower = split(table)
    return np.concatenate([upper, lower, upper], axis=1)


def right_table(table):
    upper, lower = split(table)
    return np.concatenate([upper, upper, lower], axis=0)


def odd_waves(count, size):
    angles = np.pi * (np.outer(np.arange(count), 2 * np.arange(size // 2) + 1) % (2 * size)) / size
    return np.cos(angles), np.sin(angles)


def line_table(count, size):
    cos, sin = odd_waves(count, size)
    return np.concatenate([cos, -sin, -sin, -cos], axis=1)


def row_waves(size, count):
    angles = 2.0 * np.pi * (np.outer(np.arange(size), np.arange(count)) % size) / size
    return np.cos(angles), np.sin(angles)


def template_lines(edge, size, strips):
    span = edge // strips
    waves = line_table(edge, size)
    table = np.zeros((LANES, 2, span, size))
    for b in range(span):
        for half in range(2):
            table[b * edge : (b + 1) * edge, half, b] = waves[:, half * size : (half + 1) * size]
    return right_table(table.reshape(LANES, -1))


def template_rows(size, edge, strips):
    order = np.arange(edge).reshape(strips, edge // strips).T.reshape(-1)
    return left_table(np.concatenate([wave[:, order] for wave in row_waves(size, edge)], axis=1))


def volume_rows(size):
    cos, sin = row_waves(size, size)
    return left_table(np.block([[cos, sin], [-sin, cos]]))


def score_rows(size, rows):
    cos, sin = (wave.T / size for wave in row_waves(size, rows))
    return left_table(np.block([[cos, -sin], [sin, cos]]))


def score_lines(size, count):
    cos, sin = (wave.T * (2.0 / size) for wave in odd_waves(count, size))
    return right_table(np.concatenate([cos, cos, -sin, -sin], axis=0))


def box_table(size, count, edge):
    offsets = np.arange(size)[:, None] - np.arange(count)[None, :]
    return ((offsets >= 0) & (offsets < edge)).astype(jnp.bfloat16)


def split_table(template_ref, shifted):
    lines, edge = template_ref.shape
    template = template_ref[...] - 0.5
    shifted[...] = template
    mean = jnp.sum(template, keepdims=True) / (lines * edge)
    centred = template - mean
    scale = lax.rsqrt(jnp.sum(centred * centred, keepdims=True) + epsilon)
    table = jnp.concatenate([shifted[pl.ds(j, lines // 8, stride=8), :] for j in range(8)], axis=1)
    spare = round_up(lines // 8, 16) - lines // 8
    table = jnp.concatenate([table, jnp.zeros((spare, 8 * edge), jnp.float32)], axis=0)
    return jnp.concatenate(halves(table), axis=0), mean, scale


def look_up(pieces, index):
    count, span = pieces.shape
    width = index.shape[1]
    high = ((index.astype(jnp.float32) + 0.5) * (1.0 / span)).astype(jnp.int32)
    low = (index - high * span).astype(jnp.float32).astype(jnp.bfloat16)
    row = lax.broadcasted_iota(jnp.int32, (span, width), 0).astype(jnp.float32).astype(jnp.bfloat16)
    one = jnp.ones((), jnp.bfloat16)
    lanes = product(pieces, jnp.where(row == low, one, jnp.zeros_like(one)))
    lanes = lanes[: count // 2] + lanes[count // 2 :]
    mine = lax.broadcasted_iota(jnp.int32, lanes.shape, 0) == high
    return jnp.sum(jnp.where(mine, lanes, 0.0), axis=0, keepdims=True)


def halves(x):
    upper = x.astype(jnp.bfloat16)
    return upper, (x - upper.astype(jnp.float32)).astype(jnp.bfloat16)


def product(a, b):
    return jnp.dot(a, b, preferred_element_type=jnp.float32)


def by_table(x, table):
    upper, lower = halves(x)
    return product(jnp.concatenate([upper, lower, upper], axis=1), table)


def by_halves(x, upper, lower):
    high, low = halves(x)
    return product(high, upper) + (product(low, upper) + product(high, lower))


def table_by(table, x):
    upper, lower = halves(x)
    return product(table, jnp.concatenate([upper, upper, lower], axis=0))


def match_kernel(
    sizes,
    refs,
    copies,
    rotated,
    rotations,
    lines,
    templates,
    volumes,
    pencils,
    windows,
    energy,
    totals,
    normed,
    table,
    stats,
    own_sem,
    gather_sems,
    share_sems,
    turn_sems,
    window_sems,
    margin_sems,
    send_sems,
    tokens,
    best_ref,
    scaling_ref,
):
    orients, brows, bcols, parts, edge, base, margin, batch, strips = sizes
    half_edge = edge // 2
    rows, cols = refs["brick"].shape[1:]
    tile_rows, size = energy.shape
    skip = margin - half_edge
    me = lax.axis_index("orient")
    row_id = lax.axis_index("brow")
    col_id = lax.axis_index("bcol")
    share = orients // parts
    mine = lax.rem(row_id, parts)
    plane_voxels = edge * edge
    span = edge // strips

    def column_peer(column):
        return {"orient": me, "brow": row_id, "bcol": column}

    def partner(step):
        assert orients & (orients - 1) == 0
        other, weight = 0, 1
        while weight < orients:
            other = other + lax.rem(me // weight + step // weight, 2) * weight
            weight *= 2
        return other

    partners = [partner(step) for step in range(orients)]
    pair, last = me // 2, orients // 2 - 1
    odd = lax.rem(me, 2)
    by_column, by_row, by_pair, by_near, by_far = (tokens.at[i] for i in range(5))

    def plane_peer(plane):
        return {"orient": plane, "brow": row_id, "bcol": col_id}

    def row_peer(row):
        return {"orient": me, "brow": row, "bcol": col_id}

    def expect(semaphore, count):
        pl.when(count > 0)(lambda: pl.semaphore_wait(semaphore, count))

    def each(count, own, step, do):
        for other in range(count):

            @pl.when(step * other > step * own)
            def _():
                do(other)

    def greet(semaphore, peer):
        pl.semaphore_signal(semaphore, inc=1, device_id=peer, device_id_type=MESH)

    def first_of(part, plane):
        start = orients - plane
        rest = lax.rem(start, 2 * parts) + 2 * parts - 2 * part
        return start // (2 * parts) * 2 + (rest - 1) // (2 * parts) + (rest - 2) // (2 * parts)

    def plane_of(slot):
        part, index = slot // share, slot % share
        found = first_of(part, me) + index
        return found // 2 * (2 * parts) + 2 * part + lax.rem(found, 2) - orients + me

    windows[...] = jnp.zeros_like(windows)
    barrier = pltpu.get_barrier_semaphore()
    @pl.when(odd == 0)
    def _():
        each(orients, me, 1, lambda plane: greet(barrier, plane_peer(plane)))

    @pl.when(odd == 1)
    def _():
        each(orients // 2, pair, 1, lambda other: greet(barrier, plane_peer(2 * other + 1)))

    each(bcols, col_id, 1, lambda column: greet(barrier, column_peer(column)))
    each(brows, row_id, 1, lambda row: greet(barrier, row_peer(row)))
    tables = ("template_lines", "template_rows", "volume_lines", "volume_rows", "score_rows", "score_lines", "box")
    for name, copy in copies.items():
        if name not in tables:
            copy.start()
    own = pltpu.make_async_copy(refs["brick"].at[0], pencils.at[col_id], own_sem)
    own.start()
    energy[...] = jnp.zeros_like(energy)
    rotated[...] = jnp.zeros_like(rotated)
    planes_of = [plane_of(slot) for slot in range(orients)]

    def tabulate():
        copies["template"].wait()
        table[...], stats[0:1, 0:1], stats[1:2, 0:1] = split_table(refs["template"], normed)
        copies["index"].wait()

    def find(first, end):
        def one(index):
            plane = base + 2 * mine + 2 * parts * index

            def fill():
                start = pl.multiple_of(plane * plane_voxels, 2 * plane_voxels)
                found = look_up(table[...], refs["index"][0:1, pl.ds(start, 2 * plane_voxels)])
                found = (found - stats[0:1, 0:1]) * stats[1:2, 0:1]
                for i in range(2):
                    rotated[2 * index + i, :, :plane_voxels] = found[:, i * plane_voxels : (i + 1) * plane_voxels]

            if base < 0 or base + 2 * orients > edge:
                pl.when(jnp.logical_and(plane >= 0, plane < edge))(fill)
            else:
                fill()

        if share <= 4:
            for index in range(first, end):
                one(index)
        else:
            pl.loop(first, end)(one)

    expect(barrier, pair + odd * (pair + 1) + col_id + row_id)

    def gather_of(column, brick):
        return pltpu.make_async_remote_copy(
            src_ref=brick,
            dst_ref=pencils.at[col_id],
            send_sem=send_sems.at[0],
            recv_sem=gather_sems.at[col_id],
            device_id=column_peer(column),
            device_id_type=MESH,
        )

    each(bcols, col_id, -1, lambda column: gather_of(column, refs["brick"].at[0]).start())
    each(bcols, col_id, -1, lambda column: greet(by_column, column_peer(column)))
    each(brows, row_id, -1, lambda row: greet(by_row, row_peer(row)))

    @pl.when(odd == 1)
    def _():
        def answer(other):
            for i in range(2):
                greet(by_far, plane_peer(2 * other + i))

        greet(by_pair, plane_peer(me - 1))
        each(orients // 2, pair - 1, -1, answer)

        @pl.when(pair > 0)
        def _():
            for i in range(2):
                greet(by_near, plane_peer(2 * pair - 2 + i))

    for name in tables:
        copies[name].start()
    tabulate()
    find(0, share // 2)
    expect(by_column, bcols - 1 - col_id)
    own.wait()
    each(bcols, col_id, 1, lambda column: gather_of(column, pencils.at[col_id]).start())
    find(share // 2, share)
    expect(by_row, brows - 1 - row_id)

    def block(rotation, part):
        return rotations.at[rotation, pl.ds(part * share, share)]

    def share_of(plane):
        return pltpu.make_async_remote_copy(
            src_ref=rotated.at[pl.ds(first_of(mine, plane), share)],
            dst_ref=block(me, mine),
            send_sem=send_sems.at[1],
            recv_sem=share_sems.at[me],
            device_id=plane_peer(plane),
            device_id_type=MESH,
        )

    def turn_of(rotation, turn):
        row = lax.rem(row_id + turn, brows)
        return pltpu.make_async_remote_copy(
            src_ref=block(rotation, mine),
            dst_ref=block(rotation, mine),
            send_sem=send_sems.at[2],
            recv_sem=turn_sems.at[rotation],
            device_id=row_peer(row),
            device_id_type=MESH,
        )

    rotations[me, pl.ds(mine * share, share)] = rotated[pl.ds(first_of(mine, me), share)]
    for turn in range(1, parts):
        turn_of(me, turn).start()
    expect(by_pair, 1 - odd)
    each(orients, me, -1, lambda plane: share_of(plane).start())
    pl.when(odd == 0)(lambda: share_of(me + 1).start())
    near = (2 * last - pair) // (last + 1)
    far = last - pair - near

    def send(kind, planes):
        def one(plane):
            if planes == "near":
                pl.when(plane < 2 * pair + 4)(lambda: kind(plane).start())
            else:
                pl.when(plane >= 2 * pair + 4)(lambda: kind(plane).start())

        each(orients, 2 * pair + 1, 1, one)

    expect(by_near, near)
    send(share_of, "near")

    def forward(steps):
        for step in steps:
            if step:
                arrived = block(partners[step], mine)
                pltpu.make_async_copy(arrived, arrived, share_sems.at[partners[step]]).wait()
                for turn in range(1, parts):
                    turn_of(partners[step], turn).start()

    groups = [list(range(first, first + batch)) for first in range(0, orients, batch)]
    for name in ("forward", "smoothing", "inverse"):
        copies[name].wait()

    def wave(column):
        return by_halves(pencils[column], refs["forward"][0, column], refs["forward"][1, column])

    both = wave(col_id)
    for step in range(1, bcols):
        column = lax.rem(col_id + step, bcols)
        arrived = pencils.at[column]
        pltpu.make_async_copy(arrived, arrived, gather_sems.at[column]).wait()
    for step in range(1, bcols):
        both = both + wave(lax.rem(col_id + step, bcols))
    padded = both.shape[1] // 2
    real, imag = both[:, :padded], both[:, padded:]
    power = real * real + imag * imag
    weights = lax.rsqrt(by_halves(power, refs["smoothing"][0], refs["smoothing"][1]) + epsilon)
    white = both * jnp.concatenate([weights, weights], axis=1)
    windows[me, margin : margin + rows] = by_halves(
        white, refs["inverse"][0, col_id], refs["inverse"][1, col_id]
    )

    def window_of(plane):
        part = windows.at[me, pl.ds(margin, rows)]
        return pltpu.make_async_remote_copy(
            src_ref=part,
            dst_ref=part,
            send_sem=send_sems.at[3],
            recv_sem=window_sems.at[me],
            device_id=plane_peer(plane),
            device_id_type=MESH,
        )

    def margin_of(plane):
        return pltpu.make_async_remote_copy(
            src_ref=windows.at[plane, pl.ds(pl.multiple_of(rows - row_id * (rows - margin), 8), margin)],
            dst_ref=windows.at[plane, pl.ds(pl.multiple_of(row_id * (margin + rows), 8), margin)],
            send_sem=send_sems.at[4],
            recv_sem=margin_sems.at[plane],
            device_id=row_peer(lax.rem(row_id + 1, brows)),
            device_id_type=MESH,
        )

    each(orients, me, -1, lambda plane: window_of(plane).start())
    pl.when(odd == 0)(lambda: window_of(me + 1).start())
    send(window_of, "near")
    if brows > 1:
        margin_of(me).start()
    for name in tables:
        copies[name].wait()

    def normalise():
        summed = energy[0:rows, :]
        for b in range(1, edge):
            summed = summed + energy[b : b + rows, :]
        upper, lower = halves(summed)
        boxed = product(upper, refs["box"][...]) + product(lower, refs["box"][...])
        scaling_ref[0] = lax.rsqrt(boxed / edge**3 + epsilon)

    def transform(steps):
        tiles = []
        for step in steps:
            plane = partners[step]
            if brows > 1:
                arrived = windows.at[plane, pl.ds(0, margin)]
                pltpu.make_async_copy(arrived, arrived, margin_sems.at[plane]).wait()
            tile = windows[plane, skip : skip + tile_rows]
            gap = plane - me
            near = jnp.logical_and(gap >= -half_edge, gap < half_edge).astype(jnp.float32)
            energy[...] += tile * tile * near
            tiles.append(tile)
        turned = by_table(jnp.concatenate(tiles, axis=0), refs["volume_lines"][...])
        if steps is groups[-1]:
            normalise()
        for first in range(0, len(steps), 2):
            pair = []
            for i in range(first, first + 2):
                part = turned[i * tile_rows : (i + 1) * tile_rows]
                pair.append(jnp.concatenate([part[:, :size], part[:, size:]], axis=0))
            spun = table_by(refs["volume_rows"][...], jnp.concatenate(pair, axis=1))
            for i in range(2):
                volumes[partners[steps[first + i]]] = spun[:, i * size : (i + 1) * size]

    def unfold(steps):
        for step in steps:
            if parts > 1:
                arrived = rotations.at[partners[step], pl.ds(0, orients - share)]
                pltpu.make_async_copy(arrived, arrived, turn_sems.at[partners[step]]).wait()
        width = span * edge
        pieces = []
        for step in steps:
            planes = rotations[partners[step]][:, 0, :]
            pieces += [planes[:, j * width : j * width + LANES] for j in range(strips)]
        turned = by_table(jnp.concatenate(pieces, axis=0), refs["template_lines"][...])
        for k in range(2 * span):
            lines[k, : turned.shape[0]] = turned[:, k * size : (k + 1) * size]
        for i, step in enumerate(steps):
            for first in range(0, orients, 2):
                pair = [
                    jnp.concatenate(
                        [lines[k, pl.ds(i * strips * orients + slot, strips, stride=orients), :] for k in range(2 * span)],
                        axis=0,
                    )
                    for slot in (first, first + 1)
                ]
                spun = table_by(refs["template_rows"][...], jnp.concatenate(pair, axis=1))
                for j in range(2):
                    templates[partners[step], planes_of[first + j]] = spun[:, j * size : (j + 1) * size]

    def spread(steps):
        for step in steps:
            if step:
                arrived = windows.at[partners[step], pl.ds(margin, rows)]
                pltpu.make_async_copy(arrived, arrived, window_sems.at[partners[step]]).wait()
                if brows > 1:
                    margin_of(partners[step]).start()

    forward(groups[0])
    expect(by_far, far)
    send(share_of, "far")
    send(window_of, "far")
    bunch = math.gcd(orients, 8)

    def rounds(do):
        if orients == bunch:
            do(0)
        else:
            pl.loop(0, orients // bunch)(lambda i: do(i * bunch))

    def combine(steps, lowest, more):
        for first in range(0, bunch, 2):
            for half in range(tile_rows // 8):
                top = pl.ds(half * 8, 8)
                low = pl.ds(tile_rows + half * 8, 8)
                for rotation in (lowest + first, lowest + first + 1):
                    straight = totals[rotation, top, :] if more else None
                    crossed = totals[rotation, low, :] if more else None
                    for step in steps:
                        plane = partners[step]
                        wave = templates[rotation, plane, top, :]
                        term = volumes[plane, top, :] * wave
                        turn = volumes[plane, low, :] * wave
                        straight = term if straight is None else straight + term
                        crossed = turn if crossed is None else crossed + turn
                    totals[rotation, top, :] = straight
                    totals[rotation, low, :] = crossed

    def finish(lowest, best):
        turned = []
        for first in range(0, bunch, 2):
            pair = jnp.concatenate([totals[lowest + first], totals[lowest + first + 1]], axis=1)
            turned.append(table_by(refs["score_rows"][...], pair))
        for part in turned:
            halved = [part[:, i * size : (i + 1) * size] for i in range(2)]
            waves = [jnp.concatenate([half[:rows], half[rows:]], axis=1) for half in halved]
            scored = by_table(jnp.concatenate(waves, axis=0), refs["score_lines"][...])
            found = jnp.maximum(scored[:rows], scored[rows:])
            best = found if best is None else jnp.maximum(best, found)
        return best

    unfold(groups[0])
    spread(groups[0])
    for steps in groups[1:]:
        forward(steps)
    transform(groups[0])
    for steps in groups[1:]:
        unfold(steps[: batch // 2])
        spread(steps)
        unfold(steps[batch // 2 :])
    for i, steps in enumerate(groups):
        if i:
            transform(steps)
        rounds(lambda lowest: combine(steps, lowest, i > 0))
    best = finish(0, None)
    if orients > bunch:
        best = lax.fori_loop(1, orients // bunch, lambda i, best: finish(i * bunch, best), best)
    best_ref[0] = best
    sent = [
        pencils.at[pl.ds(0, bcols - 1)],
        rotations.at[pl.ds(0, orients - 1), pl.ds(0, share)],
        rotations.at[pl.ds(0, orients), pl.ds(0, orients - share)],
        windows.at[pl.ds(0, orients - 1), pl.ds(margin, rows)],
        windows.at[pl.ds(0, orients), pl.ds(0, margin)],
    ]
    wanted = [bcols > 1, True, parts > 1, True, brows > 1]
    for i, ref in enumerate(sent):
        if wanted[i]:
            pltpu.make_async_copy(ref, ref, send_sems.at[i]).wait()


names = (
    "template",
    "index",
    "forward",
    "smoothing",
    "inverse",
    "template_lines",
    "template_rows",
    "volume_lines",
    "volume_rows",
    "score_rows",
    "score_lines",
    "box",
)


def staged(sizes, *refs):
    brick, sources = refs[0], refs[1 : len(names) + 1]
    results = refs[len(names) + 1 : len(names) + 3]
    held = refs[len(names) + 3 : 2 * len(names) + 3]
    rest = refs[2 * len(names) + 3 : -1]
    copies = {
        name: pltpu.make_async_copy(source, target, refs[-1].at[i])
        for i, (name, source, target) in enumerate(zip(names, sources, held))
    }
    named = dict(zip(names, held), brick=brick)
    match_kernel(sizes, named, copies, *rest, *results)


def shards(volume, template, voxel_maps):
    orients, brows, bcols = (lax.axis_size(axis) for axis in ("orient", "brow", "bcol"))
    planes, rows, cols = volume.shape
    edge = template.shape[0]
    half_edge = edge // 2
    length = cols * bcols
    size = cols + edge
    tile_rows = rows + edge
    margin = round_up(half_edge, 8)
    strips = 8
    batch = math.gcd(orients, 4)
    parts = brows if orients % (2 * brows) == 0 else 1
    base = half_edge - orients
    assert brows <= 2 and margin <= rows and tile_rows <= rows + 2 * margin
    assert base % 2 == 0 and orients % 2 == 0
    assert edge % strips == 0 and edge // strips * edge <= LANES
    width = edge // strips * edge * (strips - 1) + LANES
    width = round_up(width, LANES)
    vmem = pl.BlockSpec(memory_space=pltpu.VMEM)
    constants = (
        forward_table(length, bcols),
        smoothing_table(length),
        windowed_inverse(length, bcols, half_edge),
        template_lines(edge, size, strips),
        template_rows(tile_rows, edge, strips),
        right_table(line_table(size, size)),
        volume_rows(tile_rows),
        score_rows(tile_rows, rows),
        score_lines(size, cols),
        box_table(size, cols, edge),
    )
    sizes = (orients, brows, bcols, parts, edge, base, margin, batch, strips)
    operands = (volume, template.reshape(edge * edge, edge), voxel_maps)
    operands += tuple(jnp.asarray(c) for c in constants)
    best, scaling = pl.pallas_call(
        lambda *refs: staged(sizes, *refs),
        out_shape=(pltpu.VMEM((1, rows, cols), jnp.float32),) * 2,
        in_specs=[pl.BlockSpec(memory_space=pl.ANY)] * len(operands),
        out_specs=(vmem, vmem),
        scratch_shapes=[pltpu.VMEM(x.shape, x.dtype) for x in operands[1:]]
        + [
            pltpu.VMEM((2 * orients // parts, 1, width), jnp.float32),
            pltpu.VMEM((orients, orients, 1, width), jnp.float32),
            pltpu.VMEM((2 * edge // strips, strips * batch * orients, size), jnp.float32),
            pltpu.VMEM((orients, orients, tile_rows, size), jnp.float32),
            pltpu.VMEM((orients, 2 * tile_rows, size), jnp.float32),
            pltpu.VMEM((bcols, rows, cols), jnp.float32),
            pltpu.VMEM((orients, rows + 2 * margin, size), jnp.float32),
            pltpu.VMEM((tile_rows, size), jnp.float32),
            pltpu.VMEM((orients, 2 * tile_rows, size), jnp.float32),
            pltpu.VMEM((edge * edge, edge), jnp.float32),
            pltpu.VMEM((2 * round_up(edge * edge // 8, 16), 8 * edge), jnp.bfloat16),
            pltpu.VMEM((8, LANES), jnp.float32),
            pltpu.SemaphoreType.DMA,
            pltpu.SemaphoreType.DMA((bcols,)),
            pltpu.SemaphoreType.DMA((orients,)),
            pltpu.SemaphoreType.DMA((orients,)),
            pltpu.SemaphoreType.DMA((orients,)),
            pltpu.SemaphoreType.DMA((orients,)),
            pltpu.SemaphoreType.DMA((5,)),
            pltpu.SemaphoreType.REGULAR((5,)),
            pltpu.SemaphoreType.DMA((len(names),)),
        ],
        compiler_params=pltpu.CompilerParams(collective_id=0, has_side_effects=True),
        name="match",
    )(*operands)
    return best * scaling


def solution(mesh):
    in_specs = (P("orient", "brow", "bcol"), P(), P("orient", None))
    out_specs = P("orient", "brow", "bcol")
    return jax.shard_map(shards, mesh=mesh, in_specs=in_specs, out_specs=out_specs, check_vma=False)
```

```python
import math

import numpy as np
import jax
import jax.numpy as jnp
from jax import lax
from jax.experimental import pallas as pl
from jax.experimental.pallas import tpu as pltpu
from jax.sharding import PartitionSpec as P

epsilon = 1e-06
floor_share = 0.1
LANES = 128
MESH = pl.DeviceIdType.MESH


def round_up(value, step):
    return -(-value // step) * step


def split(table):
    upper = table.astype(jnp.bfloat16)
    lower = (table - upper.astype(np.float64)).astype(jnp.bfloat16)
    return upper, lower


def forward_table(length, parts):
    half = length // 2 + 1
    padded = round_up(half, LANES)
    angles = 2.0 * np.pi * (np.outer(np.arange(length), np.arange(half)) % length) / length
    table = np.zeros((length, 2 * padded))
    table[:, :half] = np.cos(angles)
    table[:, padded : padded + half] = -np.sin(angles)
    return np.stack(split(table.reshape(parts, length // parts, 2 * padded)))


def smoothing_table(length):
    half = length // 2 + 1
    padded = round_up(half, LANES)
    table = np.zeros((padded, padded))
    fold = np.minimum(np.arange(length), length - np.arange(length))
    for k in range(half):
        for shift in (-1, 0, 1):
            table[fold[(k + shift) % length], k] += 1.0 / 3.0
        for other in range(length):
            table[fold[other], k] += floor_share / length
    return np.stack(split(table))


def windowed_inverse(length, parts, margin):
    half = length // 2 + 1
    padded = round_up(half, LANES)
    width = length // parts
    tables = np.zeros((parts, 2 * padded, width + 2 * margin))
    k = np.arange(half)
    share = np.where((k == 0) | (2 * k == length), 1.0, 2.0)[:, None] / math.sqrt(length)
    for part in range(parts):
        columns = np.arange(width + 2 * margin) + part * width - margin
        inside = (columns >= 0) & (columns < length)
        angles = 2.0 * np.pi * (np.outer(k, columns) % length) / length
        tables[part, :half] = share * np.cos(angles) * inside
        tables[part, padded : padded + half] = -share * np.sin(angles) * inside
    return np.stack(split(tables))


def left_table(table):
    upper, lower = split(table)
    return np.concatenate([upper, lower, upper], axis=1)


def right_table(table):
    upper, lower = split(table)
    return np.concatenate([upper, upper, lower], axis=0)


def odd_waves(count, size):
    angles = np.pi * (np.outer(np.arange(count), 2 * np.arange(size // 2) + 1) % (2 * size)) / size
    return np.cos(angles), np.sin(angles)


def line_table(count, size):
    cos, sin = odd_waves(count, size)
    return np.concatenate([cos, -sin, -sin, -cos], axis=1)


def row_waves(size, count):
    angles = 2.0 * np.pi * (np.outer(np.arange(size), np.arange(count)) % size) / size
    return np.cos(angles), np.sin(angles)


def template_lines(edge, size, strips):
    span = edge // strips
    waves = line_table(edge, size)
    table = np.zeros((LANES, 2, span, size))
    for b in range(span):
        for half in range(2):
            table[b * edge : (b + 1) * edge, half, b] = waves[:, half * size : (half + 1) * size]
    return right_table(table.reshape(LANES, -1))


def template_rows(size, edge, strips):
    order = np.arange(edge).reshape(strips, edge // strips).T.reshape(-1)
    return left_table(np.concatenate([wave[:, order] for wave in row_waves(size, edge)], axis=1))


def volume_rows(size):
    cos, sin = row_waves(size, size)
    return left_table(np.block([[cos, sin], [-sin, cos]]))


def score_rows(size, rows):
    cos, sin = (wave.T / size for wave in row_waves(size, rows))
    return left_table(np.block([[cos, -sin], [sin, cos]]))


def score_lines(size, count):
    cos, sin = (wave.T * (2.0 / size) for wave in odd_waves(count, size))
    return right_table(np.concatenate([cos, cos, -sin, -sin], axis=0))


def box_table(size, count, edge):
    offsets = np.arange(size)[:, None] - np.arange(count)[None, :]
    return ((offsets >= 0) & (offsets < edge)).astype(jnp.bfloat16)


def split_table(template_ref, shifted):
    lines, edge = template_ref.shape
    template = template_ref[...] - 0.5
    shifted[...] = template
    mean = jnp.sum(template, keepdims=True) / (lines * edge)
    centred = template - mean
    scale = lax.rsqrt(jnp.sum(centred * centred, keepdims=True) + epsilon)
    table = jnp.concatenate([shifted[pl.ds(j, lines // 8, stride=8), :] for j in range(8)], axis=1)
    spare = round_up(lines // 8, 16) - lines // 8
    table = jnp.concatenate([table, jnp.zeros((spare, 8 * edge), jnp.float32)], axis=0)
    return jnp.concatenate(halves(table), axis=0), mean, scale


def look_up(pieces, index):
    count, span = pieces.shape
    width = index.shape[1]
    high = ((index.astype(jnp.float32) + 0.5) * (1.0 / span)).astype(jnp.int32)
    low = (index - high * span).astype(jnp.float32).astype(jnp.bfloat16)
    row = lax.broadcasted_iota(jnp.int32, (span, width), 0).astype(jnp.float32).astype(jnp.bfloat16)
    one = jnp.ones((), jnp.bfloat16)
    lanes = product(pieces, jnp.where(row == low, one, jnp.zeros_like(one)))
    lanes = lanes[: count // 2] + lanes[count // 2 :]
    mine = lax.broadcasted_iota(jnp.int32, lanes.shape, 0) == high
    return jnp.sum(jnp.where(mine, lanes, 0.0), axis=0, keepdims=True)


def halves(x):
    upper = x.astype(jnp.bfloat16)
    return upper, (x - upper.astype(jnp.float32)).astype(jnp.bfloat16)


def product(a, b):
    return jnp.dot(a, b, preferred_element_type=jnp.float32)


def by_table(x, table):
    upper, lower = halves(x)
    return product(jnp.concatenate([upper, lower, upper], axis=1), table)


def by_halves(x, upper, lower):
    high, low = halves(x)
    return product(high, upper) + (product(low, upper) + product(high, lower))


def table_by(table, x):
    upper, lower = halves(x)
    return product(table, jnp.concatenate([upper, upper, lower], axis=0))


def match_kernel(
    sizes,
    refs,
    copies,
    rotated,
    rotations,
    lines,
    templates,
    volumes,
    pencils,
    windows,
    energy,
    totals,
    normed,
    table,
    stats,
    own_sem,
    gather_sems,
    share_sems,
    turn_sems,
    window_sems,
    margin_sems,
    send_sems,
    tokens,
    best_ref,
    scaling_ref,
):
    orients, brows, bcols, parts, edge, base, margin, batch, strips = sizes
    half_edge = edge // 2
    rows, cols = refs["brick"].shape[1:]
    tile_rows, size = energy.shape
    skip = margin - half_edge
    me = lax.axis_index("orient")
    row_id = lax.axis_index("brow")
    col_id = lax.axis_index("bcol")
    share = orients // parts
    mine = lax.rem(row_id, parts)
    plane_voxels = edge * edge
    span = edge // strips

    def column_peer(column):
        return {"orient": me, "brow": row_id, "bcol": column}

    def partner(step):
        assert orients & (orients - 1) == 0
        other, weight = 0, 1
        while weight < orients:
            other = other + lax.rem(me // weight + step // weight, 2) * weight
            weight *= 2
        return other

    partners = [partner(step) for step in range(orients)]
    pair, last = me // 2, orients // 2 - 1
    odd = lax.rem(me, 2)
    by_column, by_row, by_pair, by_near, by_far = (tokens.at[i] for i in range(5))

    def plane_peer(plane):
        return {"orient": plane, "brow": row_id, "bcol": col_id}

    def row_peer(row):
        return {"orient": me, "brow": row, "bcol": col_id}

    def expect(semaphore, count):
        pl.when(count > 0)(lambda: pl.semaphore_wait(semaphore, count))

    def each(count, own, step, do):
        for other in range(count):

            @pl.when(step * other > step * own)
            def _():
                do(other)

    def greet(semaphore, peer):
        pl.semaphore_signal(semaphore, inc=1, device_id=peer, device_id_type=MESH)

    def first_of(part, plane):
        start = orients - plane
        rest = lax.rem(start, 2 * parts) + 2 * parts - 2 * part
        return start // (2 * parts) * 2 + (rest - 1) // (2 * parts) + (rest - 2) // (2 * parts)

    def plane_of(slot):
        part, index = slot // share, slot % share
        found = first_of(part, me) + index
        return found // 2 * (2 * parts) + 2 * part + lax.rem(found, 2) - orients + me

    windows[...] = jnp.zeros_like(windows)
    barrier = pltpu.get_barrier_semaphore()
    @pl.when(odd == 0)
    def _():
        each(orients, me, 1, lambda plane: greet(barrier, plane_peer(plane)))

    @pl.when(odd == 1)
    def _():
        each(orients // 2, pair, 1, lambda other: greet(barrier, plane_peer(2 * other + 1)))

    each(bcols, col_id, 1, lambda column: greet(barrier, column_peer(column)))
    each(brows, row_id, 1, lambda row: greet(barrier, row_peer(row)))
    tables = ("template_lines", "template_rows", "volume_lines", "volume_rows", "score_rows", "score_lines", "box")
    for name, copy in copies.items():
        if name not in tables:
            copy.start()
    own = pltpu.make_async_copy(refs["brick"].at[0], pencils.at[col_id], own_sem)
    own.start()
    energy[...] = jnp.zeros_like(energy)
    rotated[...] = jnp.zeros_like(rotated)
    planes_of = [plane_of(slot) for slot in range(orients)]

    def tabulate():
        copies["template"].wait()
        table[...], stats[0:1, 0:1], stats[1:2, 0:1] = split_table(refs["template"], normed)
        copies["index"].wait()

    def find(first, end):
        def one(index):
            plane = base + 2 * mine + 2 * parts * index

            def fill():
                start = pl.multiple_of(plane * plane_voxels, 2 * plane_voxels)
                found = look_up(table[...], refs["index"][0:1, pl.ds(start, 2 * plane_voxels)])
                found = (found - stats[0:1, 0:1]) * stats[1:2, 0:1]
                for i in range(2):
                    rotated[2 * index + i, :, :plane_voxels] = found[:, i * plane_voxels : (i + 1) * plane_voxels]

            if base < 0 or base + 2 * orients > edge:
                pl.when(jnp.logical_and(plane >= 0, plane < edge))(fill)
            else:
                fill()

        if share <= 4:
            for index in range(first, end):
                one(index)
        else:
            pl.loop(first, end)(one)

    expect(barrier, pair + odd * (pair + 1) + col_id + row_id)

    def gather_of(column, brick):
        return pltpu.make_async_remote_copy(
            src_ref=brick,
            dst_ref=pencils.at[col_id],
            send_sem=send_sems.at[0],
            recv_sem=gather_sems.at[col_id],
            device_id=column_peer(column),
            device_id_type=MESH,
        )

    each(bcols, col_id, -1, lambda column: gather_of(column, refs["brick"].at[0]).start())
    each(bcols, col_id, -1, lambda column: greet(by_column, column_peer(column)))
    each(brows, row_id, -1, lambda row: greet(by_row, row_peer(row)))

    @pl.when(odd == 1)
    def _():
        def answer(other):
            for i in range(2):
                greet(by_far, plane_peer(2 * other + i))

        greet(by_pair, plane_peer(me - 1))
        each(orients // 2, pair - 1, -1, answer)

        @pl.when(pair > 0)
        def _():
            for i in range(2):
                greet(by_near, plane_peer(2 * pair - 2 + i))

    for name in tables:
        copies[name].start()
    tabulate()
    find(0, share // 2)
    expect(by_column, bcols - 1 - col_id)
    own.wait()
    each(bcols, col_id, 1, lambda column: gather_of(column, pencils.at[col_id]).start())
    find(share // 2, share)
    expect(by_row, brows - 1 - row_id)

    def block(rotation, part):
        return rotations.at[rotation, pl.ds(part * share, share)]

    def share_of(plane):
        return pltpu.make_async_remote_copy(
            src_ref=rotated.at[pl.ds(first_of(mine, plane), share)],
            dst_ref=block(me, mine),
            send_sem=send_sems.at[1],
            recv_sem=share_sems.at[me],
            device_id=plane_peer(plane),
            device_id_type=MESH,
        )

    def turn_of(rotation, turn):
        row = lax.rem(row_id + turn, brows)
        return pltpu.make_async_remote_copy(
            src_ref=block(rotation, mine),
            dst_ref=block(rotation, mine),
            send_sem=send_sems.at[2],
            recv_sem=turn_sems.at[rotation],
            device_id=row_peer(row),
            device_id_type=MESH,
        )

    rotations[me, pl.ds(mine * share, share)] = rotated[pl.ds(first_of(mine, me), share)]
    for turn in range(1, parts):
        turn_of(me, turn).start()
    expect(by_pair, 1 - odd)
    each(orients, me, -1, lambda plane: share_of(plane).start())
    pl.when(odd == 0)(lambda: share_of(me + 1).start())
    near = (2 * last - pair) // (last + 1)
    far = last - pair - near

    def send(kind, planes):
        def one(plane):
            if planes == "near":
                pl.when(plane < 2 * pair + 4)(lambda: kind(plane).start())
            else:
                pl.when(plane >= 2 * pair + 4)(lambda: kind(plane).start())

        each(orients, 2 * pair + 1, 1, one)

    expect(by_near, near)
    send(share_of, "near")

    def forward(steps):
        for step in steps:
            if step:
                arrived = block(partners[step], mine)
                pltpu.make_async_copy(arrived, arrived, share_sems.at[partners[step]]).wait()
                for turn in range(1, parts):
                    turn_of(partners[step], turn).start()

    groups = [list(range(first, first + batch)) for first in range(0, orients, batch)]
    for name in ("forward", "smoothing", "inverse"):
        copies[name].wait()

    def wave(column):
        return by_halves(pencils[column], refs["forward"][0, column], refs["forward"][1, column])

    both = wave(col_id)
    for step in range(1, bcols):
        column = lax.rem(col_id + step, bcols)
        arrived = pencils.at[column]
        pltpu.make_async_copy(arrived, arrived, gather_sems.at[column]).wait()
    for step in range(1, bcols):
        both = both + wave(lax.rem(col_id + step, bcols))
    padded = both.shape[1] // 2
    real, imag = both[:, :padded], both[:, padded:]
    power = real * real + imag * imag
    weights = lax.rsqrt(by_halves(power, refs["smoothing"][0], refs["smoothing"][1]) + epsilon)
    white = both * jnp.concatenate([weights, weights], axis=1)
    windows[me, margin : margin + rows] = by_halves(
        white, refs["inverse"][0, col_id], refs["inverse"][1, col_id]
    )

    def window_of(plane):
        part = windows.at[me, pl.ds(margin, rows)]
        return pltpu.make_async_remote_copy(
            src_ref=part,
            dst_ref=part,
            send_sem=send_sems.at[3],
            recv_sem=window_sems.at[me],
            device_id=plane_peer(plane),
            device_id_type=MESH,
        )

    def margin_of(plane):
        return pltpu.make_async_remote_copy(
            src_ref=windows.at[plane, pl.ds(pl.multiple_of(rows - row_id * (rows - margin), 8), margin)],
            dst_ref=windows.at[plane, pl.ds(pl.multiple_of(row_id * (margin + rows), 8), margin)],
            send_sem=send_sems.at[4],
            recv_sem=margin_sems.at[plane],
            device_id=row_peer(lax.rem(row_id + 1, brows)),
            device_id_type=MESH,
        )

    each(orients, me, -1, lambda plane: window_of(plane).start())
    pl.when(odd == 0)(lambda: window_of(me + 1).start())
    send(window_of, "near")
    if brows > 1:
        margin_of(me).start()
    for name in tables:
        copies[name].wait()

    def normalise():
        summed = energy[0:rows, :]
        for b in range(1, edge):
            summed = summed + energy[b : b + rows, :]
        upper, lower = halves(summed)
        boxed = product(upper, refs["box"][...]) + product(lower, refs["box"][...])
        scaling_ref[0] = lax.rsqrt(boxed / edge**3 + epsilon)

    def transform(steps):
        tiles = []
        for step in steps:
            plane = partners[step]
            if brows > 1:
                arrived = windows.at[plane, pl.ds(0, margin)]
                pltpu.make_async_copy(arrived, arrived, margin_sems.at[plane]).wait()
            tile = windows[plane, skip : skip + tile_rows]
            gap = plane - me
            near = jnp.logical_and(gap >= -half_edge, gap < half_edge).astype(jnp.float32)
            energy[...] += tile * tile * near
            tiles.append(tile)
        turned = by_table(jnp.concatenate(tiles, axis=0), refs["volume_lines"][...])
        if steps is groups[-1]:
            normalise()
        for first in range(0, len(steps), 2):
            pair = []
            for i in range(first, first + 2):
                part = turned[i * tile_rows : (i + 1) * tile_rows]
                pair.append(jnp.concatenate([part[:, :size], part[:, size:]], axis=0))
            spun = table_by(refs["volume_rows"][...], jnp.concatenate(pair, axis=1))
            for i in range(2):
                volumes[partners[steps[first + i]]] = spun[:, i * size : (i + 1) * size]

    def unfold(steps):
        for step in steps:
            if parts > 1:
                arrived = rotations.at[partners[step], pl.ds(0, orients - share)]
                pltpu.make_async_copy(arrived, arrived, turn_sems.at[partners[step]]).wait()
        width = span * edge
        pieces = []
        for step in steps:
            planes = rotations[partners[step]][:, 0, :]
            pieces += [planes[:, j * width : j * width + LANES] for j in range(strips)]
        turned = by_table(jnp.concatenate(pieces, axis=0), refs["template_lines"][...])
        for k in range(2 * span):
            lines[k, : turned.shape[0]] = turned[:, k * size : (k + 1) * size]
        for i, step in enumerate(steps):
            for first in range(0, orients, 2):
                pair = [
                    jnp.concatenate(
                        [lines[k, pl.ds(i * strips * orients + slot, strips, stride=orients), :] for k in range(2 * span)],
                        axis=0,
                    )
                    for slot in (first, first + 1)
                ]
                spun = table_by(refs["template_rows"][...], jnp.concatenate(pair, axis=1))
                for j in range(2):
                    templates[partners[step], planes_of[first + j]] = spun[:, j * size : (j + 1) * size]

    def spread(steps):
        for step in steps:
            if step:
                arrived = windows.at[partners[step], pl.ds(margin, rows)]
                pltpu.make_async_copy(arrived, arrived, window_sems.at[partners[step]]).wait()
                if brows > 1:
                    margin_of(partners[step]).start()

    forward(groups[0])
    expect(by_far, far)
    send(share_of, "far")
    send(window_of, "far")
    bunch = math.gcd(orients, 8)

    def rounds(do):
        if orients == bunch:
            do(0)
        else:
            pl.loop(0, orients // bunch)(lambda i: do(i * bunch))

    def combine(steps, lowest, more):
        for first in range(0, bunch, 2):
            for half in range(tile_rows // 8):
                top = pl.ds(half * 8, 8)
                low = pl.ds(tile_rows + half * 8, 8)
                for rotation in (lowest + first, lowest + first + 1):
                    straight = totals[rotation, top, :] if more else None
                    crossed = totals[rotation, low, :] if more else None
                    for step in steps:
                        plane = partners[step]
                        wave = templates[rotation, plane, top, :]
                        term = volumes[plane, top, :] * wave
                        turn = volumes[plane, low, :] * wave
                        straight = term if straight is None else straight + term
                        crossed = turn if crossed is None else crossed + turn
                    totals[rotation, top, :] = straight
                    totals[rotation, low, :] = crossed

    def finish(lowest, best):
        turned = []
        for first in range(0, bunch, 2):
            pair = jnp.concatenate([totals[lowest + first], totals[lowest + first + 1]], axis=1)
            turned.append(table_by(refs["score_rows"][...], pair))
        for part in turned:
            halved = [part[:, i * size : (i + 1) * size] for i in range(2)]
            waves = [jnp.concatenate([half[:rows], half[rows:]], axis=1) for half in halved]
            scored = by_table(jnp.concatenate(waves, axis=0), refs["score_lines"][...])
            found = jnp.maximum(scored[:rows], scored[rows:])
            best = found if best is None else jnp.maximum(best, found)
        return best

    unfold(groups[0])
    spread(groups[0])
    for steps in groups[1:]:
        forward(steps)
    transform(groups[0])
    for steps in groups[1:]:
        pl.when(row_id == brows - 1)(lambda: spread(steps))
        unfold(steps[: batch // 2])
        pl.when(row_id < brows - 1)(lambda: spread(steps))
        unfold(steps[batch // 2 :])
    for i, steps in enumerate(groups):
        if i:
            transform(steps)
        rounds(lambda lowest: combine(steps, lowest, i > 0))
    best = finish(0, None)
    if orients > bunch:
        best = lax.fori_loop(1, orients // bunch, lambda i, best: finish(i * bunch, best), best)
    best_ref[0] = best
    sent = [
        pencils.at[pl.ds(0, bcols - 1)],
        rotations.at[pl.ds(0, orients - 1), pl.ds(0, share)],
        rotations.at[pl.ds(0, orients), pl.ds(0, orients - share)],
        windows.at[pl.ds(0, orients - 1), pl.ds(margin, rows)],
        windows.at[pl.ds(0, orients), pl.ds(0, margin)],
    ]
    wanted = [bcols > 1, True, parts > 1, True, brows > 1]
    for i, ref in enumerate(sent):
        if wanted[i]:
            pltpu.make_async_copy(ref, ref, send_sems.at[i]).wait()


names = (
    "template",
    "index",
    "forward",
    "smoothing",
    "inverse",
    "template_lines",
    "template_rows",
    "volume_lines",
    "volume_rows",
    "score_rows",
    "score_lines",
    "box",
)


def staged(sizes, *refs):
    brick, sources = refs[0], refs[1 : len(names) + 1]
    results = refs[len(names) + 1 : len(names) + 3]
    held = refs[len(names) + 3 : 2 * len(names) + 3]
    rest = refs[2 * len(names) + 3 : -1]
    copies = {
        name: pltpu.make_async_copy(source, target, refs[-1].at[i])
        for i, (name, source, target) in enumerate(zip(names, sources, held))
    }
    named = dict(zip(names, held), brick=brick)
    match_kernel(sizes, named, copies, *rest, *results)


def shards(volume, template, voxel_maps):
    orients, brows, bcols = (lax.axis_size(axis) for axis in ("orient", "brow", "bcol"))
    planes, rows, cols = volume.shape
    edge = template.shape[0]
    half_edge = edge // 2
    length = cols * bcols
    size = cols + edge
    tile_rows = rows + edge
    margin = round_up(half_edge, 8)
    strips = 8
    batch = math.gcd(orients, 4)
    parts = brows if orients % (2 * brows) == 0 else 1
    base = half_edge - orients
    assert brows <= 2 and margin <= rows and tile_rows <= rows + 2 * margin
    assert base % 2 == 0 and orients % 2 == 0
    assert edge % strips == 0 and edge // strips * edge <= LANES
    width = edge // strips * edge * (strips - 1) + LANES
    width = round_up(width, LANES)
    vmem = pl.BlockSpec(memory_space=pltpu.VMEM)
    constants = (
        forward_table(length, bcols),
        smoothing_table(length),
        windowed_inverse(length, bcols, half_edge),
        template_lines(edge, size, strips),
        template_rows(tile_rows, edge, strips),
        right_table(line_table(size, size)),
        volume_rows(tile_rows),
        score_rows(tile_rows, rows),
        score_lines(size, cols),
        box_table(size, cols, edge),
    )
    sizes = (orients, brows, bcols, parts, edge, base, margin, batch, strips)
    operands = (volume, template.reshape(edge * edge, edge), voxel_maps)
    operands += tuple(jnp.asarray(c) for c in constants)
    best, scaling = pl.pallas_call(
        lambda *refs: staged(sizes, *refs),
        out_shape=(pltpu.VMEM((1, rows, cols), jnp.float32),) * 2,
        in_specs=[pl.BlockSpec(memory_space=pl.ANY)] * len(operands),
        out_specs=(vmem, vmem),
        scratch_shapes=[pltpu.VMEM(x.shape, x.dtype) for x in operands[1:]]
        + [
            pltpu.VMEM((2 * orients // parts, 1, width), jnp.float32),
            pltpu.VMEM((orients, orients, 1, width), jnp.float32),
            pltpu.VMEM((2 * edge // strips, strips * batch * orients, size), jnp.float32),
            pltpu.VMEM((orients, orients, tile_rows, size), jnp.float32),
            pltpu.VMEM((orients, 2 * tile_rows, size), jnp.float32),
            pltpu.VMEM((bcols, rows, cols), jnp.float32),
            pltpu.VMEM((orients, rows + 2 * margin, size), jnp.float32),
            pltpu.VMEM((tile_rows, size), jnp.float32),
            pltpu.VMEM((orients, 2 * tile_rows, size), jnp.float32),
            pltpu.VMEM((edge * edge, edge), jnp.float32),
            pltpu.VMEM((2 * round_up(edge * edge // 8, 16), 8 * edge), jnp.bfloat16),
            pltpu.VMEM((8, LANES), jnp.float32),
            pltpu.SemaphoreType.DMA,
            pltpu.SemaphoreType.DMA((bcols,)),
            pltpu.SemaphoreType.DMA((orients,)),
            pltpu.SemaphoreType.DMA((orients,)),
            pltpu.SemaphoreType.DMA((orients,)),
            pltpu.SemaphoreType.DMA((orients,)),
            pltpu.SemaphoreType.DMA((5,)),
            pltpu.SemaphoreType.REGULAR((5,)),
            pltpu.SemaphoreType.DMA((len(names),)),
        ],
        compiler_params=pltpu.CompilerParams(collective_id=0, has_side_effects=True),
        name="match",
    )(*operands)
    return best * scaling


def solution(mesh):
    in_specs = (P("orient", "brow", "bcol"), P(), P("orient", None))
    out_specs = P("orient", "brow", "bcol")
    return jax.shard_map(shards, mesh=mesh, in_specs=in_specs, out_specs=out_specs, check_vma=False)
```

```python
import math

import numpy as np
import jax
import jax.numpy as jnp
from jax import lax
from jax.experimental import pallas as pl
from jax.experimental.pallas import tpu as pltpu
from jax.sharding import PartitionSpec as P

epsilon = 1e-06
floor_share = 0.1
LANES = 128
MESH = pl.DeviceIdType.MESH


def round_up(value, step):
    return -(-value // step) * step


def split(table):
    upper = table.astype(jnp.bfloat16)
    lower = (table - upper.astype(np.float64)).astype(jnp.bfloat16)
    return upper, lower


def forward_table(length, parts):
    half = length // 2 + 1
    padded = round_up(half, LANES)
    angles = 2.0 * np.pi * (np.outer(np.arange(length), np.arange(half)) % length) / length
    table = np.zeros((length, 2 * padded))
    table[:, :half] = np.cos(angles)
    table[:, padded : padded + half] = -np.sin(angles)
    return np.stack(split(table.reshape(parts, length // parts, 2 * padded)))


def smoothing_table(length):
    half = length // 2 + 1
    padded = round_up(half, LANES)
    table = np.zeros((padded, padded))
    fold = np.minimum(np.arange(length), length - np.arange(length))
    for k in range(half):
        for shift in (-1, 0, 1):
            table[fold[(k + shift) % length], k] += 1.0 / 3.0
        for other in range(length):
            table[fold[other], k] += floor_share / length
    return np.stack(split(table))


def windowed_inverse(length, parts, margin):
    half = length // 2 + 1
    padded = round_up(half, LANES)
    width = length // parts
    tables = np.zeros((parts, 2 * padded, width + 2 * margin))
    k = np.arange(half)
    share = np.where((k == 0) | (2 * k == length), 1.0, 2.0)[:, None] / math.sqrt(length)
    for part in range(parts):
        columns = np.arange(width + 2 * margin) + part * width - margin
        inside = (columns >= 0) & (columns < length)
        angles = 2.0 * np.pi * (np.outer(k, columns) % length) / length
        tables[part, :half] = share * np.cos(angles) * inside
        tables[part, padded : padded + half] = -share * np.sin(angles) * inside
    return np.stack(split(tables))


def left_table(table):
    upper, lower = split(table)
    return np.concatenate([upper, lower, upper], axis=1)


def right_table(table):
    upper, lower = split(table)
    return np.concatenate([upper, upper, lower], axis=0)


def odd_waves(count, size):
    angles = np.pi * (np.outer(np.arange(count), 2 * np.arange(size // 2) + 1) % (2 * size)) / size
    return np.cos(angles), np.sin(angles)


def line_table(count, size):
    cos, sin = odd_waves(count, size)
    return np.concatenate([cos, -sin, -sin, -cos], axis=1)


def row_waves(size, count):
    angles = 2.0 * np.pi * (np.outer(np.arange(size), np.arange(count)) % size) / size
    return np.cos(angles), np.sin(angles)


def template_lines(edge, size, strips):
    span = edge // strips
    waves = line_table(edge, size)
    table = np.zeros((LANES, 2, span, size))
    for b in range(span):
        for half in range(2):
            table[b * edge : (b + 1) * edge, half, b] = waves[:, half * size : (half + 1) * size]
    return right_table(table.reshape(LANES, -1))


def template_rows(size, edge, strips):
    order = np.arange(edge).reshape(strips, edge // strips).T.reshape(-1)
    return left_table(np.concatenate([wave[:, order] for wave in row_waves(size, edge)], axis=1))


def volume_rows(size):
    cos, sin = row_waves(size, size)
    return left_table(np.block([[cos, sin], [-sin, cos]]))


def score_rows(size, rows):
    cos, sin = (wave.T / size for wave in row_waves(size, rows))
    return left_table(np.block([[cos, -sin], [sin, cos]]))


def score_lines(size, count):
    cos, sin = (wave.T * (2.0 / size) for wave in odd_waves(count, size))
    return right_table(np.concatenate([cos, cos, -sin, -sin], axis=0))


def box_table(size, count, edge):
    offsets = np.arange(size)[:, None] - np.arange(count)[None, :]
    return ((offsets >= 0) & (offsets < edge)).astype(jnp.bfloat16)


def split_table(template_ref, shifted):
    lines, edge = template_ref.shape
    template = template_ref[...] - 0.5
    shifted[...] = template
    mean = jnp.sum(template, keepdims=True) / (lines * edge)
    centred = template - mean
    scale = lax.rsqrt(jnp.sum(centred * centred, keepdims=True) + epsilon)
    table = jnp.concatenate([shifted[pl.ds(j, lines // 8, stride=8), :] for j in range(8)], axis=1)
    spare = round_up(lines // 8, 16) - lines // 8
    table = jnp.concatenate([table, jnp.zeros((spare, 8 * edge), jnp.float32)], axis=0)
    return jnp.concatenate(halves(table), axis=0), mean, scale


def look_up(pieces, index):
    count, span = pieces.shape
    width = index.shape[1]
    high = ((index.astype(jnp.float32) + 0.5) * (1.0 / span)).astype(jnp.int32)
    low = (index - high * span).astype(jnp.float32).astype(jnp.bfloat16)
    row = lax.broadcasted_iota(jnp.int32, (span, width), 0).astype(jnp.float32).astype(jnp.bfloat16)
    one = jnp.ones((), jnp.bfloat16)
    lanes = product(pieces, jnp.where(row == low, one, jnp.zeros_like(one)))
    lanes = lanes[: count // 2] + lanes[count // 2 :]
    mine = lax.broadcasted_iota(jnp.int32, lanes.shape, 0) == high
    return jnp.sum(jnp.where(mine, lanes, 0.0), axis=0, keepdims=True)


def halves(x):
    upper = x.astype(jnp.bfloat16)
    return upper, (x - upper.astype(jnp.float32)).astype(jnp.bfloat16)


def product(a, b):
    return jnp.dot(a, b, preferred_element_type=jnp.float32)


def by_table(x, table):
    upper, lower = halves(x)
    return product(jnp.concatenate([upper, lower, upper], axis=1), table)


def by_halves(x, upper, lower):
    high, low = halves(x)
    return product(high, upper) + (product(low, upper) + product(high, lower))


def table_by(table, x):
    upper, lower = halves(x)
    return product(table, jnp.concatenate([upper, upper, lower], axis=0))


def match_kernel(
    sizes,
    refs,
    copies,
    rotated,
    rotations,
    lines,
    templates,
    volumes,
    pencils,
    windows,
    energy,
    totals,
    normed,
    table,
    stats,
    own_sem,
    gather_sems,
    share_sems,
    turn_sems,
    window_sems,
    margin_sems,
    send_sems,
    tokens,
    best_ref,
    scaling_ref,
):
    orients, brows, bcols, parts, edge, base, margin, batch, strips = sizes
    half_edge = edge // 2
    rows, cols = refs["brick"].shape[1:]
    tile_rows, size = energy.shape
    skip = margin - half_edge
    me = lax.axis_index("orient")
    row_id = lax.axis_index("brow")
    col_id = lax.axis_index("bcol")
    share = orients // parts
    mine = lax.rem(row_id, parts)
    plane_voxels = edge * edge
    span = edge // strips

    def column_peer(column):
        return {"orient": me, "brow": row_id, "bcol": column}

    def partner(step):
        assert orients & (orients - 1) == 0
        other, weight = 0, 1
        while weight < orients:
            other = other + lax.rem(me // weight + step // weight, 2) * weight
            weight *= 2
        return other

    partners = [partner(step) for step in range(orients)]
    pair, last = me // 2, orients // 2 - 1
    odd = lax.rem(me, 2)
    by_column, by_row, by_pair, by_near, by_far = (tokens.at[i] for i in range(5))

    def plane_peer(plane):
        return {"orient": plane, "brow": row_id, "bcol": col_id}

    def row_peer(row):
        return {"orient": me, "brow": row, "bcol": col_id}

    def expect(semaphore, count):
        pl.when(count > 0)(lambda: pl.semaphore_wait(semaphore, count))

    def each(count, own, step, do):
        for other in range(count):

            @pl.when(step * other > step * own)
            def _():
                do(other)

    def greet(semaphore, peer):
        pl.semaphore_signal(semaphore, inc=1, device_id=peer, device_id_type=MESH)

    def first_of(part, plane):
        start = orients - plane
        rest = lax.rem(start, 2 * parts) + 2 * parts - 2 * part
        return start // (2 * parts) * 2 + (rest - 1) // (2 * parts) + (rest - 2) // (2 * parts)

    def plane_of(slot):
        part, index = slot // share, slot % share
        found = first_of(part, me) + index
        return found // 2 * (2 * parts) + 2 * part + lax.rem(found, 2) - orients + me

    windows[...] = jnp.zeros_like(windows)
    barrier = pltpu.get_barrier_semaphore()
    @pl.when(odd == 0)
    def _():
        each(orients, me, 1, lambda plane: greet(barrier, plane_peer(plane)))

    @pl.when(odd == 1)
    def _():
        each(orients // 2, pair, 1, lambda other: greet(barrier, plane_peer(2 * other + 1)))

    each(bcols, col_id, 1, lambda column: greet(barrier, column_peer(column)))
    each(brows, row_id, 1, lambda row: greet(barrier, row_peer(row)))
    tables = ("template_lines", "template_rows", "volume_lines", "volume_rows", "score_rows", "score_lines", "box")
    for name, copy in copies.items():
        if name not in tables:
            copy.start()
    own = pltpu.make_async_copy(refs["brick"].at[0], pencils.at[col_id], own_sem)
    own.start()
    energy[...] = jnp.zeros_like(energy)
    rotated[...] = jnp.zeros_like(rotated)
    planes_of = [plane_of(slot) for slot in range(orients)]

    def tabulate():
        copies["template"].wait()
        table[...], stats[0:1, 0:1], stats[1:2, 0:1] = split_table(refs["template"], normed)
        copies["index"].wait()

    def find(first, end):
        def one(index):
            plane = base + 2 * mine + 2 * parts * index

            def fill():
                start = pl.multiple_of(plane * plane_voxels, 2 * plane_voxels)
                found = look_up(table[...], refs["index"][0:1, pl.ds(start, 2 * plane_voxels)])
                found = (found - stats[0:1, 0:1]) * stats[1:2, 0:1]
                for i in range(2):
                    rotated[2 * index + i, :, :plane_voxels] = found[:, i * plane_voxels : (i + 1) * plane_voxels]

            if base < 0 or base + 2 * orients > edge:
                pl.when(jnp.logical_and(plane >= 0, plane < edge))(fill)
            else:
                fill()

        if share <= 4:
            for index in range(first, end):
                one(index)
        else:
            pl.loop(first, end)(one)

    expect(barrier, pair + odd * (pair + 1) + col_id + row_id)

    def gather_of(column, brick):
        return pltpu.make_async_remote_copy(
            src_ref=brick,
            dst_ref=pencils.at[col_id],
            send_sem=send_sems.at[0],
            recv_sem=gather_sems.at[col_id],
            device_id=column_peer(column),
            device_id_type=MESH,
        )

    each(bcols, col_id, -1, lambda column: gather_of(column, refs["brick"].at[0]).start())
    each(bcols, col_id, -1, lambda column: greet(by_column, column_peer(column)))
    each(brows, row_id, -1, lambda row: greet(by_row, row_peer(row)))

    @pl.when(odd == 1)
    def _():
        def answer(other):
            for i in range(2):
                greet(by_far, plane_peer(2 * other + i))

        greet(by_pair, plane_peer(me - 1))
        each(orients // 2, pair - 1, -1, answer)

        @pl.when(pair > 0)
        def _():
            for i in range(2):
                greet(by_near, plane_peer(2 * pair - 2 + i))

    for name in tables:
        copies[name].start()
    tabulate()
    find(0, share // 2)
    expect(by_column, bcols - 1 - col_id)
    own.wait()
    each(bcols, col_id, 1, lambda column: gather_of(column, pencils.at[col_id]).start())
    find(share // 2, share)
    expect(by_row, brows - 1 - row_id)

    def block(rotation, part):
        return rotations.at[rotation, pl.ds(part * share, share)]

    def share_of(plane):
        return pltpu.make_async_remote_copy(
            src_ref=rotated.at[pl.ds(first_of(mine, plane), share)],
            dst_ref=block(me, mine),
            send_sem=send_sems.at[1],
            recv_sem=share_sems.at[me],
            device_id=plane_peer(plane),
            device_id_type=MESH,
        )

    def turn_of(rotation, turn):
        row = lax.rem(row_id + turn, brows)
        return pltpu.make_async_remote_copy(
            src_ref=block(rotation, mine),
            dst_ref=block(rotation, mine),
            send_sem=send_sems.at[2],
            recv_sem=turn_sems.at[rotation],
            device_id=row_peer(row),
            device_id_type=MESH,
        )

    rotations[me, pl.ds(mine * share, share)] = rotated[pl.ds(first_of(mine, me), share)]
    for turn in range(1, parts):
        turn_of(me, turn).start()
    expect(by_pair, 1 - odd)
    each(orients, me, -1, lambda plane: share_of(plane).start())
    pl.when(odd == 0)(lambda: share_of(me + 1).start())
    near = (2 * last - pair) // (last + 1)
    far = last - pair - near

    def send(kind, planes):
        def one(plane):
            if planes == "near":
                pl.when(plane < 2 * pair + 4)(lambda: kind(plane).start())
            else:
                pl.when(plane >= 2 * pair + 4)(lambda: kind(plane).start())

        each(orients, 2 * pair + 1, 1, one)

    expect(by_near, near)
    send(share_of, "near")

    def forward(steps):
        for step in steps:
            if step:
                arrived = block(partners[step], mine)
                pltpu.make_async_copy(arrived, arrived, share_sems.at[partners[step]]).wait()
                for turn in range(1, parts):
                    turn_of(partners[step], turn).start()

    groups = [list(range(first, first + batch)) for first in range(0, orients, batch)]
    for name in ("forward", "smoothing", "inverse"):
        copies[name].wait()

    def wave(column):
        return by_halves(pencils[column], refs["forward"][0, column], refs["forward"][1, column])

    both = wave(col_id)
    for step in range(1, bcols):
        column = lax.rem(col_id + step, bcols)
        arrived = pencils.at[column]
        pltpu.make_async_copy(arrived, arrived, gather_sems.at[column]).wait()
    for step in range(1, bcols):
        both = both + wave(lax.rem(col_id + step, bcols))
    padded = both.shape[1] // 2
    real, imag = both[:, :padded], both[:, padded:]
    power = real * real + imag * imag
    weights = lax.rsqrt(by_halves(power, refs["smoothing"][0], refs["smoothing"][1]) + epsilon)
    white = both * jnp.concatenate([weights, weights], axis=1)
    windows[me, margin : margin + rows] = by_halves(
        white, refs["inverse"][0, col_id], refs["inverse"][1, col_id]
    )

    def window_of(plane):
        part = windows.at[me, pl.ds(margin, rows)]
        return pltpu.make_async_remote_copy(
            src_ref=part,
            dst_ref=part,
            send_sem=send_sems.at[3],
            recv_sem=window_sems.at[me],
            device_id=plane_peer(plane),
            device_id_type=MESH,
        )

    def margin_of(plane):
        return pltpu.make_async_remote_copy(
            src_ref=windows.at[plane, pl.ds(pl.multiple_of(rows - row_id * (rows - margin), 8), margin)],
            dst_ref=windows.at[plane, pl.ds(pl.multiple_of(row_id * (margin + rows), 8), margin)],
            send_sem=send_sems.at[4],
            recv_sem=margin_sems.at[plane],
            device_id=row_peer(lax.rem(row_id + 1, brows)),
            device_id_type=MESH,
        )

    each(orients, me, -1, lambda plane: window_of(plane).start())
    pl.when(odd == 0)(lambda: window_of(me + 1).start())
    send(window_of, "near")
    if brows > 1:
        margin_of(me).start()
    for name in tables:
        copies[name].wait()

    def normalise():
        summed = energy[0:rows, :]
        for b in range(1, edge):
            summed = summed + energy[b : b + rows, :]
        upper, lower = halves(summed)
        boxed = product(upper, refs["box"][...]) + product(lower, refs["box"][...])
        scaling_ref[0] = lax.rsqrt(boxed / edge**3 + epsilon)

    def transform(steps):
        tiles = []
        for step in steps:
            plane = partners[step]
            if brows > 1:
                arrived = windows.at[plane, pl.ds(0, margin)]
                pltpu.make_async_copy(arrived, arrived, margin_sems.at[plane]).wait()
            tile = windows[plane, skip : skip + tile_rows]
            gap = plane - me
            near = jnp.logical_and(gap >= -half_edge, gap < half_edge).astype(jnp.float32)
            energy[...] += tile * tile * near
            tiles.append(tile)
        turned = by_table(jnp.concatenate(tiles, axis=0), refs["volume_lines"][...])
        if steps is groups[-1]:
            normalise()
        for first in range(0, len(steps), 2):
            pair = []
            for i in range(first, first + 2):
                part = turned[i * tile_rows : (i + 1) * tile_rows]
                pair.append(jnp.concatenate([part[:, :size], part[:, size:]], axis=0))
            spun = table_by(refs["volume_rows"][...], jnp.concatenate(pair, axis=1))
            for i in range(2):
                volumes[partners[steps[first + i]]] = spun[:, i * size : (i + 1) * size]

    def unfold(steps):
        for step in steps:
            if parts > 1:
                arrived = rotations.at[partners[step], pl.ds(0, orients - share)]
                pltpu.make_async_copy(arrived, arrived, turn_sems.at[partners[step]]).wait()
        width = span * edge
        pieces = []
        for step in steps:
            planes = rotations[partners[step]][:, 0, :]
            pieces += [planes[:, j * width : j * width + LANES] for j in range(strips)]
        turned = by_table(jnp.concatenate(pieces, axis=0), refs["template_lines"][...])
        for k in range(2 * span):
            lines[k, : turned.shape[0]] = turned[:, k * size : (k + 1) * size]
        for i, step in enumerate(steps):
            for first in range(0, orients, 2):
                pair = [
                    jnp.concatenate(
                        [lines[k, pl.ds(i * strips * orients + slot, strips, stride=orients), :] for k in range(2 * span)],
                        axis=0,
                    )
                    for slot in (first, first + 1)
                ]
                spun = table_by(refs["template_rows"][...], jnp.concatenate(pair, axis=1))
                for j in range(2):
                    templates[partners[step], planes_of[first + j]] = spun[:, j * size : (j + 1) * size]

    def spread(steps):
        for step in steps:
            if step:
                arrived = windows.at[partners[step], pl.ds(margin, rows)]
                pltpu.make_async_copy(arrived, arrived, window_sems.at[partners[step]]).wait()
                if brows > 1:
                    margin_of(partners[step]).start()

    forward(groups[0])
    expect(by_far, far)
    send(share_of, "far")
    send(window_of, "far")
    bunch = math.gcd(orients, 8)

    def rounds(do):
        if orients == bunch:
            do(0)
        else:
            pl.loop(0, orients // bunch)(lambda i: do(i * bunch))

    def combine(steps, lowest, more):
        for first in range(0, bunch, 2):
            for half in range(tile_rows // 8):
                top = pl.ds(half * 8, 8)
                low = pl.ds(tile_rows + half * 8, 8)
                for rotation in (lowest + first, lowest + first + 1):
                    straight = totals[rotation, top, :] if more else None
                    crossed = totals[rotation, low, :] if more else None
                    for step in steps:
                        plane = partners[step]
                        wave = templates[rotation, plane, top, :]
                        term = volumes[plane, top, :] * wave
                        turn = volumes[plane, low, :] * wave
                        straight = term if straight is None else straight + term
                        crossed = turn if crossed is None else crossed + turn
                    totals[rotation, top, :] = straight
                    totals[rotation, low, :] = crossed

    def finish(lowest, best):
        turned = []
        for first in range(0, bunch, 2):
            pair = jnp.concatenate([totals[lowest + first], totals[lowest + first + 1]], axis=1)
            turned.append(table_by(refs["score_rows"][...], pair))
        for part in turned:
            halved = [part[:, i * size : (i + 1) * size] for i in range(2)]
            waves = [jnp.concatenate([half[:rows], half[rows:]], axis=1) for half in halved]
            scored = by_table(jnp.concatenate(waves, axis=0), refs["score_lines"][...])
            found = jnp.maximum(scored[:rows], scored[rows:])
            best = found if best is None else jnp.maximum(best, found)
        return best

    unfold(groups[0])
    for steps in groups[1:]:
        forward(steps)
    spread(groups[0])
    for steps in groups[1:]:
        unfold(steps)
        pl.when(row_id == brows - 1)(lambda: spread(steps))
    transform(groups[0])
    for steps in groups[1:]:
        pl.when(row_id < brows - 1)(lambda: spread(steps))
    for i, steps in enumerate(groups):
        if i:
            transform(steps)
        rounds(lambda lowest: combine(steps, lowest, i > 0))
    best = finish(0, None)
    if orients > bunch:
        best = lax.fori_loop(1, orients // bunch, lambda i, best: finish(i * bunch, best), best)
    best_ref[0] = best
    sent = [
        pencils.at[pl.ds(0, bcols - 1)],
        rotations.at[pl.ds(0, orients - 1), pl.ds(0, share)],
        rotations.at[pl.ds(0, orients), pl.ds(0, orients - share)],
        windows.at[pl.ds(0, orients - 1), pl.ds(margin, rows)],
        windows.at[pl.ds(0, orients), pl.ds(0, margin)],
    ]
    wanted = [bcols > 1, True, parts > 1, True, brows > 1]
    for i, ref in enumerate(sent):
        if wanted[i]:
            pltpu.make_async_copy(ref, ref, send_sems.at[i]).wait()


names = (
    "template",
    "index",
    "forward",
    "smoothing",
    "inverse",
    "template_lines",
    "template_rows",
    "volume_lines",
    "volume_rows",
    "score_rows",
    "score_lines",
    "box",
)


def staged(sizes, *refs):
    brick, sources = refs[0], refs[1 : len(names) + 1]
    results = refs[len(names) + 1 : len(names) + 3]
    held = refs[len(names) + 3 : 2 * len(names) + 3]
    rest = refs[2 * len(names) + 3 : -1]
    copies = {
        name: pltpu.make_async_copy(source, target, refs[-1].at[i])
        for i, (name, source, target) in enumerate(zip(names, sources, held))
    }
    named = dict(zip(names, held), brick=brick)
    match_kernel(sizes, named, copies, *rest, *results)


def shards(volume, template, voxel_maps):
    orients, brows, bcols = (lax.axis_size(axis) for axis in ("orient", "brow", "bcol"))
    planes, rows, cols = volume.shape
    edge = template.shape[0]
    half_edge = edge // 2
    length = cols * bcols
    size = cols + edge
    tile_rows = rows + edge
    margin = round_up(half_edge, 8)
    strips = 8
    batch = math.gcd(orients, 4)
    parts = brows if orients % (2 * brows) == 0 else 1
    base = half_edge - orients
    assert brows <= 2 and margin <= rows and tile_rows <= rows + 2 * margin
    assert base % 2 == 0 and orients % 2 == 0
    assert edge % strips == 0 and edge // strips * edge <= LANES
    width = edge // strips * edge * (strips - 1) + LANES
    width = round_up(width, LANES)
    vmem = pl.BlockSpec(memory_space=pltpu.VMEM)
    constants = (
        forward_table(length, bcols),
        smoothing_table(length),
        windowed_inverse(length, bcols, half_edge),
        template_lines(edge, size, strips),
        template_rows(tile_rows, edge, strips),
        right_table(line_table(size, size)),
        volume_rows(tile_rows),
        score_rows(tile_rows, rows),
        score_lines(size, cols),
        box_table(size, cols, edge),
    )
    sizes = (orients, brows, bcols, parts, edge, base, margin, batch, strips)
    operands = (volume, template.reshape(edge * edge, edge), voxel_maps)
    operands += tuple(jnp.asarray(c) for c in constants)
    best, scaling = pl.pallas_call(
        lambda *refs: staged(sizes, *refs),
        out_shape=(pltpu.VMEM((1, rows, cols), jnp.float32),) * 2,
        in_specs=[pl.BlockSpec(memory_space=pl.ANY)] * len(operands),
        out_specs=(vmem, vmem),
        scratch_shapes=[pltpu.VMEM(x.shape, x.dtype) for x in operands[1:]]
        + [
            pltpu.VMEM((2 * orients // parts, 1, width), jnp.float32),
            pltpu.VMEM((orients, orients, 1, width), jnp.float32),
            pltpu.VMEM((2 * edge // strips, strips * batch * orients, size), jnp.float32),
            pltpu.VMEM((orients, orients, tile_rows, size), jnp.float32),
            pltpu.VMEM((orients, 2 * tile_rows, size), jnp.float32),
            pltpu.VMEM((bcols, rows, cols), jnp.float32),
            pltpu.VMEM((orients, rows + 2 * margin, size), jnp.float32),
            pltpu.VMEM((tile_rows, size), jnp.float32),
            pltpu.VMEM((orients, 2 * tile_rows, size), jnp.float32),
            pltpu.VMEM((edge * edge, edge), jnp.float32),
            pltpu.VMEM((2 * round_up(edge * edge // 8, 16), 8 * edge), jnp.bfloat16),
            pltpu.VMEM((8, LANES), jnp.float32),
            pltpu.SemaphoreType.DMA,
            pltpu.SemaphoreType.DMA((bcols,)),
            pltpu.SemaphoreType.DMA((orients,)),
            pltpu.SemaphoreType.DMA((orients,)),
            pltpu.SemaphoreType.DMA((orients,)),
            pltpu.SemaphoreType.DMA((orients,)),
            pltpu.SemaphoreType.DMA((5,)),
            pltpu.SemaphoreType.REGULAR((5,)),
            pltpu.SemaphoreType.DMA((len(names),)),
        ],
        compiler_params=pltpu.CompilerParams(collective_id=0, has_side_effects=True),
        name="match",
    )(*operands)
    return best * scaling


def solution(mesh):
    in_specs = (P("orient", "brow", "bcol"), P(), P("orient", None))
    out_specs = P("orient", "brow", "bcol")
    return jax.shard_map(shards, mesh=mesh, in_specs=in_specs, out_specs=out_specs, check_vma=False)
```

```python
import math

import numpy as np
import jax
import jax.numpy as jnp
from jax import lax
from jax.experimental import pallas as pl
from jax.experimental.pallas import tpu as pltpu
from jax.sharding import PartitionSpec as P

epsilon = 1e-06
floor_share = 0.1
LANES = 128
MESH = pl.DeviceIdType.MESH


def round_up(value, step):
    return -(-value // step) * step


def split(table):
    upper = table.astype(jnp.bfloat16)
    lower = (table - upper.astype(np.float64)).astype(jnp.bfloat16)
    return upper, lower


def forward_table(length, parts):
    half = length // 2 + 1
    padded = round_up(half, LANES)
    angles = 2.0 * np.pi * (np.outer(np.arange(length), np.arange(half)) % length) / length
    table = np.zeros((length, 2 * padded))
    table[:, :half] = np.cos(angles)
    table[:, padded : padded + half] = -np.sin(angles)
    return np.stack(split(table.reshape(parts, length // parts, 2 * padded)))


def smoothing_table(length):
    half = length // 2 + 1
    padded = round_up(half, LANES)
    table = np.zeros((padded, padded))
    fold = np.minimum(np.arange(length), length - np.arange(length))
    for k in range(half):
        for shift in (-1, 0, 1):
            table[fold[(k + shift) % length], k] += 1.0 / 3.0
        for other in range(length):
            table[fold[other], k] += floor_share / length
    return np.stack(split(table))


def windowed_inverse(length, parts, margin):
    half = length // 2 + 1
    padded = round_up(half, LANES)
    width = length // parts
    tables = np.zeros((parts, 2 * padded, width + 2 * margin))
    k = np.arange(half)
    share = np.where((k == 0) | (2 * k == length), 1.0, 2.0)[:, None] / math.sqrt(length)
    for part in range(parts):
        columns = np.arange(width + 2 * margin) + part * width - margin
        inside = (columns >= 0) & (columns < length)
        angles = 2.0 * np.pi * (np.outer(k, columns) % length) / length
        tables[part, :half] = share * np.cos(angles) * inside
        tables[part, padded : padded + half] = -share * np.sin(angles) * inside
    return np.stack(split(tables))


def left_table(table):
    upper, lower = split(table)
    return np.concatenate([upper, lower, upper], axis=1)


def right_table(table):
    upper, lower = split(table)
    return np.concatenate([upper, upper, lower], axis=0)


def odd_waves(count, size):
    angles = np.pi * (np.outer(np.arange(count), 2 * np.arange(size // 2) + 1) % (2 * size)) / size
    return np.cos(angles), np.sin(angles)


def line_table(count, size):
    cos, sin = odd_waves(count, size)
    return np.concatenate([cos, -sin, -sin, -cos], axis=1)


def row_waves(size, count):
    angles = 2.0 * np.pi * (np.outer(np.arange(size), np.arange(count)) % size) / size
    return np.cos(angles), np.sin(angles)


def template_lines(edge, size, strips):
    span = edge // strips
    waves = line_table(edge, size)
    table = np.zeros((LANES, 2, span, size))
    for b in range(span):
        for half in range(2):
            table[b * edge : (b + 1) * edge, half, b] = waves[:, half * size : (half + 1) * size]
    return right_table(table.reshape(LANES, -1))


def template_rows(size, edge, strips):
    order = np.arange(edge).reshape(strips, edge // strips).T.reshape(-1)
    return left_table(np.concatenate([wave[:, order] for wave in row_waves(size, edge)], axis=1))


def volume_rows(size):
    cos, sin = row_waves(size, size)
    return left_table(np.block([[cos, sin], [-sin, cos]]))


def score_rows(size, rows):
    cos, sin = (wave.T / size for wave in row_waves(size, rows))
    return left_table(np.block([[cos, -sin], [sin, cos]]))


def score_lines(size, count):
    cos, sin = (wave.T * (2.0 / size) for wave in odd_waves(count, size))
    return right_table(np.concatenate([cos, cos, -sin, -sin], axis=0))


def box_table(size, count, edge):
    offsets = np.arange(size)[:, None] - np.arange(count)[None, :]
    return ((offsets >= 0) & (offsets < edge)).astype(jnp.bfloat16)


def split_table(template_ref, shifted):
    lines, edge = template_ref.shape
    template = template_ref[...] - 0.5
    shifted[...] = template
    mean = jnp.sum(template, keepdims=True) / (lines * edge)
    centred = template - mean
    scale = lax.rsqrt(jnp.sum(centred * centred, keepdims=True) + epsilon)
    table = jnp.concatenate([shifted[pl.ds(j, lines // 8, stride=8), :] for j in range(8)], axis=1)
    spare = round_up(lines // 8, 16) - lines // 8
    table = jnp.concatenate([table, jnp.zeros((spare, 8 * edge), jnp.float32)], axis=0)
    return jnp.concatenate(halves(table), axis=0), mean, scale


def look_up(pieces, index):
    count, span = pieces.shape
    width = index.shape[1]
    high = ((index.astype(jnp.float32) + 0.5) * (1.0 / span)).astype(jnp.int32)
    low = (index - high * span).astype(jnp.float32).astype(jnp.bfloat16)
    row = lax.broadcasted_iota(jnp.int32, (span, width), 0).astype(jnp.float32).astype(jnp.bfloat16)
    one = jnp.ones((), jnp.bfloat16)
    lanes = product(pieces, jnp.where(row == low, one, jnp.zeros_like(one)))
    lanes = lanes[: count // 2] + lanes[count // 2 :]
    mine = lax.broadcasted_iota(jnp.int32, lanes.shape, 0) == high
    return jnp.sum(jnp.where(mine, lanes, 0.0), axis=0, keepdims=True)


def halves(x):
    upper = x.astype(jnp.bfloat16)
    return upper, (x - upper.astype(jnp.float32)).astype(jnp.bfloat16)


def product(a, b):
    return jnp.dot(a, b, preferred_element_type=jnp.float32)


def by_table(x, table):
    upper, lower = halves(x)
    return product(jnp.concatenate([upper, lower, upper], axis=1), table)


def by_halves(x, upper, lower):
    high, low = halves(x)
    return product(high, upper) + (product(low, upper) + product(high, lower))


def table_by(table, x):
    upper, lower = halves(x)
    return product(table, jnp.concatenate([upper, upper, lower], axis=0))


def match_kernel(
    sizes,
    refs,
    copies,
    rotated,
    rotations,
    lines,
    templates,
    volumes,
    pencils,
    windows,
    energy,
    totals,
    normed,
    table,
    stats,
    own_sem,
    gather_sems,
    share_sems,
    turn_sems,
    window_sems,
    margin_sems,
    send_sems,
    tokens,
    best_ref,
    scaling_ref,
):
    orients, brows, bcols, parts, edge, base, margin, batch, strips = sizes
    half_edge = edge // 2
    rows, cols = refs["brick"].shape[1:]
    tile_rows, size = energy.shape
    skip = margin - half_edge
    me = lax.axis_index("orient")
    row_id = lax.axis_index("brow")
    col_id = lax.axis_index("bcol")
    share = orients // parts
    mine = lax.rem(row_id, parts)
    plane_voxels = edge * edge
    span = edge // strips

    def column_peer(column):
        return {"orient": me, "brow": row_id, "bcol": column}

    def partner(step):
        assert orients & (orients - 1) == 0
        other, weight = 0, 1
        while weight < orients:
            other = other + lax.rem(me // weight + step // weight, 2) * weight
            weight *= 2
        return other

    partners = [partner(step) for step in range(orients)]
    pair, last = me // 2, orients // 2 - 1
    odd = lax.rem(me, 2)
    by_column, by_row, by_pair, by_near, by_far = (tokens.at[i] for i in range(5))

    def plane_peer(plane):
        return {"orient": plane, "brow": row_id, "bcol": col_id}

    def row_peer(row):
        return {"orient": me, "brow": row, "bcol": col_id}

    def expect(semaphore, count):
        pl.when(count > 0)(lambda: pl.semaphore_wait(semaphore, count))

    def each(count, own, step, do):
        for other in range(count):

            @pl.when(step * other > step * own)
            def _():
                do(other)

    def greet(semaphore, peer):
        pl.semaphore_signal(semaphore, inc=1, device_id=peer, device_id_type=MESH)

    def first_of(part, plane):
        start = orients - plane
        rest = lax.rem(start, 2 * parts) + 2 * parts - 2 * part
        return start // (2 * parts) * 2 + (rest - 1) // (2 * parts) + (rest - 2) // (2 * parts)

    def plane_of(slot):
        part, index = slot // share, slot % share
        found = first_of(part, me) + index
        return found // 2 * (2 * parts) + 2 * part + lax.rem(found, 2) - orients + me

    windows[...] = jnp.zeros_like(windows)
    barrier = pltpu.get_barrier_semaphore()
    @pl.when(odd == 0)
    def _():
        each(orients, me, 1, lambda plane: greet(barrier, plane_peer(plane)))

    @pl.when(odd == 1)
    def _():
        each(orients // 2, pair, 1, lambda other: greet(barrier, plane_peer(2 * other + 1)))

    each(bcols, col_id, 1, lambda column: greet(barrier, column_peer(column)))
    each(brows, row_id, 1, lambda row: greet(barrier, row_peer(row)))
    tables = ("template_lines", "template_rows", "volume_lines", "volume_rows", "score_rows", "score_lines", "box")
    for name, copy in copies.items():
        if name not in tables:
            copy.start()
    own = pltpu.make_async_copy(refs["brick"].at[0], pencils.at[col_id], own_sem)
    own.start()
    energy[...] = jnp.zeros_like(energy)
    rotated[...] = jnp.zeros_like(rotated)
    planes_of = [plane_of(slot) for slot in range(orients)]

    def tabulate():
        copies["template"].wait()
        table[...], stats[0:1, 0:1], stats[1:2, 0:1] = split_table(refs["template"], normed)
        copies["index"].wait()

    def find(first, end):
        def one(index):
            plane = base + 2 * mine + 2 * parts * index

            def fill():
                start = pl.multiple_of(plane * plane_voxels, 2 * plane_voxels)
                found = look_up(table[...], refs["index"][0:1, pl.ds(start, 2 * plane_voxels)])
                found = (found - stats[0:1, 0:1]) * stats[1:2, 0:1]
                for i in range(2):
                    rotated[2 * index + i, :, :plane_voxels] = found[:, i * plane_voxels : (i + 1) * plane_voxels]

            if base < 0 or base + 2 * orients > edge:
                pl.when(jnp.logical_and(plane >= 0, plane < edge))(fill)
            else:
                fill()

        if share <= 4:
            for index in range(first, end):
                one(index)
        else:
            pl.loop(first, end)(one)

    expect(barrier, pair + odd * (pair + 1) + col_id + row_id)

    def gather_of(column, brick):
        return pltpu.make_async_remote_copy(
            src_ref=brick,
            dst_ref=pencils.at[col_id],
            send_sem=send_sems.at[0],
            recv_sem=gather_sems.at[col_id],
            device_id=column_peer(column),
            device_id_type=MESH,
        )

    each(bcols, col_id, -1, lambda column: gather_of(column, refs["brick"].at[0]).start())
    each(bcols, col_id, -1, lambda column: greet(by_column, column_peer(column)))
    each(brows, row_id, -1, lambda row: greet(by_row, row_peer(row)))

    @pl.when(odd == 1)
    def _():
        def answer(other):
            for i in range(2):
                greet(by_far, plane_peer(2 * other + i))

        greet(by_pair, plane_peer(me - 1))
        each(orients // 2, pair - 1, -1, answer)

        @pl.when(pair > 0)
        def _():
            for i in range(2):
                greet(by_near, plane_peer(2 * pair - 2 + i))

    for name in tables:
        copies[name].start()
    tabulate()
    find(0, share // 2)
    expect(by_column, bcols - 1 - col_id)
    own.wait()
    each(bcols, col_id, 1, lambda column: gather_of(column, pencils.at[col_id]).start())
    find(share // 2, share)

    def block(rotation, part):
        return rotations.at[rotation, pl.ds(part * share, share)]

    def share_of(plane):
        return pltpu.make_async_remote_copy(
            src_ref=rotated.at[pl.ds(first_of(mine, plane), share)],
            dst_ref=block(me, mine),
            send_sem=send_sems.at[1],
            recv_sem=share_sems.at[me],
            device_id=plane_peer(plane),
            device_id_type=MESH,
        )

    def turn_of(step, turn):
        rotation = partners[step]
        row = lax.rem(row_id + turn, brows)
        return pltpu.make_async_remote_copy(
            src_ref=block(rotation, mine),
            dst_ref=block(rotation, mine),
            send_sem=send_sems.at[2],
            recv_sem=turn_sems.at[step // batch],
            device_id=row_peer(row),
            device_id_type=MESH,
        )

    expect(by_pair, 1 - odd)
    each(orients, me, -1, lambda plane: share_of(plane).start())
    pl.when(odd == 0)(lambda: share_of(me + 1).start())
    expect(by_row, brows - 1 - row_id)
    rotations[me, pl.ds(mine * share, share)] = rotated[pl.ds(first_of(mine, me), share)]
    for turn in range(1, parts):
        turn_of(0, turn).start()
    near = (2 * last - pair) // (last + 1)
    far = last - pair - near

    def send(kind, planes):
        def one(plane):
            if planes == "near":
                pl.when(plane < 2 * pair + 4)(lambda: kind(plane).start())
            else:
                pl.when(plane >= 2 * pair + 4)(lambda: kind(plane).start())

        each(orients, 2 * pair + 1, 1, one)

    expect(by_near, near)
    send(share_of, "near")

    def forward(steps):
        for step in steps:
            if step:
                arrived = block(partners[step], mine)
                pltpu.make_async_copy(arrived, arrived, share_sems.at[partners[step]]).wait()
                for turn in range(1, parts):
                    turn_of(step, turn).start()

    groups = [list(range(first, first + batch)) for first in range(0, orients, batch)]
    for name in ("forward", "smoothing", "inverse"):
        copies[name].wait()

    def wave(column):
        return by_halves(pencils[column], refs["forward"][0, column], refs["forward"][1, column])

    both = wave(col_id)
    for step in range(1, bcols):
        column = lax.rem(col_id + step, bcols)
        arrived = pencils.at[column]
        pltpu.make_async_copy(arrived, arrived, gather_sems.at[column]).wait()
    for step in range(1, bcols):
        both = both + wave(lax.rem(col_id + step, bcols))
    padded = both.shape[1] // 2
    real, imag = both[:, :padded], both[:, padded:]
    power = real * real + imag * imag
    weights = lax.rsqrt(by_halves(power, refs["smoothing"][0], refs["smoothing"][1]) + epsilon)
    white = both * jnp.concatenate([weights, weights], axis=1)
    windows[me, margin : margin + rows] = by_halves(
        white, refs["inverse"][0, col_id], refs["inverse"][1, col_id]
    )

    def window_of(plane):
        part = windows.at[me, pl.ds(margin, rows)]
        return pltpu.make_async_remote_copy(
            src_ref=part,
            dst_ref=part,
            send_sem=send_sems.at[3],
            recv_sem=window_sems.at[me],
            device_id=plane_peer(plane),
            device_id_type=MESH,
        )

    def margin_of(step):
        plane = partners[step]
        return pltpu.make_async_remote_copy(
            src_ref=windows.at[plane, pl.ds(pl.multiple_of(rows - row_id * (rows - margin), 8), margin)],
            dst_ref=windows.at[plane, pl.ds(pl.multiple_of(row_id * (margin + rows), 8), margin)],
            send_sem=send_sems.at[4],
            recv_sem=margin_sems.at[step // batch],
            device_id=row_peer(lax.rem(row_id + 1, brows)),
            device_id_type=MESH,
        )

    each(orients, me, -1, lambda plane: window_of(plane).start())
    pl.when(odd == 0)(lambda: window_of(me + 1).start())
    send(window_of, "near")
    if brows > 1:
        margin_of(0).start()
    for name in tables:
        copies[name].wait()

    def normalise():
        summed = energy[0:rows, :]
        for b in range(1, edge):
            summed = summed + energy[b : b + rows, :]
        upper, lower = halves(summed)
        boxed = product(upper, refs["box"][...]) + product(lower, refs["box"][...])
        scaling_ref[0] = lax.rsqrt(boxed / edge**3 + epsilon)

    def transform(steps):
        if brows > 1:
            arrived = windows.at[pl.ds(0, batch), pl.ds(0, margin)]
            pltpu.make_async_copy(arrived, arrived, margin_sems.at[steps[0] // batch]).wait()
        tiles = []
        for step in steps:
            plane = partners[step]
            tile = windows[plane, skip : skip + tile_rows]
            gap = plane - me
            near = jnp.logical_and(gap >= -half_edge, gap < half_edge).astype(jnp.float32)
            energy[...] += tile * tile * near
            tiles.append(tile)
        turned = by_table(jnp.concatenate(tiles, axis=0), refs["volume_lines"][...])
        if steps is groups[-1]:
            normalise()
        for first in range(0, len(steps), 2):
            pair = []
            for i in range(first, first + 2):
                part = turned[i * tile_rows : (i + 1) * tile_rows]
                pair.append(jnp.concatenate([part[:, :size], part[:, size:]], axis=0))
            spun = table_by(refs["volume_rows"][...], jnp.concatenate(pair, axis=1))
            for i in range(2):
                volumes[partners[steps[first + i]]] = spun[:, i * size : (i + 1) * size]

    def unfold(steps):
        if parts > 1:
            arrived = rotations.at[pl.ds(0, batch), pl.ds(0, orients - share)]
            pltpu.make_async_copy(arrived, arrived, turn_sems.at[steps[0] // batch]).wait()
        width = span * edge
        pieces = []
        for step in steps:
            planes = rotations[partners[step]][:, 0, :]
            pieces += [planes[:, j * width : j * width + LANES] for j in range(strips)]
        turned = by_table(jnp.concatenate(pieces, axis=0), refs["template_lines"][...])
        for k in range(2 * span):
            lines[k, : turned.shape[0]] = turned[:, k * size : (k + 1) * size]
        for i, step in enumerate(steps):
            for first in range(0, orients, 2):
                pair = [
                    jnp.concatenate(
                        [lines[k, pl.ds(i * strips * orients + slot, strips, stride=orients), :] for k in range(2 * span)],
                        axis=0,
                    )
                    for slot in (first, first + 1)
                ]
                spun = table_by(refs["template_rows"][...], jnp.concatenate(pair, axis=1))
                for j in range(2):
                    templates[partners[step], planes_of[first + j]] = spun[:, j * size : (j + 1) * size]

    def spread(steps):
        for step in steps:
            if step:
                arrived = windows.at[partners[step], pl.ds(margin, rows)]
                pltpu.make_async_copy(arrived, arrived, window_sems.at[partners[step]]).wait()
                if brows > 1:
                    margin_of(step).start()

    forward(groups[0])
    expect(by_far, far)
    send(share_of, "far")
    send(window_of, "far")
    bunch = math.gcd(orients, 8)

    def rounds(do):
        if orients == bunch:
            do(0)
        else:
            pl.loop(0, orients // bunch)(lambda i: do(i * bunch))

    def combine(steps, lowest, more):
        for first in range(0, bunch, 2):
            for half in range(tile_rows // 8):
                top = pl.ds(half * 8, 8)
                low = pl.ds(tile_rows + half * 8, 8)
                for rotation in (lowest + first, lowest + first + 1):
                    straight = totals[rotation, top, :] if more else None
                    crossed = totals[rotation, low, :] if more else None
                    for step in steps:
                        plane = partners[step]
                        wave = templates[rotation, plane, top, :]
                        term = volumes[plane, top, :] * wave
                        turn = volumes[plane, low, :] * wave
                        straight = term if straight is None else straight + term
                        crossed = turn if crossed is None else crossed + turn
                    totals[rotation, top, :] = straight
                    totals[rotation, low, :] = crossed

    def finish(lowest, best):
        turned = []
        for first in range(0, bunch, 2):
            pair = jnp.concatenate([totals[lowest + first], totals[lowest + first + 1]], axis=1)
            turned.append(table_by(refs["score_rows"][...], pair))
        for part in turned:
            halved = [part[:, i * size : (i + 1) * size] for i in range(2)]
            waves = [jnp.concatenate([half[:rows], half[rows:]], axis=1) for half in halved]
            scored = by_table(jnp.concatenate(waves, axis=0), refs["score_lines"][...])
            found = jnp.maximum(scored[:rows], scored[rows:])
            best = found if best is None else jnp.maximum(best, found)
        return best

    unfold(groups[0])
    for steps in groups[1:]:
        forward(steps)
    spread(groups[0])
    for steps in groups[1:]:
        unfold(steps)
        pl.when(row_id == brows - 1)(lambda: spread(steps))
    transform(groups[0])
    for steps in groups[1:]:
        pl.when(row_id < brows - 1)(lambda: spread(steps))
    for i, steps in enumerate(groups):
        if i:
            transform(steps)
        rounds(lambda lowest: combine(steps, lowest, i > 0))
    best = finish(0, None)
    if orients > bunch:
        best = lax.fori_loop(1, orients // bunch, lambda i, best: finish(i * bunch, best), best)
    best_ref[0] = best
    sent = [
        pencils.at[pl.ds(0, bcols - 1)],
        rotations.at[pl.ds(0, orients - 1), pl.ds(0, share)],
        rotations.at[pl.ds(0, orients), pl.ds(0, orients - share)],
        windows.at[pl.ds(0, orients - 1), pl.ds(margin, rows)],
        windows.at[pl.ds(0, orients), pl.ds(0, margin)],
    ]
    wanted = [bcols > 1, True, parts > 1, True, brows > 1]
    for i, ref in enumerate(sent):
        if wanted[i]:
            pltpu.make_async_copy(ref, ref, send_sems.at[i]).wait()


names = (
    "template",
    "index",
    "forward",
    "smoothing",
    "inverse",
    "template_lines",
    "template_rows",
    "volume_lines",
    "volume_rows",
    "score_rows",
    "score_lines",
    "box",
)


def staged(sizes, *refs):
    brick, sources = refs[0], refs[1 : len(names) + 1]
    results = refs[len(names) + 1 : len(names) + 3]
    held = refs[len(names) + 3 : 2 * len(names) + 3]
    rest = refs[2 * len(names) + 3 : -1]
    copies = {
        name: pltpu.make_async_copy(source, target, refs[-1].at[i])
        for i, (name, source, target) in enumerate(zip(names, sources, held))
    }
    named = dict(zip(names, held), brick=brick)
    match_kernel(sizes, named, copies, *rest, *results)


def shards(volume, template, voxel_maps):
    orients, brows, bcols = (lax.axis_size(axis) for axis in ("orient", "brow", "bcol"))
    planes, rows, cols = volume.shape
    edge = template.shape[0]
    half_edge = edge // 2
    length = cols * bcols
    size = cols + edge
    tile_rows = rows + edge
    margin = round_up(half_edge, 8)
    strips = 8
    batch = math.gcd(orients, 4)
    parts = brows if orients % (2 * brows) == 0 else 1
    base = half_edge - orients
    assert brows <= 2 and margin <= rows and tile_rows <= rows + 2 * margin
    assert base % 2 == 0 and orients % 2 == 0
    assert edge % strips == 0 and edge // strips * edge <= LANES
    width = edge // strips * edge * (strips - 1) + LANES
    width = round_up(width, LANES)
    vmem = pl.BlockSpec(memory_space=pltpu.VMEM)
    constants = (
        forward_table(length, bcols),
        smoothing_table(length),
        windowed_inverse(length, bcols, half_edge),
        template_lines(edge, size, strips),
        template_rows(tile_rows, edge, strips),
        right_table(line_table(size, size)),
        volume_rows(tile_rows),
        score_rows(tile_rows, rows),
        score_lines(size, cols),
        box_table(size, cols, edge),
    )
    sizes = (orients, brows, bcols, parts, edge, base, margin, batch, strips)
    operands = (volume, template.reshape(edge * edge, edge), voxel_maps)
    operands += tuple(jnp.asarray(c) for c in constants)
    best, scaling = pl.pallas_call(
        lambda *refs: staged(sizes, *refs),
        out_shape=(pltpu.VMEM((1, rows, cols), jnp.float32),) * 2,
        in_specs=[pl.BlockSpec(memory_space=pl.ANY)] * len(operands),
        out_specs=(vmem, vmem),
        scratch_shapes=[pltpu.VMEM(x.shape, x.dtype) for x in operands[1:]]
        + [
            pltpu.VMEM((2 * orients // parts, 1, width), jnp.float32),
            pltpu.VMEM((orients, orients, 1, width), jnp.float32),
            pltpu.VMEM((2 * edge // strips, strips * batch * orients, size), jnp.float32),
            pltpu.VMEM((orients, orients, tile_rows, size), jnp.float32),
            pltpu.VMEM((orients, 2 * tile_rows, size), jnp.float32),
            pltpu.VMEM((bcols, rows, cols), jnp.float32),
            pltpu.VMEM((orients, rows + 2 * margin, size), jnp.float32),
            pltpu.VMEM((tile_rows, size), jnp.float32),
            pltpu.VMEM((orients, 2 * tile_rows, size), jnp.float32),
            pltpu.VMEM((edge * edge, edge), jnp.float32),
            pltpu.VMEM((2 * round_up(edge * edge // 8, 16), 8 * edge), jnp.bfloat16),
            pltpu.VMEM((8, LANES), jnp.float32),
            pltpu.SemaphoreType.DMA,
            pltpu.SemaphoreType.DMA((bcols,)),
            pltpu.SemaphoreType.DMA((orients,)),
            pltpu.SemaphoreType.DMA((orients // batch,)),
            pltpu.SemaphoreType.DMA((orients,)),
            pltpu.SemaphoreType.DMA((orients // batch,)),
            pltpu.SemaphoreType.DMA((5,)),
            pltpu.SemaphoreType.REGULAR((5,)),
            pltpu.SemaphoreType.DMA((len(names),)),
        ],
        compiler_params=pltpu.CompilerParams(collective_id=0, has_side_effects=True),
        name="match",
    )(*operands)
    return best * scaling


def solution(mesh):
    in_specs = (P("orient", "brow", "bcol"), P(), P("orient", None))
    out_specs = P("orient", "brow", "bcol")
    return jax.shard_map(shards, mesh=mesh, in_specs=in_specs, out_specs=out_specs, check_vma=False)
```

```python
import math

import numpy as np
import jax
import jax.numpy as jnp
from jax import lax
from jax.experimental import pallas as pl
from jax.experimental.pallas import tpu as pltpu
from jax.sharding import PartitionSpec as P

epsilon = 1e-06
floor_share = 0.1
LANES = 128
MESH = pl.DeviceIdType.MESH


def round_up(value, step):
    return -(-value // step) * step


def split(table):
    upper = table.astype(jnp.bfloat16)
    lower = (table - upper.astype(np.float64)).astype(jnp.bfloat16)
    return upper, lower


def forward_table(length, parts):
    half = length // 2 + 1
    padded = round_up(half, LANES)
    angles = 2.0 * np.pi * (np.outer(np.arange(length), np.arange(half)) % length) / length
    table = np.zeros((length, 2 * padded))
    table[:, :half] = np.cos(angles)
    table[:, padded : padded + half] = -np.sin(angles)
    return np.stack(split(table.reshape(parts, length // parts, 2 * padded)))


def smoothing_table(length):
    half = length // 2 + 1
    padded = round_up(half, LANES)
    table = np.zeros((padded, padded))
    fold = np.minimum(np.arange(length), length - np.arange(length))
    for k in range(half):
        for shift in (-1, 0, 1):
            table[fold[(k + shift) % length], k] += 1.0 / 3.0
        for other in range(length):
            table[fold[other], k] += floor_share / length
    return np.stack(split(table))


def windowed_inverse(length, parts, margin):
    half = length // 2 + 1
    padded = round_up(half, LANES)
    width = length // parts
    tables = np.zeros((parts, 2 * padded, width + 2 * margin))
    k = np.arange(half)
    share = np.where((k == 0) | (2 * k == length), 1.0, 2.0)[:, None] / math.sqrt(length)
    for part in range(parts):
        columns = np.arange(width + 2 * margin) + part * width - margin
        inside = (columns >= 0) & (columns < length)
        angles = 2.0 * np.pi * (np.outer(k, columns) % length) / length
        tables[part, :half] = share * np.cos(angles) * inside
        tables[part, padded : padded + half] = -share * np.sin(angles) * inside
    return np.stack(split(tables))


def left_table(table):
    upper, lower = split(table)
    return np.concatenate([upper, lower, upper], axis=1)


def right_table(table):
    upper, lower = split(table)
    return np.concatenate([upper, upper, lower], axis=0)


def odd_waves(count, size):
    angles = np.pi * (np.outer(np.arange(count), 2 * np.arange(size // 2) + 1) % (2 * size)) / size
    return np.cos(angles), np.sin(angles)


def line_table(count, size):
    cos, sin = odd_waves(count, size)
    return np.concatenate([cos, -sin, -sin, -cos], axis=1)


def row_waves(size, count):
    angles = 2.0 * np.pi * (np.outer(np.arange(size), np.arange(count)) % size) / size
    return np.cos(angles), np.sin(angles)


def template_lines(edge, size, strips):
    span = edge // strips
    waves = line_table(edge, size)
    table = np.zeros((LANES, 2, span, size))
    for b in range(span):
        for half in range(2):
            table[b * edge : (b + 1) * edge, half, b] = waves[:, half * size : (half + 1) * size]
    return right_table(table.reshape(LANES, -1))


def template_rows(size, edge, strips):
    order = np.arange(edge).reshape(strips, edge // strips).T.reshape(-1)
    return left_table(np.concatenate([wave[:, order] for wave in row_waves(size, edge)], axis=1))


def volume_rows(size):
    cos, sin = row_waves(size, size)
    return left_table(np.block([[cos, sin], [-sin, cos]]))


def score_rows(size, rows):
    cos, sin = (wave.T / size for wave in row_waves(size, rows))
    return left_table(np.block([[cos, -sin], [sin, cos]]))


def score_lines(size, count):
    cos, sin = (wave.T * (2.0 / size) for wave in odd_waves(count, size))
    return right_table(np.concatenate([cos, cos, -sin, -sin], axis=0))


def box_table(size, count, edge):
    offsets = np.arange(size)[:, None] - np.arange(count)[None, :]
    return ((offsets >= 0) & (offsets < edge)).astype(jnp.bfloat16)


def split_table(template_ref, shifted):
    lines, edge = template_ref.shape
    template = template_ref[...] - 0.5
    shifted[...] = template
    mean = jnp.sum(template, keepdims=True) / (lines * edge)
    centred = template - mean
    scale = lax.rsqrt(jnp.sum(centred * centred, keepdims=True) + epsilon)
    table = jnp.concatenate([shifted[pl.ds(j, lines // 8, stride=8), :] for j in range(8)], axis=1)
    spare = round_up(lines // 8, 16) - lines // 8
    table = jnp.concatenate([table, jnp.zeros((spare, 8 * edge), jnp.float32)], axis=0)
    return jnp.concatenate(halves(table), axis=0), mean, scale


def look_up(pieces, index):
    count, span = pieces.shape
    width = index.shape[1]
    high = ((index.astype(jnp.float32) + 0.5) * (1.0 / span)).astype(jnp.int32)
    low = (index - high * span).astype(jnp.float32).astype(jnp.bfloat16)
    row = lax.broadcasted_iota(jnp.int32, (span, width), 0).astype(jnp.float32).astype(jnp.bfloat16)
    one = jnp.ones((), jnp.bfloat16)
    lanes = product(pieces, jnp.where(row == low, one, jnp.zeros_like(one)))
    lanes = lanes[: count // 2] + lanes[count // 2 :]
    mine = lax.broadcasted_iota(jnp.int32, lanes.shape, 0) == high
    return jnp.sum(jnp.where(mine, lanes, 0.0), axis=0, keepdims=True)


def halves(x):
    upper = x.astype(jnp.bfloat16)
    return upper, (x - upper.astype(jnp.float32)).astype(jnp.bfloat16)


def product(a, b):
    return jnp.dot(a, b, preferred_element_type=jnp.float32)


def by_table(x, table):
    upper, lower = halves(x)
    return product(jnp.concatenate([upper, lower, upper], axis=1), table)


def by_halves(x, upper, lower):
    high, low = halves(x)
    return product(high, upper) + (product(low, upper) + product(high, lower))


def table_by(table, x):
    upper, lower = halves(x)
    return product(table, jnp.concatenate([upper, upper, lower], axis=0))


def match_kernel(
    sizes,
    refs,
    copies,
    rotated,
    rotations,
    lines,
    templates,
    volumes,
    pencils,
    windows,
    energy,
    totals,
    normed,
    table,
    stats,
    own_sem,
    gather_sems,
    share_sems,
    turn_sems,
    window_sems,
    margin_sems,
    send_sems,
    tokens,
    best_ref,
    scaling_ref,
):
    orients, brows, bcols, parts, edge, base, margin, batch, strips = sizes
    half_edge = edge // 2
    rows, cols = refs["brick"].shape[1:]
    tile_rows, size = energy.shape
    skip = margin - half_edge
    me = lax.axis_index("orient")
    row_id = lax.axis_index("brow")
    col_id = lax.axis_index("bcol")
    share = orients // parts
    mine = lax.rem(row_id, parts)
    plane_voxels = edge * edge
    span = edge // strips

    def column_peer(column):
        return {"orient": me, "brow": row_id, "bcol": column}

    def partner(step):
        assert orients & (orients - 1) == 0
        other, weight = 0, 1
        while weight < orients:
            other = other + lax.rem(me // weight + step // weight, 2) * weight
            weight *= 2
        return other

    partners = [partner(step) for step in range(orients)]
    pair, last = me // 2, orients // 2 - 1
    odd = lax.rem(me, 2)
    by_column, by_row, by_pair, by_near, by_far = (tokens.at[i] for i in range(5))

    def plane_peer(plane):
        return {"orient": plane, "brow": row_id, "bcol": col_id}

    def row_peer(row):
        return {"orient": me, "brow": row, "bcol": col_id}

    def expect(semaphore, count):
        pl.when(count > 0)(lambda: pl.semaphore_wait(semaphore, count))

    def each(count, own, step, do):
        for other in range(count):

            @pl.when(step * other > step * own)
            def _():
                do(other)

    def greet(semaphore, peer):
        pl.semaphore_signal(semaphore, inc=1, device_id=peer, device_id_type=MESH)

    def first_of(part, plane):
        start = orients - plane
        rest = lax.rem(start, 2 * parts) + 2 * parts - 2 * part
        return start // (2 * parts) * 2 + (rest - 1) // (2 * parts) + (rest - 2) // (2 * parts)

    def plane_of(slot):
        part, index = slot // share, slot % share
        found = first_of(part, me) + index
        return found // 2 * (2 * parts) + 2 * part + lax.rem(found, 2) - orients + me

    tables = ("template_lines", "template_rows", "volume_lines", "volume_rows", "score_rows", "score_lines", "box")
    for name, copy in copies.items():
        if name not in tables:
            copy.start()
    windows[...] = jnp.zeros_like(windows)
    barrier = pltpu.get_barrier_semaphore()
    @pl.when(odd == 0)
    def _():
        each(orients, me, 1, lambda plane: greet(barrier, plane_peer(plane)))

    @pl.when(odd == 1)
    def _():
        each(orients // 2, pair, 1, lambda other: greet(barrier, plane_peer(2 * other + 1)))

    each(bcols, col_id, 1, lambda column: greet(barrier, column_peer(column)))
    each(brows, row_id, 1, lambda row: greet(barrier, row_peer(row)))
    own = pltpu.make_async_copy(refs["brick"].at[0], pencils.at[col_id], own_sem)
    own.start()
    energy[...] = jnp.zeros_like(energy)
    rotated[...] = jnp.zeros_like(rotated)
    planes_of = [plane_of(slot) for slot in range(orients)]

    def tabulate():
        copies["template"].wait()
        table[...], stats[0:1, 0:1], stats[1:2, 0:1] = split_table(refs["template"], normed)
        copies["index"].wait()

    def find(first, end):
        def one(index):
            plane = base + 2 * mine + 2 * parts * index

            def fill():
                start = pl.multiple_of(plane * plane_voxels, 2 * plane_voxels)
                found = look_up(table[...], refs["index"][0:1, pl.ds(start, 2 * plane_voxels)])
                found = (found - stats[0:1, 0:1]) * stats[1:2, 0:1]
                for i in range(2):
                    rotated[2 * index + i, :, :plane_voxels] = found[:, i * plane_voxels : (i + 1) * plane_voxels]

            if base < 0 or base + 2 * orients > edge:
                pl.when(jnp.logical_and(plane >= 0, plane < edge))(fill)
            else:
                fill()

        if share <= 4:
            for index in range(first, end):
                one(index)
        else:
            pl.loop(first, end)(one)

    expect(barrier, pair + odd * (pair + 1) + col_id + row_id)

    def gather_of(column, brick):
        return pltpu.make_async_remote_copy(
            src_ref=brick,
            dst_ref=pencils.at[col_id],
            send_sem=send_sems.at[0],
            recv_sem=gather_sems.at[col_id],
            device_id=column_peer(column),
            device_id_type=MESH,
        )

    each(bcols, col_id, -1, lambda column: gather_of(column, refs["brick"].at[0]).start())
    each(bcols, col_id, -1, lambda column: greet(by_column, column_peer(column)))
    each(brows, row_id, -1, lambda row: greet(by_row, row_peer(row)))

    @pl.when(odd == 1)
    def _():
        def answer(other):
            for i in range(2):
                greet(by_far, plane_peer(2 * other + i))

        greet(by_pair, plane_peer(me - 1))
        each(orients // 2, pair - 1, -1, answer)

        @pl.when(pair > 0)
        def _():
            for i in range(2):
                greet(by_near, plane_peer(2 * pair - 2 + i))

    for name in tables:
        copies[name].start()
    tabulate()
    find(0, share // 2)
    expect(by_column, bcols - 1 - col_id)
    own.wait()
    each(bcols, col_id, 1, lambda column: gather_of(column, pencils.at[col_id]).start())
    find(share // 2, share)

    def block(rotation, part):
        return rotations.at[rotation, pl.ds(part * share, share)]

    def share_of(plane):
        return pltpu.make_async_remote_copy(
            src_ref=rotated.at[pl.ds(first_of(mine, plane), share)],
            dst_ref=block(me, mine),
            send_sem=send_sems.at[1],
            recv_sem=share_sems.at[me],
            device_id=plane_peer(plane),
            device_id_type=MESH,
        )

    def turn_of(step, turn):
        rotation = partners[step]
        row = lax.rem(row_id + turn, brows)
        return pltpu.make_async_remote_copy(
            src_ref=block(rotation, mine),
            dst_ref=block(rotation, mine),
            send_sem=send_sems.at[2],
            recv_sem=turn_sems.at[step // batch],
            device_id=row_peer(row),
            device_id_type=MESH,
        )

    expect(by_pair, 1 - odd)
    each(orients, me, -1, lambda plane: share_of(plane).start())
    pl.when(odd == 0)(lambda: share_of(me + 1).start())
    expect(by_row, brows - 1 - row_id)
    rotations[me, pl.ds(mine * share, share)] = rotated[pl.ds(first_of(mine, me), share)]
    for turn in range(1, parts):
        turn_of(0, turn).start()
    near = (2 * last - pair) // (last + 1)
    far = last - pair - near

    def send(kind, planes):
        def one(plane):
            if planes == "near":
                pl.when(plane < 2 * pair + 4)(lambda: kind(plane).start())
            else:
                pl.when(plane >= 2 * pair + 4)(lambda: kind(plane).start())

        each(orients, 2 * pair + 1, 1, one)

    expect(by_near, near)
    send(share_of, "near")

    def forward(steps):
        for step in steps:
            if step:
                arrived = block(partners[step], mine)
                pltpu.make_async_copy(arrived, arrived, share_sems.at[partners[step]]).wait()
                for turn in range(1, parts):
                    turn_of(step, turn).start()

    groups = [list(range(first, first + batch)) for first in range(0, orients, batch)]
    for name in ("forward", "smoothing", "inverse"):
        copies[name].wait()

    def wave(column):
        return by_halves(pencils[column], refs["forward"][0, column], refs["forward"][1, column])

    both = wave(col_id)
    for step in range(1, bcols):
        column = lax.rem(col_id + step, bcols)
        arrived = pencils.at[column]
        pltpu.make_async_copy(arrived, arrived, gather_sems.at[column]).wait()
    for step in range(1, bcols):
        both = both + wave(lax.rem(col_id + step, bcols))
    padded = both.shape[1] // 2
    real, imag = both[:, :padded], both[:, padded:]
    power = real * real + imag * imag
    weights = lax.rsqrt(by_halves(power, refs["smoothing"][0], refs["smoothing"][1]) + epsilon)
    white = both * jnp.concatenate([weights, weights], axis=1)
    windows[me, margin : margin + rows] = by_halves(
        white, refs["inverse"][0, col_id], refs["inverse"][1, col_id]
    )

    def window_of(plane):
        part = windows.at[me, pl.ds(margin, rows)]
        return pltpu.make_async_remote_copy(
            src_ref=part,
            dst_ref=part,
            send_sem=send_sems.at[3],
            recv_sem=window_sems.at[me],
            device_id=plane_peer(plane),
            device_id_type=MESH,
        )

    def margin_of(step):
        plane = partners[step]
        return pltpu.make_async_remote_copy(
            src_ref=windows.at[plane, pl.ds(pl.multiple_of(rows - row_id * (rows - margin), 8), margin)],
            dst_ref=windows.at[plane, pl.ds(pl.multiple_of(row_id * (margin + rows), 8), margin)],
            send_sem=send_sems.at[4],
            recv_sem=margin_sems.at[step // batch],
            device_id=row_peer(lax.rem(row_id + 1, brows)),
            device_id_type=MESH,
        )

    each(orients, me, -1, lambda plane: window_of(plane).start())
    pl.when(odd == 0)(lambda: window_of(me + 1).start())
    send(window_of, "near")
    if brows > 1:
        margin_of(0).start()
    for name in tables:
        copies[name].wait()

    def normalise():
        summed = energy[0:rows, :]
        for b in range(1, edge):
            summed = summed + energy[b : b + rows, :]
        upper, lower = halves(summed)
        boxed = product(upper, refs["box"][...]) + product(lower, refs["box"][...])
        scaling_ref[0] = lax.rsqrt(boxed / edge**3 + epsilon)

    def transform(steps):
        if brows > 1:
            arrived = windows.at[pl.ds(0, batch), pl.ds(0, margin)]
            pltpu.make_async_copy(arrived, arrived, margin_sems.at[steps[0] // batch]).wait()
        tiles = []
        for step in steps:
            plane = partners[step]
            tile = windows[plane, skip : skip + tile_rows]
            gap = plane - me
            near = jnp.logical_and(gap >= -half_edge, gap < half_edge).astype(jnp.float32)
            energy[...] += tile * tile * near
            tiles.append(tile)
        turned = by_table(jnp.concatenate(tiles, axis=0), refs["volume_lines"][...])
        if steps is groups[-1]:
            normalise()
        for first in range(0, len(steps), 2):
            pair = []
            for i in range(first, first + 2):
                part = turned[i * tile_rows : (i + 1) * tile_rows]
                pair.append(jnp.concatenate([part[:, :size], part[:, size:]], axis=0))
            spun = table_by(refs["volume_rows"][...], jnp.concatenate(pair, axis=1))
            for i in range(2):
                volumes[partners[steps[first + i]]] = spun[:, i * size : (i + 1) * size]

    def unfold(steps):
        if parts > 1:
            arrived = rotations.at[pl.ds(0, batch), pl.ds(0, orients - share)]
            pltpu.make_async_copy(arrived, arrived, turn_sems.at[steps[0] // batch]).wait()
        width = span * edge
        pieces = []
        for step in steps:
            planes = rotations[partners[step]][:, 0, :]
            pieces += [planes[:, j * width : j * width + LANES] for j in range(strips)]
        turned = by_table(jnp.concatenate(pieces, axis=0), refs["template_lines"][...])
        for k in range(2 * span):
            lines[k, : turned.shape[0]] = turned[:, k * size : (k + 1) * size]
        for i, step in enumerate(steps):
            for first in range(0, orients, 2):
                pair = [
                    jnp.concatenate(
                        [lines[k, pl.ds(i * strips * orients + slot, strips, stride=orients), :] for k in range(2 * span)],
                        axis=0,
                    )
                    for slot in (first, first + 1)
                ]
                spun = table_by(refs["template_rows"][...], jnp.concatenate(pair, axis=1))
                for j in range(2):
                    templates[partners[step], planes_of[first + j]] = spun[:, j * size : (j + 1) * size]

    def spread(steps):
        for step in steps:
            if step:
                arrived = windows.at[partners[step], pl.ds(margin, rows)]
                pltpu.make_async_copy(arrived, arrived, window_sems.at[partners[step]]).wait()
                if brows > 1:
                    margin_of(step).start()

    forward(groups[0])
    expect(by_far, far)
    send(share_of, "far")
    send(window_of, "far")
    bunch = math.gcd(orients, 8)

    def rounds(do):
        if orients == bunch:
            do(0)
        else:
            pl.loop(0, orients // bunch)(lambda i: do(i * bunch))

    def combine(steps, lowest, more):
        for first in range(0, bunch, 2):
            for half in range(tile_rows // 8):
                top = pl.ds(half * 8, 8)
                low = pl.ds(tile_rows + half * 8, 8)
                for rotation in (lowest + first, lowest + first + 1):
                    straight = totals[rotation, top, :] if more else None
                    crossed = totals[rotation, low, :] if more else None
                    for step in steps:
                        plane = partners[step]
                        wave = templates[rotation, plane, top, :]
                        term = volumes[plane, top, :] * wave
                        turn = volumes[plane, low, :] * wave
                        straight = term if straight is None else straight + term
                        crossed = turn if crossed is None else crossed + turn
                    totals[rotation, top, :] = straight
                    totals[rotation, low, :] = crossed

    def finish(lowest, best):
        turned = []
        for first in range(0, bunch, 2):
            pair = jnp.concatenate([totals[lowest + first], totals[lowest + first + 1]], axis=1)
            turned.append(table_by(refs["score_rows"][...], pair))
        for part in turned:
            halved = [part[:, i * size : (i + 1) * size] for i in range(2)]
            waves = [jnp.concatenate([half[:rows], half[rows:]], axis=1) for half in halved]
            scored = by_table(jnp.concatenate(waves, axis=0), refs["score_lines"][...])
            found = jnp.maximum(scored[:rows], scored[rows:])
            best = found if best is None else jnp.maximum(best, found)
        return best

    unfold(groups[0])
    for steps in groups[1:]:
        forward(steps)
    spread(groups[0])
    for steps in groups[1:]:
        unfold(steps)
        pl.when(row_id == brows - 1)(lambda: spread(steps))
    transform(groups[0])
    for steps in groups[1:]:
        pl.when(row_id < brows - 1)(lambda: spread(steps))
    for i, steps in enumerate(groups):
        if i:
            transform(steps)
        rounds(lambda lowest: combine(steps, lowest, i > 0))
    best = finish(0, None)
    if orients > bunch:
        best = lax.fori_loop(1, orients // bunch, lambda i, best: finish(i * bunch, best), best)
    best_ref[0] = best
    sent = [
        pencils.at[pl.ds(0, bcols - 1)],
        rotations.at[pl.ds(0, orients - 1), pl.ds(0, share)],
        rotations.at[pl.ds(0, orients), pl.ds(0, orients - share)],
        windows.at[pl.ds(0, orients - 1), pl.ds(margin, rows)],
        windows.at[pl.ds(0, orients), pl.ds(0, margin)],
    ]
    wanted = [bcols > 1, True, parts > 1, True, brows > 1]
    for i, ref in enumerate(sent):
        if wanted[i]:
            pltpu.make_async_copy(ref, ref, send_sems.at[i]).wait()


names = (
    "template",
    "index",
    "forward",
    "smoothing",
    "inverse",
    "template_lines",
    "template_rows",
    "volume_lines",
    "volume_rows",
    "score_rows",
    "score_lines",
    "box",
)


def staged(sizes, *refs):
    brick, sources = refs[0], refs[1 : len(names) + 1]
    results = refs[len(names) + 1 : len(names) + 3]
    held = refs[len(names) + 3 : 2 * len(names) + 3]
    rest = refs[2 * len(names) + 3 : -1]
    copies = {
        name: pltpu.make_async_copy(source, target, refs[-1].at[i])
        for i, (name, source, target) in enumerate(zip(names, sources, held))
    }
    named = dict(zip(names, held), brick=brick)
    match_kernel(sizes, named, copies, *rest, *results)


def shards(volume, template, voxel_maps):
    orients, brows, bcols = (lax.axis_size(axis) for axis in ("orient", "brow", "bcol"))
    planes, rows, cols = volume.shape
    edge = template.shape[0]
    half_edge = edge // 2
    length = cols * bcols
    size = cols + edge
    tile_rows = rows + edge
    margin = round_up(half_edge, 8)
    strips = 8
    batch = math.gcd(orients, 4)
    parts = brows if orients % (2 * brows) == 0 else 1
    base = half_edge - orients
    assert brows <= 2 and margin <= rows and tile_rows <= rows + 2 * margin
    assert base % 2 == 0 and orients % 2 == 0
    assert edge % strips == 0 and edge // strips * edge <= LANES
    width = edge // strips * edge * (strips - 1) + LANES
    width = round_up(width, LANES)
    vmem = pl.BlockSpec(memory_space=pltpu.VMEM)
    constants = (
        forward_table(length, bcols),
        smoothing_table(length),
        windowed_inverse(length, bcols, half_edge),
        template_lines(edge, size, strips),
        template_rows(tile_rows, edge, strips),
        right_table(line_table(size, size)),
        volume_rows(tile_rows),
        score_rows(tile_rows, rows),
        score_lines(size, cols),
        box_table(size, cols, edge),
    )
    sizes = (orients, brows, bcols, parts, edge, base, margin, batch, strips)
    operands = (volume, template.reshape(edge * edge, edge), voxel_maps)
    operands += tuple(jnp.asarray(c) for c in constants)
    best, scaling = pl.pallas_call(
        lambda *refs: staged(sizes, *refs),
        out_shape=(pltpu.VMEM((1, rows, cols), jnp.float32),) * 2,
        in_specs=[pl.BlockSpec(memory_space=pl.ANY)] * len(operands),
        out_specs=(vmem, vmem),
        scratch_shapes=[pltpu.VMEM(x.shape, x.dtype) for x in operands[1:]]
        + [
            pltpu.VMEM((2 * orients // parts, 1, width), jnp.float32),
            pltpu.VMEM((orients, orients, 1, width), jnp.float32),
            pltpu.VMEM((2 * edge // strips, strips * batch * orients, size), jnp.float32),
            pltpu.VMEM((orients, orients, tile_rows, size), jnp.float32),
            pltpu.VMEM((orients, 2 * tile_rows, size), jnp.float32),
            pltpu.VMEM((bcols, rows, cols), jnp.float32),
            pltpu.VMEM((orients, rows + 2 * margin, size), jnp.float32),
            pltpu.VMEM((tile_rows, size), jnp.float32),
            pltpu.VMEM((orients, 2 * tile_rows, size), jnp.float32),
            pltpu.VMEM((edge * edge, edge), jnp.float32),
            pltpu.VMEM((2 * round_up(edge * edge // 8, 16), 8 * edge), jnp.bfloat16),
            pltpu.VMEM((8, LANES), jnp.float32),
            pltpu.SemaphoreType.DMA,
            pltpu.SemaphoreType.DMA((bcols,)),
            pltpu.SemaphoreType.DMA((orients,)),
            pltpu.SemaphoreType.DMA((orients // batch,)),
            pltpu.SemaphoreType.DMA((orients,)),
            pltpu.SemaphoreType.DMA((orients // batch,)),
            pltpu.SemaphoreType.DMA((5,)),
            pltpu.SemaphoreType.REGULAR((5,)),
            pltpu.SemaphoreType.DMA((len(names),)),
        ],
        compiler_params=pltpu.CompilerParams(collective_id=0, has_side_effects=True),
        name="match",
    )(*operands)
    return best * scaling


def solution(mesh):
    in_specs = (P("orient", "brow", "bcol"), P(), P("orient", None))
    out_specs = P("orient", "brow", "bcol")
    return jax.shard_map(shards, mesh=mesh, in_specs=in_specs, out_specs=out_specs, check_vma=False)
```
